256 devices in a mesh: layer: 16 (over z_lo, x), ctx: 16 (over y, z_hi, core).
Axes of the slice: x: 4, y: 4, z: 8 (z_hi: 2, z_lo: 4; z = z_hi * 4 + z_lo), core: 2. Of those that a mesh axis runs over, the one named last changes fastest.
Arguments:
- queries: bfloat16 [16, 2048, 1536], P('layer', 'ctx'), may hold values from -9 to 9
- keys: bfloat16 [2048, 512], P(('ctx', 'layer')), may hold values from -4 to 4
- values: bfloat16 [2048, 512], P(('ctx', 'layer')), may hold values from -6 to 6
- head: float32 [16, 1536, 2], P('layer'), may hold values from -1.5 to 1.5
- segments: int32 [2048], replicated, may hold values from 0 to 4, as said below
- label_mask: int32 [2048], P('ctx'), may hold values 0 or 1
- labels: int32 [2048], P('ctx'), may hold values from 0 to 1
Outputs:
- loss: float32 [16], P('layer')
- query_gradient: float32 [16, 2048, 1536], P('layer', 'ctx')
- grad_keys: float32 [2048, 512], P(('ctx', 'layer'))
- grad_values: float32 [2048, 512], P(('ctx', 'layer'))
- head_gradient_rows: float32 [16, 1536, 2], P('layer')
The draws below stay inside these ranges and needn't reach their ends.
Inputs may be any that keep to these rules, and one draw needn't show every extreme that they name: `segments`: document ids never fall; the first document spans exactly 1536 positions and the positions after it form exactly four more documents, each of one position or more.
All inputs are finite; a program needn't handle non-finite values. No bound on the sum of `label_mask` on one device may be relied on, other than what follows from the above.
Results may differ from the reference program's by a relative error of at most 0.019.
Values may be sent and summed in bfloat16 or wider, within the bound.
No kernel may reach another device: no remote copies, remote signals or barrier semaphores. Data moves between devices by JAX's collectives and lax.ppermute only.
A program may use at most 128 MiB of HBM per device.

```python
import jax
import jax.numpy as jnp
from jax import lax

QUERY_HEADS = 12
KEY_VALUE_HEADS = 4
HEAD_WIDTH = 128
CLASSES = 2
LOCAL_TOKENS = 128
TOKEN_COUNT = 2048
LAYERS = 16
DOC_MOST = 1536
N_CTX = 16


rest_cuts = 3


def doc_ids(key):
    base_offset = jax.random.fold_in(key, 11)
    rest_rows = TOKEN_COUNT - DOC_MOST
    order = jax.random.permutation(base_offset, rest_rows - 1)
    cuts = order[:rest_cuts].astype(jnp.int32) + 1
    positions = jnp.arange(TOKEN_COUNT, dtype=jnp.int32)
    offset_rows = positions - DOC_MOST
    later = 1 + jnp.sum((cuts[None, :] <= offset_rows[:, None]).astype(jnp.int32), axis=1)
    return jnp.where(positions < DOC_MOST, 0, later).astype(jnp.int32)


def draw_segments(key, part):
    return doc_ids(key)


def draw_keys(key, part):
    row_count = jnp.clip(jax.random.normal(jax.random.fold_in(key, 41), (TOKEN_COUNT, KEY_VALUE_HEADS * HEAD_WIDTH), jnp.float32), -4.0, 4.0)
    return row_count.astype(jnp.bfloat16)


def draw_queries(key, part):
    row_count = jnp.clip(jax.random.normal(jax.random.fold_in(key, 51), (LAYERS, TOKEN_COUNT, QUERY_HEADS * HEAD_WIDTH), jnp.float32), -4.0, 4.0)
    return row_count.astype(jnp.bfloat16)


def with_ends(entries, rng, least, high):
    longest = entries.shape.index(max(entries.shape))
    spots = []
    for shift in (0, 1):
        where = [jax.random.randint(jax.random.fold_in(rng, axis), (), 0, length) for axis, length in enumerate(entries.shape)]
        where[longest] = (where[longest] + shift) % entries.shape[longest]
        spots.append(tuple(where))
    return entries.at[spots[0]].set(least).at[spots[1]].set(high)


def level_of(key, shape, shards, low, largest):
    def one(position, shards_of):
        draws = jax.random.uniform(jax.random.fold_in(jax.random.fold_in(key, 6), position), (shards_of,), jnp.float32, low / len(shards), largest / len(shards))
        return jnp.repeat(jnp.exp(draws), shape[position] // shards_of).reshape((-1,) + (1,) * (len(shape) - position - 1))

    loudness = one(*shards[0])
    for cut in shards[1:]:
        loudness = loudness * one(*cut)
    return loudness


def bell_draw(own_key, dims, scale, reach, split=(), held_as=jnp.bfloat16):
    loudness = level_of(own_key, dims, split, -0.22, 0.18) if split else 1.0
    result = jax.random.normal(own_key, dims, jnp.float32) * scale * loudness
    return jnp.minimum(jnp.maximum(result, -reach), reach).astype(held_as)


def setup_inputs(seed: int = 0) -> dict:
    splits = jax.random.split(jax.random.key(seed), 8)
    queries = draw_queries(jax.random.fold_in(splits[7], 71), 0)
    keys = draw_keys(jax.random.fold_in(splits[7], 71), 0)
    values = bell_draw(splits[2], (TOKEN_COUNT, KEY_VALUE_HEADS * HEAD_WIDTH), 1.0, 6.0, ((0, 256),))
    head = bell_draw(splits[3], (LAYERS, QUERY_HEADS * HEAD_WIDTH, CLASSES), 0.25, 1.5, ((0, 16),), jnp.float32)
    segments = draw_segments(jax.random.fold_in(splits[7], 71), 0)
    label_mask = with_ends((jax.random.randint(splits[5], (TOKEN_COUNT,), 0, 2) < 1).astype(jnp.int32), jax.random.fold_in(splits[5], 1), 0, 1)
    labels = with_ends(jax.random.randint(splits[6], (TOKEN_COUNT,), 0, CLASSES), jax.random.fold_in(splits[6], 1), 0, CLASSES - 1).astype(jnp.int32)
    return {"queries": queries, "keys": keys, "values": values, "head": head, "segments": segments, "label_mask": label_mask, "labels": labels}


NEGATIVE_FILL = -1.0e30
HIGH = lax.Precision.HIGHEST


def masked_scores(query_tensor_four, key_tensor_three, seg_q, seg_k, q_start, k_start):
    s = jnp.einsum("tgrd,ngd->tgrn", query_tensor_four.astype(jnp.float32), key_tensor_three.astype(jnp.float32), precision=HIGH) * (HEAD_WIDTH ** -0.5)
    q_pos = q_start + jnp.arange(query_tensor_four.shape[0], dtype=jnp.int32)
    k_pos = k_start + jnp.arange(key_tensor_three.shape[0], dtype=jnp.int32)
    allowed = (k_pos[None, :] <= q_pos[:, None]) & (seg_k[None, :] == seg_q[:, None])
    return jnp.where(allowed[:, None, None, :], s, NEGATIVE_FILL)


def reference(queries, keys, values, head, segments, label_mask, labels):
    head_group = QUERY_HEADS // KEY_VALUE_HEADS
    key_tensor_three = keys.reshape(TOKEN_COUNT, KEY_VALUE_HEADS, HEAD_WIDTH)
    value_tensor_three = values.reshape(TOKEN_COUNT, KEY_VALUE_HEADS, HEAD_WIDTH)
    weights_mask = label_mask.astype(jnp.float32)
    classes = jnp.arange(CLASSES, dtype=jnp.int32)

    def one_layer(carry, layer_in):
        key_gradient_sum, value_gradient_sum = carry
        query_layer, head_layer = layer_in
        loss_sum = jnp.zeros((), jnp.float32)
        head_grad = jnp.zeros((QUERY_HEADS * HEAD_WIDTH, CLASSES), jnp.float32)
        dq_rows = []
        for block in range(N_CTX):
            lower_limit = block * LOCAL_TOKENS
            upper_limit = lower_limit + LOCAL_TOKENS
            query_tensor_four = query_layer[lower_limit:upper_limit].reshape(LOCAL_TOKENS, KEY_VALUE_HEADS, head_group, HEAD_WIDTH)
            k_part = key_tensor_three[:upper_limit]
            v_part = value_tensor_three[:upper_limit].astype(jnp.float32)
            s = masked_scores(query_tensor_four, k_part, segments[lower_limit:upper_limit], segments[:upper_limit], lower_limit, 0)
            top = jnp.max(s, axis=-1)
            lse = top + jnp.log(jnp.sum(jnp.exp(s - top[..., None]), axis=-1))
            prob = jnp.exp(s - lse[..., None])
            attended = jnp.einsum("tgrn,ngd->tgrd", prob, v_part, precision=HIGH)
            flat_rows = attended.reshape(LOCAL_TOKENS, QUERY_HEADS * HEAD_WIDTH)
            logits = jnp.dot(flat_rows, head_layer, precision=HIGH)
            mx = jnp.max(logits, axis=-1)
            log_total = mx + jnp.log(jnp.sum(jnp.exp(logits - mx[:, None]), axis=-1))
            onehot = (labels[lower_limit:upper_limit, None] == classes[None, :]).astype(jnp.float32)
            mask = weights_mask[lower_limit:upper_limit]
            loss_sum = loss_sum + jnp.sum(mask * (log_total - jnp.sum(onehot * logits, axis=-1)))
            d_logits = mask[:, None] * (jnp.exp(logits - log_total[:, None]) - onehot)
            head_grad = head_grad + jnp.dot(flat_rows.T, d_logits, precision=HIGH)
            attention_gradient = jnp.dot(d_logits, head_layer.T, precision=HIGH)
            delta_rows = jnp.sum((attention_gradient * flat_rows).reshape(LOCAL_TOKENS, KEY_VALUE_HEADS, head_group, HEAD_WIDTH), axis=-1)
            attention_gradient_half = attention_gradient.astype(jnp.bfloat16).reshape(LOCAL_TOKENS, KEY_VALUE_HEADS, head_group, HEAD_WIDTH).astype(jnp.float32)
            prob16 = prob.astype(jnp.bfloat16).astype(jnp.float32)
            dv_t = jnp.einsum("tgrn,tgrd->ngd", prob16, attention_gradient_half, precision=HIGH)
            dp = jnp.einsum("tgrd,ngd->tgrn", attention_gradient_half, v_part, precision=HIGH)
            ds16 = (prob * (dp - delta_rows[..., None]) * (HEAD_WIDTH ** -0.5)).astype(jnp.bfloat16).astype(jnp.float32)
            dq_t = jnp.einsum("tgrn,ngd->tgrd", ds16, k_part.astype(jnp.float32), precision=HIGH)
            dk_t = jnp.einsum("tgrn,tgrd->ngd", ds16, query_tensor_four.astype(jnp.float32), precision=HIGH)
            pad = ((0, TOKEN_COUNT - upper_limit), (0, 0), (0, 0))
            key_gradient_sum = key_gradient_sum + jnp.pad(dk_t, pad)
            value_gradient_sum = value_gradient_sum + jnp.pad(dv_t, pad)
            dq_rows.append(dq_t.reshape(LOCAL_TOKENS, QUERY_HEADS * HEAD_WIDTH))
        return (key_gradient_sum, value_gradient_sum), (loss_sum / TOKEN_COUNT, jnp.concatenate(dq_rows, axis=0), head_grad)

    start_offset = (jnp.zeros((TOKEN_COUNT, KEY_VALUE_HEADS, HEAD_WIDTH), jnp.float32), jnp.zeros((TOKEN_COUNT, KEY_VALUE_HEADS, HEAD_WIDTH), jnp.float32))
    (key_gradient_sum, value_gradient_sum), (loss, query_gradient, head_gradient_rows) = lax.scan(one_layer, start_offset, (queries, head))
    return loss, query_gradient, key_gradient_sum.reshape(TOKEN_COUNT, KEY_VALUE_HEADS * HEAD_WIDTH), value_gradient_sum.reshape(TOKEN_COUNT, KEY_VALUE_HEADS * HEAD_WIDTH), head_gradient_rows
```

```python
import jax
import jax.numpy as jnp
from jax import lax
from jax.experimental import pallas as pl
from jax.experimental.pallas import tpu as pltpu
from jax.sharding import Mesh, PartitionSpec as P

HEAD_WIDTH = 128
GROUP = 3
WIDE = GROUP * HEAD_WIDTH
BLOCK = 128
CHUNK = 512
TOKENS = 2048
SCALE = HEAD_WIDTH ** -0.5
LOG2E = 1.4426950408889634
NEG = -1.0e30
HIGH = lax.Precision.HIGHEST
F32 = jnp.float32
BF16 = jnp.bfloat16
CHUNKS = ((0,), (0, 1), (0, 1, 2), (3,))
P_AT = (0, 1, 3, 6)
Z_AXES = ("zl", "zh")


VMEM = pl.BlockSpec(memory_space=pltpu.VMEM)
SMEM = pl.BlockSpec(memory_space=pltpu.SMEM)


def coords(did_ref):
    d = did_ref[0]
    return d // 64, (d // 16) % 4, (d // 4) % 4, (d // 2) % 2, d % 2


def prep_kernel(did, keys, values, labels, mask, queries, *outs):
    zl, x, y, zh, c = coords(did)
    lab = jnp.broadcast_to(labels[...].astype(F32), (8, BLOCK))
    msk = jnp.broadcast_to(mask[...].astype(F32), (8, BLOCK))
    for k in range(4):
        g = (y + k) % 4
        at = pl.multiple_of(g * HEAD_WIDTH, HEAD_WIDTH)
        kk = keys[:, pl.ds(at, HEAD_WIDTH)].astype(F32)
        vv = values[:, pl.ds(at, HEAD_WIDTH)].astype(F32)
        top = jnp.concatenate([kk, vv], axis=1)
        low = jnp.concatenate([lab, msk], axis=1)
        outs[k][...] = jnp.concatenate([top, low], axis=0).astype(BF16)
        outs[4 + k][...] = queries[:, pl.ds(pl.multiple_of(g * WIDE, HEAD_WIDTH), WIDE)]


def forward_kernel(did, seg, w, q0, q1, q2, q3, *rest):
    kvs = rest[:8]
    plog, p_out, att_out, linv_out, q_out, kv_out, kt_out = rest[8:15]
    qt, kvf, vt, s_buf = rest[15:]
    zl, x, y, zh, c = coords(did)
    for k, ref in enumerate((q0, q1, q2, q3)):
        slot = (y - k + 4) % 4
        for h in range(GROUP):
            one = ref[:, h * HEAD_WIDTH : (h + 1) * HEAD_WIDTH]
            q_out[slot, h * BLOCK : (h + 1) * BLOCK, :] = one
            qt[slot, :, h * BLOCK : (h + 1) * BLOCK] = one.astype(F32).T.astype(BF16)
    for cc in range(2):
        cs = (c + cc) % 2
        for kx in range(4):
            ref = kvs[cc * 4 + kx]
            xs = (x - kx + 4) % 4

            def place(z, carry, ref=ref, cs=cs, xs=xs):
                for k in range(4):
                    ys = (y - k + 4) % 4
                    row = (ys * 4 + (z % 2) * 2 + cs) * BLOCK + ((z // 2) * 4 + xs) * 8
                    kvf[pl.ds(pl.multiple_of(row, 8), 8), :] = ref[z, k].astype(F32)
                return carry

            lax.fori_loop(0, 8, place, 0)

    def turn(b, carry):
        at = pl.multiple_of(b * BLOCK, BLOCK)
        both = kvf[pl.ds(at, BLOCK), :]
        kv_out[pl.ds(at, BLOCK), :] = both.astype(BF16)
        kt_out[:, pl.ds(at, BLOCK)] = both[:, :HEAD_WIDTH].T.astype(BF16)
        vt[:, pl.ds(at, BLOCK)] = both[:, HEAD_WIDTH:].T.astype(BF16)
        return carry

    lax.fori_loop(0, TOKENS // BLOCK, turn, 0)
    j = zh * 2 + c
    key_at = lax.broadcasted_iota(jnp.int32, (BLOCK, BLOCK), 0)
    query_at = lax.broadcasted_iota(jnp.int32, (BLOCK, BLOCK), 1) + j * BLOCK
    for ys in range(4):
        qs = seg[:, pl.ds(pl.multiple_of(ys * CHUNK + j * BLOCK, BLOCK), BLOCK)]
        top = jnp.full((1, WIDE), NEG, F32)
        for i, ch in enumerate(CHUNKS[ys]):
            for b in range(CHUNK // BLOCK):
                row = ch * CHUNK + b * BLOCK
                s = jnp.dot(kv_out[row : row + BLOCK, :HEAD_WIDTH], qt[ys], preferred_element_type=F32)
                if ch == ys:
                    ks = jnp.broadcast_to(seg[:, row : row + BLOCK], (BLOCK, BLOCK)).T
                    ok = (key_at + b * BLOCK <= query_at) & (ks == qs)
                    s = jnp.where(jnp.concatenate([ok] * GROUP, axis=1), s, NEG)
                top = jnp.maximum(top, jnp.max(s, axis=0, keepdims=True))
                at = i * CHUNK + b * BLOCK
                s_buf[at : at + BLOCK, :] = s
        total = jnp.zeros((1, WIDE), F32)
        acc = jnp.zeros((HEAD_WIDTH, WIDE), F32)
        for i, ch in enumerate(CHUNKS[ys]):
            at_p = (P_AT[ys] + i) * CHUNK
            for b in range(CHUNK // BLOCK):
                at = i * CHUNK + b * BLOCK
                p = jnp.exp2((s_buf[at : at + BLOCK, :] - top) * (SCALE * LOG2E))
                total = total + jnp.sum(p, axis=0, keepdims=True)
                p_out[at_p + b * BLOCK : at_p + (b + 1) * BLOCK, :] = p.astype(BF16)
            acc = acc + jnp.dot(
                vt[:, ch * CHUNK : (ch + 1) * CHUNK], p_out[at_p : at_p + CHUNK, :], preferred_element_type=F32
            )
        inv = 1.0 / total
        att = acc * inv
        att_out[ys] = att
        linv_out[ys] = jnp.broadcast_to(inv, (8, WIDE))
        lg = jnp.zeros((8, BLOCK), F32)
        for h in range(GROUP):
            wh = w[:, pl.ds(pl.multiple_of(y * WIDE + h * HEAD_WIDTH, HEAD_WIDTH), HEAD_WIDTH)]
            lg = lg + jnp.dot(wh, att[:, h * BLOCK : (h + 1) * BLOCK], precision=HIGH, preferred_element_type=F32)
        plog[(y - ys + 4) % 4] = lg


def backward_kernel(did, w, l0, l1, l2, l3, g0, g1, g2, g3, p, att, linv, q, kv, kt, *rest):
    dq_outs = rest[:4]
    dkv_outs = rest[4:12]
    hg_out = rest[12]
    lgs, labs, dqb, acc, at16, a16, ds16 = rest[13:]
    zl, x, y, zh, c = coords(did)
    for k, ref in enumerate((l0, l1, l2, l3)):
        src = (y - k + 4) % 4
        for m in range(4):
            ys = (y - m + 4) % 4
            lgs[src, ys] = ref[(m - k) % 4]
    for k, ref in enumerate((g0, g1, g2, g3)):
        labs[(y - k + 4) % 4] = ref[...].astype(F32)[8:16, :]
    acc[...] = jnp.zeros_like(acc)
    loss = jnp.zeros((1, BLOCK), F32)
    hg = [jnp.zeros((8, HEAD_WIDTH), F32) for _ in range(GROUP)]
    row8 = lax.broadcasted_iota(jnp.int32, (8, BLOCK), 0)
    for ys in range(4):
        lg = lgs[0, ys] + lgs[1, ys] + lgs[2, ys] + lgs[3, ys]
        a, b = lg[0:1, :], lg[1:2, :]
        lab = labs[ys, 0:1, :BLOCK]
        mask = labs[ys, 0:1, BLOCK:]
        mx = jnp.maximum(a, b)
        lt = mx + jnp.log(jnp.exp(a - mx) + jnp.exp(b - mx))
        one = lab > 0.5
        loss = loss + mask * (lt - jnp.where(one, b, a))
        da = mask * (jnp.exp(a - lt) - jnp.where(one, 0.0, 1.0))
        db = mask * (jnp.exp(b - lt) - jnp.where(one, 1.0, 0.0))
        dl = jnp.where(row8 == 0, da, jnp.where(row8 == 1, db, 0.0))
        delta = []
        for h in range(GROUP):
            cols = slice(h * BLOCK, (h + 1) * BLOCK)
            wh = w[:, pl.ds(pl.multiple_of(y * WIDE + h * HEAD_WIDTH, HEAD_WIDTH), HEAD_WIDTH)]
            wt = jnp.concatenate([wh] * 16, axis=0).T
            datt = wt[:, 0:1] * da + wt[:, 1:2] * db
            at = att[ys, :, cols]
            inv = linv[ys, 0:1, cols]
            delta.append(jnp.sum(datt * at, axis=0, keepdims=True) * inv)
            scaled = datt * inv
            at16[:, cols] = scaled.astype(BF16)
            a16[cols, :] = scaled.T.astype(BF16)
            hg[h] = hg[h] + lax.dot_general(
                dl, at, (((1,), (1,)), ((), ())), precision=HIGH, preferred_element_type=F32
            )
        delta = jnp.concatenate(delta, axis=1)
        dqt = jnp.zeros((HEAD_WIDTH, WIDE), F32)
        for i, ch in enumerate(CHUNKS[ys]):
            at_p = (P_AT[ys] + i) * CHUNK
            rows = slice(ch * CHUNK, (ch + 1) * CHUNK)
            for b in range(CHUNK // BLOCK):
                row = ch * CHUNK + b * BLOCK
                dp = jnp.dot(kv[row : row + BLOCK, HEAD_WIDTH:], at16[...], preferred_element_type=F32)
                pb = p[at_p + b * BLOCK : at_p + (b + 1) * BLOCK, :].astype(F32)
                ds16[b * BLOCK : (b + 1) * BLOCK, :] = (pb * (dp - delta)).astype(BF16)
            ds = ds16[...]
            dqt = dqt + jnp.dot(kt[:, rows], ds, preferred_element_type=F32)
            acc[rows, :HEAD_WIDTH] += jnp.dot(ds, q[ys], preferred_element_type=F32)
            acc[rows, HEAD_WIDTH:] += jnp.dot(p[at_p : at_p + CHUNK, :], a16[...], preferred_element_type=F32)
        slot = (y - ys + 4) % 4
        for h in range(GROUP):
            cols = slice(h * BLOCK, (h + 1) * BLOCK)
            dqb[slot, :, cols] = (dqt[:, cols].T * SCALE).astype(BF16)
    for k in range(4):
        dq_outs[k][...] = dqb[k]
    for h in range(GROUP):
        hg_out[:, h * HEAD_WIDTH : (h + 1) * HEAD_WIDTH] = hg[h]
    hg_out[2:3, 0:BLOCK] = loss
    for cc in range(2):
        cs = (c + cc) % 2
        for kx in range(4):
            ref = dkv_outs[cc * 4 + kx]
            xs = (x - kx + 4) % 4

            def place(z, carry, ref=ref, cs=cs, xs=xs):
                for k in range(4):
                    ys = (y - k + 4) % 4
                    row = (ys * 4 + (z % 2) * 2 + cs) * BLOCK + ((z // 2) * 4 + xs) * 8
                    piece = acc[pl.ds(pl.multiple_of(row, 8), 8), :]
                    piece = jnp.concatenate([piece[:, :HEAD_WIDTH] * SCALE, piece[:, HEAD_WIDTH:]], axis=1)
                    ref[z, k] = piece.astype(BF16)
                return carry

            lax.fori_loop(0, 8, place, 0)


def finish_kernel(did, d0, d1, d2, d3, r0, r1, r2, r3, h0, h1, h2, h3, qg, gk, gv, hg):
    zl, x, y, zh, c = coords(did)
    for k, (d, r, h) in enumerate(((d0, r0, h0), (d1, r1, h1), (d2, r2, h2), (d3, r3, h3))):
        g = (y + k) % 4
        wide = pl.ds(pl.multiple_of(g * WIDE, HEAD_WIDTH), WIDE)
        narrow = pl.ds(pl.multiple_of(g * HEAD_WIDTH, HEAD_WIDTH), HEAD_WIDTH)
        qg[:, wide] = d[...].astype(F32)
        gk[:, narrow] = r[:, :HEAD_WIDTH]
        gv[:, narrow] = r[:, HEAD_WIDTH:]
        hg[:, wide] = h[...]


def shift(v, axis, size, k):
    return lax.ppermute(v, axis, [(i, (i + k) % size) for i in range(size)])


def like(shape, dtype):
    return jax.ShapeDtypeStruct(shape, dtype)


def per_device(queries, keys, values, head, segments, label_mask, labels):
    did = lax.axis_index(("zl", "x", "y", "zh", "c")).astype(jnp.int32).reshape(1)
    w = jnp.concatenate([head[0].T, jnp.zeros((6, 4 * WIDE), F32)], axis=0)
    prep = pl.pallas_call(
        prep_kernel,
        out_shape=[like((16, 256), BF16)] * 4 + [like((BLOCK, WIDE), BF16)] * 4,
        in_specs=[SMEM] + [VMEM] * 5,
        out_specs=[VMEM] * 8,
        name="prep",
    )(did, keys, values, labels.reshape(1, BLOCK), label_mask.reshape(1, BLOCK), queries[0])
    kvl = [prep[0]] + [shift(prep[k], "y", 4, k) for k in range(1, 4)]
    qs = [prep[4]] + [shift(prep[4 + k], "y", 4, k) for k in range(1, 4)]
    mine = jnp.stack([a[:8] for a in kvl])
    copies = jnp.broadcast_to(mine[None], (8, 4, 8, 256))
    own = lax.all_to_all(copies, Z_AXES, 0, 0, tiled=True)
    over_x = [own] + [shift(own, "x", 4, k) for k in range(1, 4)]
    over_c = [shift(a, "c", 2, 1) for a in over_x]
    plog, p, att, linv, q, kv, kt = pl.pallas_call(
        forward_kernel,
        out_shape=[
            like((4, 8, BLOCK), F32),
            like((7 * CHUNK, WIDE), BF16),
            like((4, HEAD_WIDTH, WIDE), F32),
            like((4, 8, WIDE), F32),
            like((4, WIDE, HEAD_WIDTH), BF16),
            like((TOKENS, 256), BF16),
            like((HEAD_WIDTH, TOKENS), BF16),
        ],
        in_specs=[SMEM] + [VMEM] * 14,
        out_specs=[VMEM] * 7,
        scratch_shapes=[
            pltpu.VMEM((4, HEAD_WIDTH, WIDE), BF16),
            pltpu.VMEM((TOKENS, 256), F32),
            pltpu.VMEM((HEAD_WIDTH, TOKENS), BF16),
            pltpu.VMEM((3 * CHUNK, WIDE), F32),
        ],
        name="forward",
    )(did, segments.reshape(1, TOKENS), w, *qs, *over_x, *over_c)
    logs = [plog] + [shift(plog, "y", 4, k) for k in range(1, 4)]
    outs = pl.pallas_call(
        backward_kernel,
        out_shape=[like((BLOCK, WIDE), BF16)] * 4 + [like((8, 4, 8, 256), BF16)] * 8 + [like((8, WIDE), F32)],
        in_specs=[SMEM] + [VMEM] * 15,
        out_specs=[VMEM] * 13,
        scratch_shapes=[
            pltpu.VMEM((4, 4, 8, BLOCK), F32),
            pltpu.VMEM((4, 8, 256), F32),
            pltpu.VMEM((4, BLOCK, WIDE), BF16),
            pltpu.VMEM((TOKENS, 256), F32),
            pltpu.VMEM((HEAD_WIDTH, WIDE), BF16),
            pltpu.VMEM((WIDE, HEAD_WIDTH), BF16),
            pltpu.VMEM((CHUNK, WIDE), BF16),
        ],
        name="backward",
    )(did, w, *logs, *kvl, p, att, linv, q, kv, kt)
    dq, own_d, far_d, hg = outs[:4], outs[4:8], outs[8:12], outs[12]
    far = [shift(a, "c", 2, 1) for a in far_d]
    by_x = [(a.astype(F32) + b.astype(F32)).astype(BF16) for a, b in zip(own_d, far)]
    got = [by_x[0]] + [shift(by_x[k], "x", 4, -k) for k in range(1, 4)]
    by_z = sum(a.astype(F32) for a in got).astype(BF16)
    pieces = lax.all_to_all(by_z, Z_AXES, 0, 0, tiled=True)
    by_y = jnp.sum(pieces.astype(F32), axis=0)
    grads = [by_y[0]] + [shift(by_y[k], "y", 4, -k) for k in range(1, 4)]
    dqs = [dq[0]] + [shift(dq[k], "y", 4, -k) for k in range(1, 4)]
    hg = hg + shift(hg, "c", 2, 1)
    hg = hg + shift(hg, "zh", 2, 1)
    hgs = [hg] + [shift(hg, "y", 4, -k) for k in range(1, 4)]
    query_gradient, grad_keys, grad_values, head_t = pl.pallas_call(
        finish_kernel,
        out_shape=[like((BLOCK, 4 * WIDE), F32), like((8, 512), F32), like((8, 512), F32), like((8, 4 * WIDE), F32)],
        in_specs=[SMEM] + [VMEM] * 12,
        out_specs=[VMEM] * 4,
        name="finish",
    )(did, *dqs, *grads, *hgs)
    loss = (jnp.sum(hg[2, :BLOCK]) / TOKENS).reshape(1)
    return loss, query_gradient[None], grad_keys, grad_values, head_t[:2].T[None]


def solution(mesh):
    fine = Mesh(mesh.devices.reshape(4, 4, 4, 2, 2), ("zl", "x", "y", "zh", "c"))
    layer, ctx = ("zl", "x"), ("y", "zh", "c")
    return jax.shard_map(
        per_device,
        mesh=fine,
        in_specs=(
            P(layer, ctx, None),
            P(ctx + layer, None),
            P(ctx + layer, None),
            P(layer, None, None),
            P(),
            P(ctx),
            P(ctx),
        ),
        out_specs=(
            P(layer),
            P(layer, ctx, None),
            P(ctx + layer, None),
            P(ctx + layer, None),
            P(layer, None, None),
        ),
        check_vma=False,
    )
```

```python
import jax
import jax.numpy as jnp
from jax import lax
from jax.experimental import pallas as pl
from jax.experimental.pallas import tpu as pltpu
from jax.sharding import Mesh, PartitionSpec as P

HEAD_WIDTH = 128
GROUP = 3
WIDE = GROUP * HEAD_WIDTH
BLOCK = 128
CHUNK = 512
TOKENS = 2048
SCALE = HEAD_WIDTH ** -0.5
LOG2E = 1.4426950408889634
NEG = -1.0e30
HIGH = lax.Precision.HIGHEST
F32 = jnp.float32
BF16 = jnp.bfloat16
CHUNKS = ((0,), (0, 1), (0, 1, 2), (3,))
P_AT = (0, 1, 3, 6)
Z_AXES = ("zl", "zh")


VMEM = pl.BlockSpec(memory_space=pltpu.VMEM)
SMEM = pl.BlockSpec(memory_space=pltpu.SMEM)


def coords(did_ref):
    d = did_ref[0]
    return d // 64, (d // 16) % 4, (d // 4) % 4, (d // 2) % 2, d % 2


def prep_kernel(did, keys, values, labels, mask, queries, *outs):
    zl, x, y, zh, c = coords(did)
    lab = jnp.broadcast_to(labels[...].astype(F32), (8, BLOCK))
    msk = jnp.broadcast_to(mask[...].astype(F32), (8, BLOCK))
    pad = jnp.zeros((16, HEAD_WIDTH), F32)
    for k in range(4):
        g = (y + k) % 4
        at = pl.multiple_of(g * HEAD_WIDTH, HEAD_WIDTH)
        kk = jnp.concatenate([keys[:, pl.ds(at, HEAD_WIDTH)].astype(F32), lab], axis=0)
        vv = jnp.concatenate([values[:, pl.ds(at, HEAD_WIDTH)].astype(F32), msk], axis=0)
        outs[k][BLOCK:, :] = jnp.concatenate([kk, vv, pad], axis=1).astype(BF16)
        outs[k][:BLOCK, :] = queries[:, pl.ds(pl.multiple_of(g * WIDE, HEAD_WIDTH), WIDE)]


def head_row(w, y, h, cls):
    at = pl.multiple_of(y * WIDE + h * HEAD_WIDTH, HEAD_WIDTH)
    return w[cls : cls + 1, pl.ds(at, HEAD_WIDTH)]


def forward_kernel(did, seg, w, q0, q1, q2, q3, *rest):
    kvs = rest[:8]
    plog, p_out, att_out, linv_out, q_out, kv_out, kt_out = rest[8:15]
    qt, kvf, vt, s_buf = rest[15:]
    zl, x, y, zh, c = coords(did)
    row8 = lax.broadcasted_iota(jnp.int32, (8, HEAD_WIDTH), 0)
    for k, ref in enumerate((q0, q1, q2, q3)):
        slot = (y - k + 4) % 4
        for h in range(GROUP):
            one = ref[:BLOCK, h * HEAD_WIDTH : (h + 1) * HEAD_WIDTH]
            q_out[slot, h * BLOCK : (h + 1) * BLOCK, :] = one
            qt[slot, :, h * BLOCK : (h + 1) * BLOCK] = one.astype(F32).T.astype(BF16)
    for cc in range(2):
        cs = (c + cc) % 2
        for kx in range(4):
            ref = kvs[cc * 4 + kx]
            xs = (x - kx + 4) % 4

            def place(z, carry, ref=ref, cs=cs, xs=xs):
                for k in range(4):
                    ys = (y - k + 4) % 4
                    row = (ys * 4 + (z % 2) * 2 + cs) * BLOCK + ((z // 2) * 4 + xs) * 8
                    kvf[pl.ds(pl.multiple_of(row, 8), 8), :] = ref[z, k].astype(F32)
                return carry

            lax.fori_loop(0, 8, place, 0)

    def turn(b, carry):
        at = pl.multiple_of(b * BLOCK, BLOCK)
        both = kvf[pl.ds(at, BLOCK), :]
        kv_out[pl.ds(at, BLOCK), :] = both.astype(BF16)
        kt_out[:, pl.ds(at, BLOCK)] = both[:, :HEAD_WIDTH].T.astype(BF16)
        vt[:, pl.ds(at, BLOCK)] = both[:, HEAD_WIDTH:].T.astype(BF16)
        return carry

    lax.fori_loop(0, TOKENS // BLOCK, turn, 0)
    j = zh * 2 + c
    key_at = lax.broadcasted_iota(jnp.int32, (BLOCK, BLOCK), 0)
    query_at = lax.broadcasted_iota(jnp.int32, (BLOCK, BLOCK), 1) + j * BLOCK
    for ys in range(4):
        qs = seg[:, pl.ds(pl.multiple_of(ys * CHUNK + j * BLOCK, BLOCK), BLOCK)]
        top = jnp.full((1, WIDE), NEG, F32)
        for i, ch in enumerate(CHUNKS[ys]):
            for b in range(CHUNK // BLOCK):
                row = ch * CHUNK + b * BLOCK
                s = jnp.dot(kv_out[row : row + BLOCK, :HEAD_WIDTH], qt[ys], preferred_element_type=F32)
                if ch == ys:
                    ks = jnp.broadcast_to(seg[:, row : row + BLOCK], (BLOCK, BLOCK)).T
                    ok = (key_at + b * BLOCK <= query_at) & (ks == qs)
                    s = jnp.where(jnp.concatenate([ok] * GROUP, axis=1), s, NEG)
                top = jnp.maximum(top, jnp.max(s, axis=0, keepdims=True))
                at = i * CHUNK + b * BLOCK
                s_buf[at : at + BLOCK, :] = s
        total = jnp.zeros((1, WIDE), F32)
        acc = jnp.zeros((HEAD_WIDTH, WIDE), F32)
        for i, ch in enumerate(CHUNKS[ys]):
            at_p = (P_AT[ys] + i) * CHUNK
            for b in range(CHUNK // BLOCK):
                at = i * CHUNK + b * BLOCK
                p = jnp.exp2((s_buf[at : at + BLOCK, :] - top) * (SCALE * LOG2E))
                total = total + jnp.sum(p, axis=0, keepdims=True)
                p_out[at_p + b * BLOCK : at_p + (b + 1) * BLOCK, :] = p.astype(BF16)
            acc = acc + jnp.dot(
                vt[:, ch * CHUNK : (ch + 1) * CHUNK], p_out[at_p : at_p + CHUNK, :], preferred_element_type=F32
            )
        inv = 1.0 / total
        att = acc * inv
        att_out[ys] = att
        linv_out[ys] = jnp.broadcast_to(inv, (8, WIDE))
        lg = jnp.zeros((8, BLOCK), F32)
        for h in range(GROUP):
            wh = jnp.where(row8 == 0, head_row(w, y, h, 0), jnp.where(row8 == 1, head_row(w, y, h, 1), 0.0))
            lg = lg + jnp.dot(wh, att[:, h * BLOCK : (h + 1) * BLOCK], precision=HIGH, preferred_element_type=F32)
        plog[(y - ys + 4) % 4] = lg


def backward_kernel(did, w, l0, l1, l2, l3, g0, g1, g2, g3, p, att, linv, q, kv, kt, *rest):
    dq_outs = rest[:4]
    dkv_outs = rest[4:6]
    lgs, labs, dqb, acc, at16, a16, ds16, wt = rest[6:]
    zl, x, y, zh, c = coords(did)
    for k, ref in enumerate((l0, l1, l2, l3)):
        src = (y - k + 4) % 4
        for m in range(4):
            ys = (y - m + 4) % 4
            lgs[src, ys] = ref[(m - k) % 4]
    for k, ref in enumerate((g0, g1, g2, g3)):
        labs[(y - k + 4) % 4] = ref[BLOCK:, :256].astype(F32)[8:16, :]
    for h in range(GROUP):
        for cls in range(2):
            wt[cls, h] = jnp.broadcast_to(head_row(w, y, h, cls), (BLOCK, HEAD_WIDTH)).T
    acc[...] = jnp.zeros_like(acc)
    loss = jnp.zeros((1, BLOCK), F32)
    hg = [jnp.zeros((8, HEAD_WIDTH), F32) for _ in range(GROUP)]
    row8 = lax.broadcasted_iota(jnp.int32, (8, BLOCK), 0)
    for ys in range(4):
        lg = lgs[0, ys] + lgs[1, ys] + lgs[2, ys] + lgs[3, ys]
        a, b = lg[0:1, :], lg[1:2, :]
        lab = labs[ys, 0:1, :BLOCK]
        mask = labs[ys, 0:1, BLOCK:]
        mx = jnp.maximum(a, b)
        lt = mx + jnp.log(jnp.exp(a - mx) + jnp.exp(b - mx))
        one = lab > 0.5
        loss = loss + mask * (lt - jnp.where(one, b, a))
        da = mask * (jnp.exp(a - lt) - jnp.where(one, 0.0, 1.0))
        db = mask * (jnp.exp(b - lt) - jnp.where(one, 1.0, 0.0))
        dl = jnp.where(row8 == 0, da, jnp.where(row8 == 1, db, 0.0))
        delta = []
        for h in range(GROUP):
            cols = slice(h * BLOCK, (h + 1) * BLOCK)
            datt = wt[0, h] * da + wt[1, h] * db
            at = att[ys, :, cols]
            inv = linv[ys, 0:1, cols]
            delta.append(jnp.sum(datt * at, axis=0, keepdims=True) * inv)
            scaled = datt * inv
            at16[:, cols] = scaled.astype(BF16)
            a16[cols, :] = scaled.T.astype(BF16)
            hg[h] = hg[h] + lax.dot_general(
                dl, at, (((1,), (1,)), ((), ())), precision=HIGH, preferred_element_type=F32
            )
        delta = jnp.concatenate(delta, axis=1)
        dqt = jnp.zeros((HEAD_WIDTH, WIDE), F32)
        for i, ch in enumerate(CHUNKS[ys]):
            at_p = (P_AT[ys] + i) * CHUNK
            rows = slice(ch * CHUNK, (ch + 1) * CHUNK)
            for b in range(CHUNK // BLOCK):
                row = ch * CHUNK + b * BLOCK
                dp = jnp.dot(kv[row : row + BLOCK, HEAD_WIDTH:], at16[...], preferred_element_type=F32)
                pb = p[at_p + b * BLOCK : at_p + (b + 1) * BLOCK, :].astype(F32)
                ds16[b * BLOCK : (b + 1) * BLOCK, :] = (pb * (dp - delta)).astype(BF16)
            ds = ds16[...]
            dqt = dqt + jnp.dot(kt[:, rows], ds, preferred_element_type=F32)
            acc[rows, :HEAD_WIDTH] += jnp.dot(ds, q[ys], preferred_element_type=F32)
            acc[rows, HEAD_WIDTH:] += jnp.dot(p[at_p : at_p + CHUNK, :], a16[...], preferred_element_type=F32)
        slot = (y - ys + 4) % 4
        for h in range(GROUP):
            cols = slice(h * BLOCK, (h + 1) * BLOCK)
            dqb[slot, :, cols] = (dqt[:, cols].T * SCALE).astype(BF16)
    for k in range(4):
        dq_outs[k][...] = dqb[k]
    hg[0] = jnp.where(row8 == 2, loss, hg[0])
    both = split_up(jnp.concatenate(hg, axis=1))
    tail = jnp.concatenate([both[:, 256:], jnp.zeros((8, BLOCK), F32)], axis=1)
    for cc in range(2):
        cs = (c + cc) % 2
        ref = dkv_outs[cc]

        def place(z, carry, ref=ref, cs=cs):
            for kx in range(4):
                xs = (x - kx + 4) % 4
                for k in range(4):
                    ys = (y - k + 4) % 4
                    row = (ys * 4 + (z % 2) * 2 + cs) * BLOCK + ((z // 2) * 4 + xs) * 8
                    piece = acc[pl.ds(pl.multiple_of(row, 8), 8), :]
                    piece = jnp.concatenate([piece[:, :HEAD_WIDTH] * SCALE, piece[:, HEAD_WIDTH:]], axis=1)
                    ref[z, kx * 4 + k] = piece.astype(BF16)
            here = jnp.where(z // 2 == zl, 1.0, 0.0)
            ref[z, 16] = (both[:, :256] * here).astype(BF16)
            ref[z, 17] = (tail * here).astype(BF16)
            return carry

        lax.fori_loop(0, 8, place, 0)


def split_up(v):
    high = v.astype(BF16).astype(F32)
    return jnp.concatenate([high[:4], (v - high)[:4]], axis=0)


def joined(v):
    one = v[:4] + v[4:]
    return jnp.concatenate([one, one], axis=0)


def core_kernel(own, far, *outs):
    def add(z, carry):
        for kx in range(4):
            at = slice(4 * kx, 4 * kx + 4)
            outs[kx][z, 0:4] = (own[z, at].astype(F32) + far[z, at].astype(F32)).astype(BF16)
        for k in range(2):
            v = joined(own[z, 16 + k].astype(F32)) + joined(far[z, 16 + k].astype(F32))
            outs[0][z, 4 + k] = split_up(v).astype(BF16)
        return carry

    lax.fori_loop(0, 8, add, 0)


def x_kernel(b0, b1, b2, b3, out):
    def add(z, carry):
        v = b0[z, 0:4].astype(F32) + b1[z].astype(F32) + b2[z].astype(F32) + b3[z].astype(F32)
        out[z, 0:4] = v.astype(BF16)
        out[z, 4:6] = b0[z, 4:6]
        return carry

    lax.fori_loop(0, 8, add, 0)


def pack_kernel(pieces, d0, d1, d2, d3, *outs):
    pad = jnp.zeros((16, HEAD_WIDTH), F32)
    hg = []
    for k in range(2):
        v = joined(pieces[0, 4 + k].astype(F32))
        for z in range(1, 8):
            v = v + joined(pieces[z, 4 + k].astype(F32))
        hg.append(split_up(v))
    hg = jnp.concatenate([hg[0], hg[1][:, :BLOCK]], axis=1)
    hg = jnp.concatenate([hg, jnp.zeros_like(hg)], axis=0).astype(BF16)
    for k, d in enumerate((d0, d1, d2, d3)):
        v = pieces[0, k].astype(F32)
        for z in range(1, 8):
            v = v + pieces[z, k].astype(F32)
        high = v.astype(BF16).astype(F32)
        v = jnp.concatenate([high, v - high], axis=0)
        outs[k][:BLOCK, :] = d[...]
        outs[k][BLOCK : BLOCK + 16, :] = jnp.concatenate([v, pad], axis=1).astype(BF16)
        outs[k][BLOCK + 16 :, :] = hg


def finish_kernel(did, r0, r1, r2, r3, qg, gk, gv, hg, loss):
    zl, x, y, zh, c = coords(did)
    for k, r in enumerate((r0, r1, r2, r3)):
        g = (y + k) % 4
        wide = pl.ds(pl.multiple_of(g * WIDE, HEAD_WIDTH), WIDE)
        narrow = pl.ds(pl.multiple_of(g * HEAD_WIDTH, HEAD_WIDTH), HEAD_WIDTH)
        qg[:, wide] = r[:BLOCK, :].astype(F32)
        v = r[BLOCK : BLOCK + 16, :256].astype(F32)
        v = v[:8] + v[8:]
        gk[:, narrow] = v[:, :HEAD_WIDTH]
        gv[:, narrow] = v[:, HEAD_WIDTH:]
        v = joined(r[BLOCK + 16 :, :].astype(F32)[:8])
        hg[:, wide] = v[0:2, :]
        if k == 0:
            loss[0] = jnp.sum(v[2:3, :BLOCK]) * (1.0 / TOKENS)


def shift(v, axis, size, k):
    return lax.ppermute(v, axis, [(i, (i + k) % size) for i in range(size)])


def like(shape, dtype):
    return jax.ShapeDtypeStruct(shape, dtype)


def call(kernel, name, out_shape, specs, out_specs=None, scratch=()):
    return pl.pallas_call(
        kernel,
        out_shape=out_shape,
        in_specs=specs,
        out_specs=out_specs or [VMEM] * len(out_shape),
        scratch_shapes=list(scratch),
        compiler_params=pltpu.CompilerParams(vmem_limit_bytes=20 << 20),
        name=name,
    )


def per_device(queries, keys, values, head, segments, label_mask, labels):
    did = lax.axis_index(("zl", "x", "y", "zh", "c")).astype(jnp.int32).reshape(1)
    w = head[0].T
    prep = call(prep_kernel, "prep", [like((BLOCK + 16, WIDE), BF16)] * 4, [SMEM] + [VMEM] * 5)(
        did, keys, values, labels.reshape(1, BLOCK), label_mask.reshape(1, BLOCK), queries[0]
    )
    packs = [prep[0]] + [shift(prep[k], "y", 4, k) for k in range(1, 4)]
    mine = jnp.stack([a[BLOCK : BLOCK + 8, :256] for a in packs])
    copies = jnp.broadcast_to(mine[None], (8, 4, 8, 256))
    own = lax.all_to_all(copies, Z_AXES, 0, 0, tiled=True)
    over_x = [own] + [shift(own, "x", 4, k) for k in range(1, 4)]
    over_c = [shift(a, "c", 2, 1) for a in over_x]
    plog, p, att, linv, q, kv, kt = call(
        forward_kernel,
        "forward",
        [
            like((4, 8, BLOCK), F32),
            like((7 * CHUNK, WIDE), BF16),
            like((4, HEAD_WIDTH, WIDE), F32),
            like((4, 8, WIDE), F32),
            like((4, WIDE, HEAD_WIDTH), BF16),
            like((TOKENS, 256), BF16),
            like((HEAD_WIDTH, TOKENS), BF16),
        ],
        [SMEM] + [VMEM] * 14,
        scratch=[
            pltpu.VMEM((4, HEAD_WIDTH, WIDE), BF16),
            pltpu.VMEM((TOKENS, 256), F32),
            pltpu.VMEM((HEAD_WIDTH, TOKENS), BF16),
            pltpu.VMEM((3 * CHUNK, WIDE), F32),
        ],
    )(did, segments.reshape(1, TOKENS), w, *packs, *over_x, *over_c)
    logs = [plog] + [shift(plog, "y", 4, k) for k in range(1, 4)]
    *dq, own_d, far_d = call(
        backward_kernel,
        "backward",
        [like((BLOCK, WIDE), BF16)] * 4 + [like((8, 18, 8, 256), BF16)] * 2,
        [SMEM] + [VMEM] * 15,
        scratch=[
            pltpu.VMEM((4, 4, 8, BLOCK), F32),
            pltpu.VMEM((4, 8, 256), F32),
            pltpu.VMEM((4, BLOCK, WIDE), BF16),
            pltpu.VMEM((TOKENS, 256), F32),
            pltpu.VMEM((HEAD_WIDTH, WIDE), BF16),
            pltpu.VMEM((WIDE, HEAD_WIDTH), BF16),
            pltpu.VMEM((CHUNK, WIDE), BF16),
            pltpu.VMEM((2, GROUP, HEAD_WIDTH, BLOCK), F32),
        ],
    )(did, w, *logs, *packs, p, att, linv, q, kv, kt)
    far = shift(far_d, "c", 2, 1)
    by_x = call(core_kernel, "core_sum", [like((8, 6, 8, 256), BF16)] + [like((8, 4, 8, 256), BF16)] * 3, [VMEM] * 2)(
        own_d, far
    )
    got = [by_x[0]] + [shift(by_x[k], "x", 4, -k) for k in range(1, 4)]
    (by_z,) = call(x_kernel, "x_sum", [like((8, 6, 8, 256), BF16)], [VMEM] * 4)(*got)
    pieces = lax.all_to_all(by_z, Z_AXES, 0, 0, tiled=True)
    pay = call(pack_kernel, "pack", [like((BLOCK + 32, WIDE), BF16)] * 4, [VMEM] * 5)(pieces, *dq)
    back = [pay[0]] + [shift(pay[k], "y", 4, -k) for k in range(1, 4)]
    query_gradient, grad_keys, grad_values, head_t, loss = call(
        finish_kernel,
        "finish",
        [
            like((BLOCK, 4 * WIDE), F32),
            like((8, 512), F32),
            like((8, 512), F32),
            like((2, 4 * WIDE), F32),
            like((1,), F32),
        ],
        [SMEM] + [VMEM] * 4,
        [VMEM] * 4 + [SMEM],
    )(did, *back)
    return loss, query_gradient[None], grad_keys, grad_values, head_t.T[None]


def solution(mesh):
    fine = Mesh(mesh.devices.reshape(4, 4, 4, 2, 2), ("zl", "x", "y", "zh", "c"))
    layer, ctx = ("zl", "x"), ("y", "zh", "c")
    return jax.shard_map(
        per_device,
        mesh=fine,
        in_specs=(
            P(layer, ctx, None),
            P(ctx + layer, None),
            P(ctx + layer, None),
            P(layer, None, None),
            P(),
            P(ctx),
            P(ctx),
        ),
        out_specs=(
            P(layer),
            P(layer, ctx, None),
            P(ctx + layer, None),
            P(ctx + layer, None),
            P(layer, None, None),
        ),
        check_vma=False,
    )
```

```python
import jax
import jax.numpy as jnp
from jax import lax
from jax.experimental import pallas as pl
from jax.experimental.pallas import tpu as pltpu
from jax.sharding import Mesh, PartitionSpec as P

HEAD_WIDTH = 128
GROUP = 3
WIDE = GROUP * HEAD_WIDTH
BLOCK = 128
CHUNK = 512
TOKENS = 2048
SCALE = HEAD_WIDTH ** -0.5
LOG2E = 1.4426950408889634
NEG = -1.0e30
F32 = jnp.float32
BF16 = jnp.bfloat16
CHUNKS = ((0,), (0, 1), (0, 1, 2), (3,))
P_AT = (0, 1, 3, 6)
YZ_AXES = ("zl", "y", "zh")


VMEM = pl.BlockSpec(memory_space=pltpu.VMEM)
HBM = pl.BlockSpec(memory_space=pltpu.HBM)
SMEM = pl.BlockSpec(memory_space=pltpu.SMEM)


def coords(did_ref):
    d = did_ref[0]
    return d // 64, (d // 16) % 4, (d // 4) % 4, (d // 2) % 2, d % 2


def prep_kernel(did, keys, values, labels, mask, queries, w, seg, kv_out, q0, q1, q2, q3, w_out, seg_out, kb, vb, lb, mb, sems):
    zl, x, y, zh, c = coords(did)
    outs = (q0, q1, q2, q3)
    early = [
        pltpu.make_async_copy(keys, kb, sems.at[0]),
        pltpu.make_async_copy(values, vb, sems.at[1]),
        pltpu.make_async_copy(labels, lb, sems.at[2]),
        pltpu.make_async_copy(mask, mb, sems.at[3]),
    ]
    late = [pltpu.make_async_copy(w, w_out, sems.at[4]), pltpu.make_async_copy(seg, seg_out, sems.at[5])]
    for k in range(4):
        g = pl.multiple_of(((y + k) % 4) * WIDE, HEAD_WIDTH)
        late.append(pltpu.make_async_copy(queries.at[:, pl.ds(g, WIDE)], outs[k].at[pl.ds(0, BLOCK)], sems.at[6 + k]))
    for copy in early + late:
        copy.start()
    for copy in early:
        copy.wait()
    for g in range(4):
        cols = slice(g * HEAD_WIDTH, (g + 1) * HEAD_WIDTH)
        both = jnp.concatenate([kb[:, cols], vb[:, cols]], axis=1)
        for zl_to in range(4):
            for zh_to in range(2):
                kv_out[zl_to, g, zh_to] = both
    lab = jnp.broadcast_to(lb[...].astype(F32), (16, BLOCK))
    msk = jnp.broadcast_to(mb[...].astype(F32), (16, BLOCK))
    tail = jnp.concatenate([lab, msk, lab], axis=1).astype(BF16)
    for k in range(4):
        outs[k][BLOCK:, :] = tail
    for copy in late:
        copy.wait()


def head_diff(w, y, h):
    at = pl.multiple_of(y * WIDE + h * HEAD_WIDTH, HEAD_WIDTH)
    return w[0:1, pl.ds(at, HEAD_WIDTH)] - w[1:2, pl.ds(at, HEAD_WIDTH)]


def halves(v):
    high = v.astype(BF16).astype(F32)
    return high, v - high


def stack8(rows):
    at = lax.broadcasted_iota(jnp.int32, (8, rows[0].shape[1]), 0)
    out = jnp.zeros((8, rows[0].shape[1]), F32)
    for r, row in enumerate(rows):
        out = jnp.where(at == r, row, out)
    return out


def on_both(v):
    high, low = halves(v)
    return jnp.concatenate([high, low], axis=0).astype(BF16)


def forward_kernel(did, seg, w, q0, q1, q2, q3, *rest):
    kvs = rest[:8]
    plog, p_out, inv_out, delta_out, qt, kv_out, kt_out, u_out = rest[8:16]
    kvf, vt, s_buf, u_rows = rest[16:]
    zl, x, y, zh, c = coords(did)
    for k, ref in enumerate((q0, q1, q2, q3)):
        slot = (y - k + 4) % 4
        for h in range(GROUP):
            one = ref[:BLOCK, h * HEAD_WIDTH : (h + 1) * HEAD_WIDTH]
            qt[slot, :, h * BLOCK : (h + 1) * BLOCK] = one.astype(F32).T.astype(BF16)
    for cc in range(2):
        cs = (c + cc) % 2
        for kx in range(4):
            ref = kvs[cc * 4 + kx]
            xs = (x - kx + 4) % 4

            def place(zl_from, carry, ref=ref, cs=cs, xs=xs):
                for ys in range(4):
                    for zh_from in range(2):
                        row = (ys * 4 + zh_from * 2 + cs) * BLOCK + (zl_from * 4 + xs) * 8
                        kvf[pl.ds(pl.multiple_of(row, 8), 8), :] = ref[zl_from, ys, zh_from].astype(F32)
                return carry

            lax.fori_loop(0, 4, place, 0)
    diffs = stack8([head_diff(w, y, h) for h in range(GROUP)])
    diffs16 = on_both(diffs)
    ones = stack8([jnp.zeros((1, BLOCK), F32)] * GROUP + [jnp.ones((1, BLOCK), F32)])

    def turn(b, carry):
        at = pl.multiple_of(b * BLOCK, BLOCK)
        both = kvf[pl.ds(at, BLOCK), :]
        kv_out[pl.ds(at, BLOCK), :] = both.astype(BF16)
        kt_out[:, pl.ds(at, BLOCK)] = both[:, :HEAD_WIDTH].T.astype(BF16)
        part = jnp.dot(diffs16, both[:, HEAD_WIDTH:].T.astype(BF16), preferred_element_type=F32)
        u = part[:8] + part[8:]
        high, low = halves(u)
        u_rows[:, pl.ds(at, BLOCK)] = jnp.concatenate([high + ones, low], axis=0).astype(BF16)
        wide = jnp.concatenate([u, jnp.zeros((BLOCK - 8, BLOCK), F32)], axis=0)
        u_out[pl.ds(at, BLOCK), :] = wide.T
        return carry

    lax.fori_loop(0, TOKENS // BLOCK, turn, 0)
    j = zh * 2 + c
    key_at = lax.broadcasted_iota(jnp.int32, (BLOCK, BLOCK), 0)
    query_at = lax.broadcasted_iota(jnp.int32, (BLOCK, BLOCK), 1) + j * BLOCK
    for ys in range(4):
        qs = seg[:, pl.ds(pl.multiple_of(ys * CHUNK + j * BLOCK, BLOCK), BLOCK)]
        top = jnp.full((1, WIDE), NEG, F32)
        for i, ch in enumerate(CHUNKS[ys]):
            for b in range(CHUNK // BLOCK):
                row = ch * CHUNK + b * BLOCK
                s = jnp.dot(kv_out[row : row + BLOCK, :HEAD_WIDTH], qt[ys], preferred_element_type=F32)
                if ch == ys:
                    ks = jnp.broadcast_to(seg[:, row : row + BLOCK], (BLOCK, BLOCK)).T
                    ok = (key_at + b * BLOCK <= query_at) & (ks == qs)
                    s = jnp.where(jnp.concatenate([ok] * GROUP, axis=1), s, NEG)
                top = jnp.maximum(top, jnp.max(s, axis=0, keepdims=True))
                at = i * CHUNK + b * BLOCK
                s_buf[at : at + BLOCK, :] = s
        sums = jnp.zeros((16, WIDE), F32)
        for i, ch in enumerate(CHUNKS[ys]):
            at_p = (P_AT[ys] + i) * CHUNK
            for b in range(CHUNK // BLOCK):
                at = i * CHUNK + b * BLOCK
                p = jnp.exp2((s_buf[at : at + BLOCK, :] - top) * (SCALE * LOG2E))
                p_out[at_p + b * BLOCK : at_p + (b + 1) * BLOCK, :] = p.astype(BF16)
            sums = sums + jnp.dot(
                u_rows[:, ch * CHUNK : (ch + 1) * CHUNK], p_out[at_p : at_p + CHUNK, :], preferred_element_type=F32
            )
        inv = 1.0 / sums[GROUP : GROUP + 1, :]
        both = (sums[:8] + sums[8:]) * inv
        delta = jnp.concatenate([both[h : h + 1, h * BLOCK : (h + 1) * BLOCK] for h in range(GROUP)], axis=1)
        inv_out[ys] = jnp.broadcast_to(inv, (8, WIDE))
        delta_out[ys] = jnp.broadcast_to(delta, (8, WIDE))
        lg = delta[:, :BLOCK] + delta[:, BLOCK : 2 * BLOCK] + delta[:, 2 * BLOCK :]
        plog[(y - ys + 4) % 4] = jnp.broadcast_to(lg, (8, BLOCK))


def middle_kernel(p, delta, u, kt, g_out, dq_out):
    for ys in range(4):
        dqt = jnp.zeros((HEAD_WIDTH, WIDE), F32)
        for i, ch in enumerate(CHUNKS[ys]):
            at_p = (P_AT[ys] + i) * CHUNK
            for b in range(CHUNK // BLOCK):
                row = ch * CHUNK + b * BLOCK
                at = slice(at_p + b * BLOCK, at_p + (b + 1) * BLOCK)
                ub = jnp.concatenate(
                    [jnp.broadcast_to(u[row : row + BLOCK, h : h + 1], (BLOCK, BLOCK)) for h in range(GROUP)], axis=1
                )
                g_out[at, :] = (p[at, :].astype(F32) * (ub - delta[ys, 0:1, :])).astype(BF16)
            dqt = dqt + jnp.dot(
                kt[:, ch * CHUNK : (ch + 1) * CHUNK], g_out[at_p : at_p + CHUNK, :], preferred_element_type=F32
            )
        dq_out[ys] = dqt


NT = (((1,), (1,)), ((), ()))


def backward_kernel(did, w, l0, l1, l2, l3, g0, g1, g2, g3, p, g, inv, qt, kv, dqt, *rest):
    dq_outs = rest[:4]
    dkv_outs = rest[4:6]
    lgs, labs, dqb, acc, ct = rest[6:]
    zl, x, y, zh, c = coords(did)
    for k, ref in enumerate((l0, l1, l2, l3)):
        src = (y - k + 4) % 4
        for m in range(4):
            ys = (y - m + 4) % 4
            lgs[src, ys] = ref[(m - k) % 4]
    for k, ref in enumerate((g0, g1, g2, g3)):
        labs[(y - k + 4) % 4] = ref[BLOCK:, :256].astype(F32)[8:16, :]
    diffs = [head_diff(w, y, h) for h in range(GROUP)]
    wt = jnp.concatenate([jnp.broadcast_to(d, (BLOCK, HEAD_WIDTH)).T for d in diffs], axis=1)
    head_of = lax.broadcasted_iota(jnp.int32, (8, WIDE), 1) // BLOCK
    head_at = lax.broadcasted_iota(jnp.int32, (8, WIDE), 0)
    loss = jnp.zeros((1, BLOCK), F32)
    seen = set()
    for ys in range(4):
        z = (lgs[0, ys] + lgs[1, ys] + lgs[2, ys] + lgs[3, ys])[0:1, :]
        one = labs[ys, 0:1, :BLOCK] > 0.5
        mask = labs[ys, 0:1, BLOCK:]
        a = jnp.where(one, z, -z)
        e = jnp.exp(-jnp.abs(a))
        loss = loss + mask * (jnp.maximum(a, 0.0) + jnp.log(1.0 + e))
        sig = jnp.where(a >= 0.0, 1.0, e) / (1.0 + e)
        d0 = mask * jnp.where(one, sig, -sig)
        f = jnp.concatenate([d0] * GROUP, axis=1) * inv[ys, 0:1, :]
        fs = f * SCALE
        at16 = (wt * f).astype(BF16)
        qf = (qt[ys].astype(F32) * fs).astype(BF16)
        fm = on_both(jnp.where(head_of == head_at, f, 0.0))
        for i, ch in enumerate(CHUNKS[ys]):
            at = slice((P_AT[ys] + i) * CHUNK, (P_AT[ys] + i + 1) * CHUNK)
            rows = slice(ch * CHUNK, (ch + 1) * CHUNK)
            dk = lax.dot_general(g[at, :], qf, NT, preferred_element_type=F32)
            dv = lax.dot_general(p[at, :], at16, NT, preferred_element_type=F32)
            cs = lax.dot_general(fm, p[at, :], NT, preferred_element_type=F32)
            cs = cs[:8] + cs[8:]
            if ch in seen:
                acc[rows, :HEAD_WIDTH] += dk
                acc[rows, HEAD_WIDTH:] += dv
                ct[:, rows] += cs
            else:
                seen.add(ch)
                acc[rows, :HEAD_WIDTH] = dk
                acc[rows, HEAD_WIDTH:] = dv
                ct[:, rows] = cs
        slot = (y - ys + 4) % 4
        dqs = dqt[ys] * fs
        for h in range(GROUP):
            cols = slice(h * BLOCK, (h + 1) * BLOCK)
            dqb[slot, :, cols] = dqs[:, cols].T.astype(BF16)
    for k in range(4):
        dq_outs[k][...] = dqb[k]
    hg = jnp.dot(on_both(ct[...]), kv[:, HEAD_WIDTH:], preferred_element_type=F32)
    hg = hg[:8] + hg[8:]
    row8 = lax.broadcasted_iota(jnp.int32, (8, BLOCK), 0)
    hg = jnp.where(row8 == GROUP, loss, hg)
    high, low = halves(hg)
    tail = jnp.concatenate([high, low], axis=1).astype(BF16)
    for cc in range(2):
        cs = (c + cc) % 2
        ref = dkv_outs[cc]
        ref[128] = tail

        def place(zl_to, carry, ref=ref, cs=cs):
            for kx in range(4):
                xs = (x - kx + 4) % 4
                for ys in range(4):
                    for zh_to in range(2):
                        row = (ys * 4 + zh_to * 2 + cs) * BLOCK + (zl_to * 4 + xs) * 8
                        piece = acc[pl.ds(pl.multiple_of(row, 8), 8), :]
                        ref[kx * 32 + zl_to * 8 + ys * 2 + zh_to] = piece.astype(BF16)
            return carry

        lax.fori_loop(0, 4, place, 0)


def core_kernel(own, far, b0, b1, b2, b3, hg):
    outs = (b0, b1, b2, b3)

    def add(z, carry):
        for kx in range(4):
            at = pl.ds(kx * 32 + z * 8, 8)
            outs[kx][pl.ds(z * 8, 8)] = (own[at].astype(F32) + far[at].astype(F32)).astype(BF16)
        return carry

    lax.fori_loop(0, 4, add, 0)
    a, b = own[128].astype(F32), far[128].astype(F32)
    hg[...] = (a[:, :BLOCK] + a[:, BLOCK:]) + (b[:, :BLOCK] + b[:, BLOCK:])


def x_kernel(b0, b1, b2, b3, hg, out):
    high, low = halves(hg[...])
    tail = jnp.concatenate([high[:4], low[:4]], axis=0).astype(BF16)
    tail = jnp.broadcast_to(tail[None], (8, 8, BLOCK))

    def add(z, carry):
        at = pl.ds(z * 8, 8)
        v = b0[at].astype(F32) + b1[at].astype(F32) + b2[at].astype(F32) + b3[at].astype(F32)
        out[z, :, :, :256] = v.astype(BF16)
        out[z, :, :, 256:] = tail
        return carry

    lax.fori_loop(0, 4, add, 0)


def finish_kernel(did, pieces, d0, d1, d2, d3, qg, gk, gv, hg, loss):
    zl, x, y, zh, c = coords(did)
    for g in range(4):
        v = jnp.zeros((8, 256), F32)
        for z in range(4):
            for k in range(2):
                v = v + pieces[z, g * 2 + k, :, :256].astype(F32)
        gk[:, g * HEAD_WIDTH : (g + 1) * HEAD_WIDTH] = v[:, :HEAD_WIDTH]
        gv[:, g * HEAD_WIDTH : (g + 1) * HEAD_WIDTH] = v[:, HEAD_WIDTH:]
        v = pieces[zl, g * 2, :, 256:].astype(F32)
        t = pieces[zl, g * 2 + 1, :, 256:].astype(F32)
        v = (v[:4] + v[4:]) + (t[:4] + t[4:])
        for h in range(GROUP):
            cols = slice(g * WIDE + h * HEAD_WIDTH, g * WIDE + (h + 1) * HEAD_WIDTH)
            hg[0:1, cols] = v[h : h + 1]
            hg[1:2, cols] = -v[h : h + 1]
        if g == 0:
            loss[0] = jnp.sum(v[GROUP : GROUP + 1]) * (1.0 / TOKENS)
    for k, d in enumerate((d0, d1, d2, d3)):
        wide = pl.ds(pl.multiple_of(((y + k) % 4) * WIDE, HEAD_WIDTH), WIDE)
        qg[:, wide] = d[...].astype(F32)


def shift(v, axis, size, k):
    return lax.ppermute(v, axis, [(i, (i + k) % size) for i in range(size)])


def like(shape, dtype):
    return jax.ShapeDtypeStruct(shape, dtype)


def in_hbm(v):
    return pltpu.with_memory_space_constraint(v, pltpu.HBM)


def call(kernel, name, out_shape, specs, out_specs=None, scratch=()):
    return pl.pallas_call(
        kernel,
        out_shape=out_shape,
        in_specs=specs,
        out_specs=out_specs or [VMEM] * len(out_shape),
        scratch_shapes=list(scratch),
        compiler_params=pltpu.CompilerParams(vmem_limit_bytes=20 << 20),
        name=name,
    )


def per_device(queries, keys, values, head, segments, label_mask, labels):
    did = lax.axis_index(("zl", "x", "y", "zh", "c")).astype(jnp.int32).reshape(1)
    copies, *packs, w, seg = call(
        prep_kernel,
        "prep",
        [like((4, 4, 2, 8, 256), BF16)]
        + [like((BLOCK + 16, WIDE), BF16)] * 4
        + [like((2, 4 * WIDE), F32), like((1, TOKENS), jnp.int32)],
        [SMEM] + [HBM] * 7,
        scratch=[
            pltpu.VMEM((8, 512), BF16),
            pltpu.VMEM((8, 512), BF16),
            pltpu.VMEM((1, BLOCK), jnp.int32),
            pltpu.VMEM((1, BLOCK), jnp.int32),
            pltpu.SemaphoreType.DMA((10,)),
        ],
    )(
        did,
        in_hbm(keys),
        in_hbm(values),
        in_hbm(labels.reshape(1, BLOCK)),
        in_hbm(label_mask.reshape(1, BLOCK)),
        in_hbm(queries[0]),
        in_hbm(head[0].T),
        in_hbm(segments.reshape(1, TOKENS)),
    )
    own = lax.all_to_all(copies.reshape(32, 8, 256), YZ_AXES, 0, 0, tiled=True).reshape(4, 4, 2, 8, 256)
    over_x = [own] + [shift(own, "x", 4, k) for k in range(1, 4)]
    over_c = [shift(a, "c", 2, 1) for a in over_x]
    packs = [packs[0]] + [shift(packs[k], "y", 4, k) for k in range(1, 4)]
    plog, p, inv, delta, qt, kv, kt, u = call(
        forward_kernel,
        "forward",
        [
            like((4, 8, BLOCK), F32),
            like((7 * CHUNK, WIDE), BF16),
            like((4, 8, WIDE), F32),
            like((4, 8, WIDE), F32),
            like((4, HEAD_WIDTH, WIDE), BF16),
            like((TOKENS, 256), BF16),
            like((HEAD_WIDTH, TOKENS), BF16),
            like((TOKENS, BLOCK), F32),
        ],
        [SMEM] + [VMEM] * 14,
        scratch=[
            pltpu.VMEM((TOKENS, 256), F32),
            pltpu.VMEM((HEAD_WIDTH, TOKENS), BF16),
            pltpu.VMEM((3 * CHUNK, WIDE), F32),
            pltpu.VMEM((16, TOKENS), BF16),
        ],
    )(did, seg, w, *packs, *over_x, *over_c)
    logs = [plog] + [shift(plog, "y", 4, k) for k in range(1, 4)]
    g, dqt = call(
        middle_kernel, "middle", [like((7 * CHUNK, WIDE), BF16), like((4, HEAD_WIDTH, WIDE), F32)], [VMEM] * 4
    )(p, delta, u, kt)
    *dq, own_d, far_d = call(
        backward_kernel,
        "backward",
        [like((BLOCK, WIDE), BF16)] * 4 + [like((129, 8, 256), BF16)] * 2,
        [SMEM] + [VMEM] * 15,
        scratch=[
            pltpu.VMEM((4, 4, 8, BLOCK), F32),
            pltpu.VMEM((4, 8, 256), F32),
            pltpu.VMEM((4, BLOCK, WIDE), BF16),
            pltpu.VMEM((TOKENS, 256), F32),
            pltpu.VMEM((8, TOKENS), F32),
        ],
    )(did, w, *logs, *packs, p, g, inv, qt, kv, dqt)
    far = shift(far_d, "c", 2, 1)
    *by_x, hg = call(core_kernel, "core_sum", [like((32, 8, 256), BF16)] * 4 + [like((8, BLOCK), F32)], [VMEM] * 2)(
        own_d, far
    )
    got = [by_x[0]] + [shift(by_x[k], "x", 4, -k) for k in range(1, 4)]
    (by_z,) = call(x_kernel, "x_sum", [like((4, 8, 8, WIDE), BF16)], [VMEM] * 5)(*got, hg)
    pieces = lax.all_to_all(by_z.reshape(32, 8, WIDE), YZ_AXES, 0, 0, tiled=True).reshape(4, 8, 8, WIDE)
    back = [dq[0]] + [shift(dq[k], "y", 4, -k) for k in range(1, 4)]
    query_gradient, grad_keys, grad_values, head_t, loss = call(
        finish_kernel,
        "finish",
        [
            like((BLOCK, 4 * WIDE), F32),
            like((8, 512), F32),
            like((8, 512), F32),
            like((2, 4 * WIDE), F32),
            like((1,), F32),
        ],
        [SMEM] + [VMEM] * 5,
        [VMEM] * 4 + [SMEM],
    )(did, pieces, *back)
    return loss, query_gradient[None], grad_keys, grad_values, head_t.T[None]


def solution(mesh):
    fine = Mesh(mesh.devices.reshape(4, 4, 4, 2, 2), ("zl", "x", "y", "zh", "c"))
    layer, ctx = ("zl", "x"), ("y", "zh", "c")
    return jax.shard_map(
        per_device,
        mesh=fine,
        in_specs=(
            P(layer, ctx, None),
            P(ctx + layer, None),
            P(ctx + layer, None),
            P(layer, None, None),
            P(),
            P(ctx),
            P(ctx),
        ),
        out_specs=(
            P(layer),
            P(layer, ctx, None),
            P(ctx + layer, None),
            P(ctx + layer, None),
            P(layer, None, None),
        ),
        check_vma=False,
    )
```

```python
import jax
import jax.numpy as jnp
from jax import lax
from jax.experimental import pallas as pl
from jax.experimental.pallas import tpu as pltpu
from jax.sharding import Mesh, PartitionSpec as P

HEAD_WIDTH = 128
GROUP = 3
WIDE = GROUP * HEAD_WIDTH
BLOCK = 128
CHUNK = 512
TOKENS = 2048
SCALE = HEAD_WIDTH ** -0.5
LOG2E = 1.4426950408889634
NEG = -1.0e30
F32 = jnp.float32
BF16 = jnp.bfloat16
CHUNKS = ((0,), (0, 1), (0, 1, 2), (3,))
P_AT = (0, 1, 3, 6)
YZ_AXES = ("zl", "y", "zh")


VMEM = pl.BlockSpec(memory_space=pltpu.VMEM)
HBM = pl.BlockSpec(memory_space=pltpu.HBM)
SMEM = pl.BlockSpec(memory_space=pltpu.SMEM)


def coords(did_ref):
    d = did_ref[0]
    return d // 64, (d // 16) % 4, (d // 4) % 4, (d // 2) % 2, d % 2


def prep_kernel(did, keys, values, labels, mask, queries, w, seg, kv_out, q0, q1, q2, q3, w_out, seg_out, kb, vb, lb, mb, sems):
    _, _, y, _, _ = coords(did)
    outs = (q0, q1, q2, q3)
    early = [
        pltpu.make_async_copy(keys, kb, sems.at[0]),
        pltpu.make_async_copy(values, vb, sems.at[1]),
        pltpu.make_async_copy(labels, lb, sems.at[2]),
        pltpu.make_async_copy(mask, mb, sems.at[3]),
    ]
    late = [pltpu.make_async_copy(w, w_out, sems.at[4]), pltpu.make_async_copy(seg, seg_out, sems.at[5])]
    for k in range(4):
        g = pl.multiple_of(((y + k) % 4) * WIDE, HEAD_WIDTH)
        late.append(pltpu.make_async_copy(queries.at[:, pl.ds(g, WIDE)], outs[k].at[pl.ds(0, BLOCK)], sems.at[6 + k]))
    for copy in early + late:
        copy.start()
    for copy in early:
        copy.wait()
    for g in range(4):
        cols = slice(g * HEAD_WIDTH, (g + 1) * HEAD_WIDTH)
        both = jnp.concatenate([kb[:, cols], vb[:, cols]], axis=1)
        for zl_to in range(4):
            for zh_to in range(2):
                kv_out[zl_to, g, zh_to] = both
    lab = jnp.broadcast_to(lb[...].astype(F32), (16, BLOCK))
    msk = jnp.broadcast_to(mb[...].astype(F32), (16, BLOCK))
    tail = jnp.concatenate([lab, msk, lab], axis=1).astype(BF16)
    for k in range(4):
        outs[k][BLOCK:, :] = tail
    for copy in late:
        copy.wait()


def head_diff(w, y, h):
    at = pl.multiple_of(y * WIDE + h * HEAD_WIDTH, HEAD_WIDTH)
    return w[0:1, pl.ds(at, HEAD_WIDTH)] - w[1:2, pl.ds(at, HEAD_WIDTH)]


def halves(v):
    high = v.astype(BF16).astype(F32)
    return high, v - high


def stack8(rows):
    at = lax.broadcasted_iota(jnp.int32, (8, rows[0].shape[1]), 0)
    out = jnp.zeros((8, rows[0].shape[1]), F32)
    for r, row in enumerate(rows):
        out = jnp.where(at == r, row, out)
    return out


def on_both(v):
    high, low = halves(v)
    return jnp.concatenate([high, low], axis=0).astype(BF16)


def forward_kernel(did, seg, w, q0, q1, q2, q3, *rest):
    kvs = rest[:8]
    plog, p_out, inv_out, delta_out, qt, kv_out, kt_out, u_out = rest[8:16]
    kvf, _, s_buf, u_rows = rest[16:]
    _, x, y, zh, c = coords(did)
    for k, ref in enumerate((q0, q1, q2, q3)):
        slot = (y - k + 4) % 4
        for h in range(GROUP):
            one = ref[:BLOCK, h * HEAD_WIDTH : (h + 1) * HEAD_WIDTH]
            qt[slot, :, h * BLOCK : (h + 1) * BLOCK] = one.astype(F32).T.astype(BF16)
    for cc in range(2):
        cs = (c + cc) % 2
        for kx in range(4):
            ref = kvs[cc * 4 + kx]
            xs = (x - kx + 4) % 4

            def place(zl_from, carry, ref=ref, cs=cs, xs=xs):
                for ys in range(4):
                    for zh_from in range(2):
                        row = (ys * 4 + zh_from * 2 + cs) * BLOCK + (zl_from * 4 + xs) * 8
                        kvf[pl.ds(pl.multiple_of(row, 8), 8), :] = ref[zl_from, ys, zh_from].astype(F32)
                return carry

            lax.fori_loop(0, 4, place, 0)
    diffs = stack8([head_diff(w, y, h) for h in range(GROUP)])
    diffs16 = on_both(diffs)
    ones = stack8([jnp.zeros((1, BLOCK), F32)] * GROUP + [jnp.ones((1, BLOCK), F32)])

    def turn(b, carry):
        at = pl.multiple_of(b * BLOCK, BLOCK)
        both = kvf[pl.ds(at, BLOCK), :]
        kv_out[pl.ds(at, BLOCK), :] = both.astype(BF16)
        kt_out[:, pl.ds(at, BLOCK)] = both[:, :HEAD_WIDTH].T.astype(BF16)
        part = jnp.dot(diffs16, both[:, HEAD_WIDTH:].T.astype(BF16), preferred_element_type=F32)
        u = part[:8] + part[8:]
        high, low = halves(u)
        u_rows[:, pl.ds(at, BLOCK)] = jnp.concatenate([high + ones, low], axis=0).astype(BF16)
        wide = jnp.concatenate([u, jnp.zeros((BLOCK - 8, BLOCK), F32)], axis=0)
        u_out[pl.ds(at, BLOCK), :] = wide.T
        return carry

    lax.fori_loop(0, TOKENS // BLOCK, turn, 0)
    j = zh * 2 + c
    key_at = lax.broadcasted_iota(jnp.int32, (BLOCK, BLOCK), 0)
    query_at = lax.broadcasted_iota(jnp.int32, (BLOCK, BLOCK), 1) + j * BLOCK
    for ys in range(4):
        qs = seg[:, pl.ds(pl.multiple_of(ys * CHUNK + j * BLOCK, BLOCK), BLOCK)]
        top = jnp.full((1, WIDE), NEG, F32)
        for i, ch in enumerate(CHUNKS[ys]):
            for b in range(CHUNK // BLOCK):
                row = ch * CHUNK + b * BLOCK
                s = jnp.dot(kv_out[row : row + BLOCK, :HEAD_WIDTH], qt[ys], preferred_element_type=F32)
                if ch == ys:
                    ks = jnp.broadcast_to(seg[:, row : row + BLOCK], (BLOCK, BLOCK)).T
                    ok = (key_at + b * BLOCK <= query_at) & (ks == qs)
                    s = jnp.where(jnp.concatenate([ok] * GROUP, axis=1), s, NEG)
                top = jnp.maximum(top, jnp.max(s, axis=0, keepdims=True))
                at = i * CHUNK + b * BLOCK
                s_buf[at : at + BLOCK, :] = s
        sums = jnp.zeros((16, WIDE), F32)
        for i, ch in enumerate(CHUNKS[ys]):
            at_p = (P_AT[ys] + i) * CHUNK
            for b in range(CHUNK // BLOCK):
                at = i * CHUNK + b * BLOCK
                p = jnp.exp2((s_buf[at : at + BLOCK, :] - top) * (SCALE * LOG2E))
                p_out[at_p + b * BLOCK : at_p + (b + 1) * BLOCK, :] = p.astype(BF16)
            sums = sums + jnp.dot(
                u_rows[:, ch * CHUNK : (ch + 1) * CHUNK], p_out[at_p : at_p + CHUNK, :], preferred_element_type=F32
            )
        inv = 1.0 / sums[GROUP : GROUP + 1, :]
        both = (sums[:8] + sums[8:]) * inv
        delta = jnp.concatenate([both[h : h + 1, h * BLOCK : (h + 1) * BLOCK] for h in range(GROUP)], axis=1)
        inv_out[ys] = jnp.broadcast_to(inv, (8, WIDE))
        delta_out[ys] = jnp.broadcast_to(delta, (8, WIDE))
        lg = delta[:, :BLOCK] + delta[:, BLOCK : 2 * BLOCK] + delta[:, 2 * BLOCK :]
        plog[(y - ys + 4) % 4] = jnp.broadcast_to(lg, (8, BLOCK))


def middle_kernel(p, delta, u, kt, g_out, dq_out):
    for ys in range(4):
        dqt = jnp.zeros((HEAD_WIDTH, WIDE), F32)
        for i, ch in enumerate(CHUNKS[ys]):
            at_p = (P_AT[ys] + i) * CHUNK
            for b in range(CHUNK // BLOCK):
                row = ch * CHUNK + b * BLOCK
                at = slice(at_p + b * BLOCK, at_p + (b + 1) * BLOCK)
                ub = jnp.concatenate(
                    [jnp.broadcast_to(u[row : row + BLOCK, h : h + 1], (BLOCK, BLOCK)) for h in range(GROUP)], axis=1
                )
                g_out[at, :] = (p[at, :].astype(F32) * (ub - delta[ys, 0:1, :])).astype(BF16)
            dqt = dqt + jnp.dot(
                kt[:, ch * CHUNK : (ch + 1) * CHUNK], g_out[at_p : at_p + CHUNK, :], preferred_element_type=F32
            )
        dq_out[ys] = dqt


NT = (((1,), (1,)), ((), ()))


def backward_kernel(did, w, l0, l1, l2, l3, g0, g1, g2, g3, p, g, inv, qt, kv, dqt, *rest):
    dq_outs = rest[:4]
    dkv_outs = rest[4:6]
    lgs, labs, dqb, acc, ct = rest[6:]
    _, x, y, _, c = coords(did)
    for k, ref in enumerate((l0, l1, l2, l3)):
        src = (y - k + 4) % 4
        for m in range(4):
            ys = (y - m + 4) % 4
            lgs[src, ys] = ref[(m - k) % 4]
    for k, ref in enumerate((g0, g1, g2, g3)):
        labs[(y - k + 4) % 4] = ref[BLOCK:, :256].astype(F32)[8:16, :]
    diffs = [head_diff(w, y, h) for h in range(GROUP)]
    wt = jnp.concatenate([jnp.broadcast_to(d, (BLOCK, HEAD_WIDTH)).T for d in diffs], axis=1)
    head_of = lax.broadcasted_iota(jnp.int32, (8, WIDE), 1) // BLOCK
    head_at = lax.broadcasted_iota(jnp.int32, (8, WIDE), 0)
    loss = jnp.zeros((1, BLOCK), F32)
    seen = set()
    for ys in range(4):
        z = (lgs[0, ys] + lgs[1, ys] + lgs[2, ys] + lgs[3, ys])[0:1, :]
        one = labs[ys, 0:1, :BLOCK] > 0.5
        mask = labs[ys, 0:1, BLOCK:]
        a = jnp.where(one, z, -z)
        e = jnp.exp(-jnp.abs(a))
        loss = loss + mask * (jnp.maximum(a, 0.0) + jnp.log(1.0 + e))
        sig = jnp.where(a >= 0.0, 1.0, e) / (1.0 + e)
        d0 = mask * jnp.where(one, sig, -sig)
        f = jnp.concatenate([d0] * GROUP, axis=1) * inv[ys, 0:1, :]
        fs = f * SCALE
        at16 = (wt * f).astype(BF16)
        qf = (qt[ys].astype(F32) * fs).astype(BF16)
        fm = on_both(jnp.where(head_of == head_at, f, 0.0))
        for i, ch in enumerate(CHUNKS[ys]):
            at = slice((P_AT[ys] + i) * CHUNK, (P_AT[ys] + i + 1) * CHUNK)
            rows = slice(ch * CHUNK, (ch + 1) * CHUNK)
            dk = lax.dot_general(g[at, :], qf, NT, preferred_element_type=F32)
            dv = lax.dot_general(p[at, :], at16, NT, preferred_element_type=F32)
            cs = lax.dot_general(fm, p[at, :], NT, preferred_element_type=F32)
            cs = cs[:8] + cs[8:]
            if ch in seen:
                acc[rows, :HEAD_WIDTH] += dk
                acc[rows, HEAD_WIDTH:] += dv
                ct[:, rows] += cs
            else:
                seen.add(ch)
                acc[rows, :HEAD_WIDTH] = dk
                acc[rows, HEAD_WIDTH:] = dv
                ct[:, rows] = cs
        slot = (y - ys + 4) % 4
        dqs = dqt[ys] * fs
        for h in range(GROUP):
            cols = slice(h * BLOCK, (h + 1) * BLOCK)
            dqb[slot, :, cols] = dqs[:, cols].T.astype(BF16)
    for k in range(4):
        dq_outs[k][...] = dqb[k]
    hg = jnp.dot(on_both(ct[...]), kv[:, HEAD_WIDTH:], preferred_element_type=F32)
    hg = hg[:8] + hg[8:]
    row8 = lax.broadcasted_iota(jnp.int32, (8, BLOCK), 0)
    hg = jnp.where(row8 == GROUP, loss, hg)
    high, low = halves(hg)
    tail = jnp.concatenate([high, low], axis=1).astype(BF16)
    for cc in range(2):
        cs = (c + cc) % 2
        ref = dkv_outs[cc]
        ref[128] = tail

        def place(zl_to, carry, ref=ref, cs=cs):
            for kx in range(4):
                xs = (x - kx + 4) % 4
                for ys in range(4):
                    for zh_to in range(2):
                        row = (ys * 4 + zh_to * 2 + cs) * BLOCK + (zl_to * 4 + xs) * 8
                        piece = acc[pl.ds(pl.multiple_of(row, 8), 8), :]
                        ref[kx * 32 + zl_to * 8 + ys * 2 + zh_to] = piece.astype(BF16)
            return carry

        lax.fori_loop(0, 4, place, 0)


def core_kernel(own, far, b0, b1, b2, b3, hg):
    outs = (b0, b1, b2, b3)

    def add(z, carry):
        for kx in range(4):
            at = pl.ds(kx * 32 + z * 8, 8)
            outs[kx][pl.ds(z * 8, 8)] = (own[at].astype(F32) + far[at].astype(F32)).astype(BF16)
        return carry

    lax.fori_loop(0, 4, add, 0)
    a, b = own[128].astype(F32), far[128].astype(F32)
    hg[...] = (a[:, :BLOCK] + a[:, BLOCK:]) + (b[:, :BLOCK] + b[:, BLOCK:])


def x_kernel(b0, b1, b2, b3, hg, out):
    high, low = halves(hg[...])
    tail = jnp.concatenate([high[:4], low[:4]], axis=0).astype(BF16)
    tail = jnp.broadcast_to(tail[None], (8, 8, BLOCK))

    def add(z, carry):
        at = pl.ds(z * 8, 8)
        v = b0[at].astype(F32) + b1[at].astype(F32) + b2[at].astype(F32) + b3[at].astype(F32)
        out[z, :, :, :256] = v.astype(BF16)
        out[z, :, :, 256:] = tail
        return carry

    lax.fori_loop(0, 4, add, 0)


def finish_kernel(did, pieces, d0, d1, d2, d3, qg, gk, gv, hg, loss):
    zl, _, y, _, _ = coords(did)
    for g in range(4):
        v = jnp.zeros((8, 256), F32)
        for z in range(4):
            for k in range(2):
                v = v + pieces[z, g * 2 + k, :, :256].astype(F32)
        gk[:, g * HEAD_WIDTH : (g + 1) * HEAD_WIDTH] = v[:, :HEAD_WIDTH]
        gv[:, g * HEAD_WIDTH : (g + 1) * HEAD_WIDTH] = v[:, HEAD_WIDTH:]
        v = pieces[zl, g * 2, :, 256:].astype(F32)
        t = pieces[zl, g * 2 + 1, :, 256:].astype(F32)
        v = (v[:4] + v[4:]) + (t[:4] + t[4:])
        for h in range(GROUP):
            cols = slice(g * WIDE + h * HEAD_WIDTH, g * WIDE + (h + 1) * HEAD_WIDTH)
            hg[0:1, cols] = v[h : h + 1]
            hg[1:2, cols] = -v[h : h + 1]
        if g == 0:
            loss[0] = jnp.sum(v[GROUP : GROUP + 1]) * (1.0 / TOKENS)
    for k, d in enumerate((d0, d1, d2, d3)):
        wide = pl.ds(pl.multiple_of(((y + k) % 4) * WIDE, HEAD_WIDTH), WIDE)
        qg[:, wide] = d[...].astype(F32)


def shift(v, axis, size, k):
    return lax.ppermute(v, axis, [(i, (i + k) % size) for i in range(size)])


def like(shape, dtype):
    return jax.ShapeDtypeStruct(shape, dtype)


def in_hbm(v):
    return pltpu.with_memory_space_constraint(v, pltpu.HBM)


def call(kernel, out_shape, specs, out_specs=None, scratch=()):
    return pl.pallas_call(
        kernel,
        out_shape=out_shape,
        in_specs=specs,
        out_specs=out_specs or [VMEM] * len(out_shape),
        scratch_shapes=list(scratch),
        compiler_params=pltpu.CompilerParams(vmem_limit_bytes=20 << 20),
    )


def per_device(queries, keys, values, head, segments, label_mask, labels):
    did = lax.axis_index(("zl", "x", "y", "zh", "c")).astype(jnp.int32).reshape(1)
    copies, *packs, w, seg = call(
        prep_kernel,
        [like((4, 4, 2, 8, 256), BF16)]
        + [like((BLOCK + 16, WIDE), BF16)] * 4
        + [like((2, 4 * WIDE), F32), like((1, TOKENS), jnp.int32)],
        [SMEM] + [HBM] * 7,
        scratch=[
            pltpu.VMEM((8, 512), BF16),
            pltpu.VMEM((8, 512), BF16),
            pltpu.VMEM((1, BLOCK), jnp.int32),
            pltpu.VMEM((1, BLOCK), jnp.int32),
            pltpu.SemaphoreType.DMA((10,)),
        ],
    )(
        did,
        in_hbm(keys),
        in_hbm(values),
        in_hbm(labels.reshape(1, BLOCK)),
        in_hbm(label_mask.reshape(1, BLOCK)),
        in_hbm(queries[0]),
        in_hbm(head[0].T),
        in_hbm(segments.reshape(1, TOKENS)),
    )
    own = lax.all_to_all(copies.reshape(32, 8, 256), YZ_AXES, 0, 0, tiled=True).reshape(4, 4, 2, 8, 256)
    over_x = [own]
    for k in range(1, 4):
        over_x.append(shift(own, "x", 4, k))
    over_c = [shift(a, "c", 2, 1) for a in over_x]
    for k in range(1, 4):
        packs[k] = shift(packs[k], "y", 4, k)
    plog, p, inv, delta, qt, kv, kt, u = call(
        forward_kernel,
        [
            like((4, 8, BLOCK), F32),
            like((7 * CHUNK, WIDE), BF16),
            like((4, 8, WIDE), F32),
            like((4, 8, WIDE), F32),
            like((4, HEAD_WIDTH, WIDE), BF16),
            like((TOKENS, 256), BF16),
            like((HEAD_WIDTH, TOKENS), BF16),
            like((TOKENS, BLOCK), F32),
        ],
        [SMEM] + [VMEM] * 14,
        scratch=[
            pltpu.VMEM((TOKENS, 256), F32),
            pltpu.VMEM((HEAD_WIDTH, TOKENS), BF16),
            pltpu.VMEM((3 * CHUNK, WIDE), F32),
            pltpu.VMEM((16, TOKENS), BF16),
        ],
    )(did, seg, w, *packs, *over_x, *over_c)
    logs = [plog] + [shift(plog, "y", 4, k) for k in range(1, 4)]
    g, dqt = call(
        middle_kernel, [like((7 * CHUNK, WIDE), BF16), like((4, HEAD_WIDTH, WIDE), F32)], [VMEM] * 4
    )(p, delta, u, kt)
    *dq, own_d, far_d = call(
        backward_kernel,
        [like((BLOCK, WIDE), BF16)] * 4 + [like((129, 8, 256), BF16)] * 2,
        [SMEM] + [VMEM] * 15,
        scratch=[
            pltpu.VMEM((4, 4, 8, BLOCK), F32),
            pltpu.VMEM((4, 8, 256), F32),
            pltpu.VMEM((4, BLOCK, WIDE), BF16),
            pltpu.VMEM((TOKENS, 256), F32),
            pltpu.VMEM((8, TOKENS), F32),
        ],
    )(did, w, *logs, *packs, p, g, inv, qt, kv, dqt)
    far = shift(far_d, "c", 2, 1)
    *by_x, hg = call(core_kernel, [like((32, 8, 256), BF16)] * 4 + [like((8, BLOCK), F32)], [VMEM] * 2)(own_d, far)
    got = [by_x[0]] + [shift(by_x[k], "x", 4, -k) for k in range(1, 4)]
    (by_z,) = call(x_kernel, [like((4, 8, 8, WIDE), BF16)], [VMEM] * 5)(*got, hg)
    pieces = lax.all_to_all(by_z.reshape(32, 8, WIDE), YZ_AXES, 0, 0, tiled=True).reshape(4, 8, 8, WIDE)
    back = [dq[0]]
    for k in range(1, 4):
        back.append(shift(dq[k], "y", 4, -k))
    query_gradient, grad_keys, grad_values, head_t, loss = call(
        finish_kernel,
        [
            like((BLOCK, 4 * WIDE), F32),
            like((8, 512), F32),
            like((8, 512), F32),
            like((2, 4 * WIDE), F32),
            like((1,), F32),
        ],
        [SMEM] + [VMEM] * 5,
        [VMEM] * 4 + [SMEM],
    )(did, pieces, *back)
    return loss, query_gradient[None], grad_keys, grad_values, head_t.T[None]


def solution(mesh):
    fine = Mesh(mesh.devices.reshape(4, 4, 4, 2, 2), ("zl", "x", "y", "zh", "c"))
    layer, ctx = ("zl", "x"), ("y", "zh", "c")
    return jax.shard_map(
        per_device,
        mesh=fine,
        in_specs=(
            P(layer, ctx, None),
            P(ctx + layer, None),
            P(ctx + layer, None),
            P(layer, None, None),
            P(),
            P(ctx),
            P(ctx),
        ),
        out_specs=(
            P(layer),
            P(layer, ctx, None),
            P(ctx + layer, None),
            P(ctx + layer, None),
            P(layer, None, None),
        ),
        check_vma=False,
    )
```

```python
import jax
import jax.numpy as jnp
from jax import lax
from jax.experimental import pallas as pl
from jax.experimental.pallas import tpu as pltpu
from jax.sharding import Mesh, PartitionSpec as P

HEAD_WIDTH = 128
GROUP = 3
WIDE = GROUP * HEAD_WIDTH
BLOCK = 128
CHUNK = 512
TOKENS = 2048
SCALE = HEAD_WIDTH ** -0.5
LOG2E = 1.4426950408889634
NEG = -1.0e30
F32 = jnp.float32
BF16 = jnp.bfloat16
CHUNKS = ((0,), (0, 1), (0, 1, 2), (3,))
P_AT = (0, 1, 3, 6)
YZ_AXES = ("y", "zh", "zl")


VMEM = pl.BlockSpec(memory_space=pltpu.VMEM)
HBM = pl.BlockSpec(memory_space=pltpu.HBM)
SMEM = pl.BlockSpec(memory_space=pltpu.SMEM)


def coords(did_ref):
    d = did_ref[0]
    return d // 64, (d // 16) % 4, (d // 4) % 4, (d // 2) % 2, d % 2


def keys_kernel(keys, values, kv_out, kb, vb, sems):
    copies = [pltpu.make_async_copy(keys, kb, sems.at[0]), pltpu.make_async_copy(values, vb, sems.at[1])]
    for copy in copies:
        copy.start()
    for copy in copies:
        copy.wait()
    for g in range(4):
        cols = slice(g * HEAD_WIDTH, (g + 1) * HEAD_WIDTH)
        both = jnp.concatenate([kb[:, cols], vb[:, cols]], axis=1)
        for z in range(8):
            kv_out[g, z] = both


def queries_kernel(did, labels, mask, queries, w, seg, q0, q1, q2, q3, w_out, seg_out, lb, mb, sems):
    _, _, y, _, _ = coords(did)
    outs = (q0, q1, q2, q3)
    early = [pltpu.make_async_copy(labels, lb, sems.at[0]), pltpu.make_async_copy(mask, mb, sems.at[1])]
    late = [pltpu.make_async_copy(w, w_out, sems.at[2]), pltpu.make_async_copy(seg, seg_out, sems.at[3])]
    for k in range(4):
        g = pl.multiple_of(((y + k) % 4) * WIDE, HEAD_WIDTH)
        late.append(pltpu.make_async_copy(queries.at[:, pl.ds(g, WIDE)], outs[k].at[pl.ds(0, BLOCK)], sems.at[4 + k]))
    for copy in early + late:
        copy.start()
    for copy in early:
        copy.wait()
    lab = jnp.broadcast_to(lb[...].astype(F32), (16, BLOCK))
    msk = jnp.broadcast_to(mb[...].astype(F32), (16, BLOCK))
    tail = jnp.concatenate([lab, msk, lab], axis=1).astype(BF16)
    for k in range(4):
        outs[k][BLOCK:, :] = tail
    for copy in late:
        copy.wait()


def head_diff(w, y, h):
    at = pl.multiple_of(y * WIDE + h * HEAD_WIDTH, HEAD_WIDTH)
    return w[0:1, pl.ds(at, HEAD_WIDTH)] - w[1:2, pl.ds(at, HEAD_WIDTH)]


def halves(v):
    high = v.astype(BF16).astype(F32)
    return high, v - high


def stack8(rows):
    at = lax.broadcasted_iota(jnp.int32, (8, rows[0].shape[1]), 0)
    out = jnp.zeros((8, rows[0].shape[1]), F32)
    for r, row in enumerate(rows):
        out = jnp.where(at == r, row, out)
    return out


def on_both(v):
    high, low = halves(v)
    return jnp.concatenate([high, low], axis=0).astype(BF16)


NT = (((1,), (1,)), ((), ()))


def times_t(a, b):
    return lax.dot_general(a, b, NT, preferred_element_type=F32)


def forward_kernel(did, seg, w, q0, q1, q2, q3, *rest):
    kvs = rest[:8]
    plog, p_out, inv_out, delta_out, q_out, kv_out = rest[8:14]
    s_buf, u_rows = rest[14:]
    _, x, y, zh, c = coords(did)
    for cc in range(2):
        for kx in range(4):
            for ys in range(4):
                for z in range(2):
                    row = ys * CHUNK + cc * 256 + z * BLOCK + kx * 32
                    kv_out[row : row + 32, :] = kvs[cc * 4 + kx][ys, z]
    for k, ref in enumerate((q0, q1, q2, q3)):
        slot = (y - k + 4) % 4
        for h in range(GROUP):
            q_out[slot, h * BLOCK : (h + 1) * BLOCK, :] = ref[:BLOCK, h * HEAD_WIDTH : (h + 1) * HEAD_WIDTH]
    diffs16 = on_both(stack8([head_diff(w, y, h) for h in range(GROUP)]))
    ones = stack8([jnp.zeros((1, CHUNK), F32)] * GROUP + [jnp.ones((1, CHUNK), F32)])
    for ch in range(4):
        rows = slice(ch * CHUNK, (ch + 1) * CHUNK)
        part = times_t(diffs16, kv_out[rows, HEAD_WIDTH:])
        high, low = halves(part[:8] + part[8:])
        u_rows[:, rows] = jnp.concatenate([high + ones, low], axis=0).astype(BF16)
    j = zh * 2 + c
    r = lax.broadcasted_iota(jnp.int32, (BLOCK, BLOCK), 0)
    from_x = jnp.bitwise_and(x + 4 - jnp.right_shift(r, 5), 3)
    inner = jnp.bitwise_and(jnp.right_shift(r, 3), 3) * 32 + from_x * 8 + jnp.bitwise_and(r, 7)
    query_at = lax.broadcasted_iota(jnp.int32, (BLOCK, BLOCK), 1) + j * BLOCK
    last = seg[:, pl.ds(pl.multiple_of(3 * CHUNK + j * BLOCK, BLOCK), BLOCK)]
    start = jnp.zeros((1, BLOCK), F32)
    for b in range(4):
        row = 3 * CHUNK + b * BLOCK
        ids = jnp.broadcast_to(seg[:, row : row + BLOCK], (BLOCK, BLOCK)).T
        start = start + jnp.sum(jnp.where(ids < last, 1.0, 0.0), axis=0, keepdims=True)
    start = start.astype(jnp.int32)
    for ys in range(4):
        top = jnp.full((1, WIDE), NEG, F32)
        for i, ch in enumerate(CHUNKS[ys]):
            for b in range(CHUNK // BLOCK):
                row = ch * CHUNK + b * BLOCK
                s = times_t(kv_out[row : row + BLOCK, :HEAD_WIDTH], q_out[ys])
                if ch == ys:
                    key_at = inner + ((b % 2) * 256 + ((c + b // 2) % 2) * BLOCK)
                    ok = key_at <= query_at
                    if ys == 3:
                        ok = ok & (key_at >= start)
                    s = jnp.where(jnp.concatenate([ok] * GROUP, axis=1), s, NEG)
                top = jnp.maximum(top, jnp.max(s, axis=0, keepdims=True))
                at = i * CHUNK + b * BLOCK
                s_buf[at : at + BLOCK, :] = s
        sums = jnp.zeros((16, WIDE), F32)
        for i, ch in enumerate(CHUNKS[ys]):
            at_p = (P_AT[ys] + i) * CHUNK
            for b in range(CHUNK // BLOCK):
                at = i * CHUNK + b * BLOCK
                p = jnp.exp2((s_buf[at : at + BLOCK, :] - top) * (SCALE * LOG2E))
                p_out[at_p + b * BLOCK : at_p + (b + 1) * BLOCK, :] = p.astype(BF16)
            sums = sums + jnp.dot(
                u_rows[:, ch * CHUNK : (ch + 1) * CHUNK], p_out[at_p : at_p + CHUNK, :], preferred_element_type=F32
            )
        inv = 1.0 / sums[GROUP : GROUP + 1, :]
        both = (sums[:8] + sums[8:]) * inv
        delta = jnp.concatenate([both[h : h + 1, h * BLOCK : (h + 1) * BLOCK] for h in range(GROUP)], axis=1)
        inv_out[ys] = jnp.broadcast_to(inv, (8, WIDE))
        delta_out[ys] = jnp.broadcast_to(delta, (8, WIDE))
        lg = delta[:, :BLOCK] + delta[:, BLOCK : 2 * BLOCK] + delta[:, 2 * BLOCK :]
        plog[(y - ys + 4) % 4] = jnp.broadcast_to(lg, (8, BLOCK))


def middle_kernel(did, w, p, delta, q, kv, g_out, dq_out, qt_out, kt, u):
    _, _, y, _, _ = coords(did)
    eye = jnp.where(
        lax.broadcasted_iota(jnp.int32, (BLOCK, BLOCK), 0) == lax.broadcasted_iota(jnp.int32, (BLOCK, BLOCK), 1), 1.0, 0.0
    ).astype(BF16)
    pad = jnp.zeros((BLOCK - 8, HEAD_WIDTH), F32)
    high, low = halves(jnp.concatenate([stack8([head_diff(w, y, h) for h in range(GROUP)]), pad], axis=0))
    high, low = high.astype(BF16), low.astype(BF16)
    for ch in range(4):
        rows = slice(ch * CHUNK, (ch + 1) * CHUNK)
        kt[:, rows] = times_t(eye, kv[rows, :HEAD_WIDTH]).astype(BF16)
        u[rows, :] = times_t(kv[rows, HEAD_WIDTH:], high) + times_t(kv[rows, HEAD_WIDTH:], low)
    for ys in range(4):
        qt_out[ys] = times_t(eye, q[ys]).astype(BF16)
        dqt = jnp.zeros((HEAD_WIDTH, WIDE), F32)
        for i, ch in enumerate(CHUNKS[ys]):
            at_p = (P_AT[ys] + i) * CHUNK
            for b in range(CHUNK // BLOCK):
                row = ch * CHUNK + b * BLOCK
                at = slice(at_p + b * BLOCK, at_p + (b + 1) * BLOCK)
                ub = jnp.concatenate(
                    [jnp.broadcast_to(u[row : row + BLOCK, h : h + 1], (BLOCK, BLOCK)) for h in range(GROUP)], axis=1
                )
                g_out[at, :] = (p[at, :].astype(F32) * (ub - delta[ys, 0:1, :])).astype(BF16)
            dqt = dqt + jnp.dot(
                kt[:, ch * CHUNK : (ch + 1) * CHUNK], g_out[at_p : at_p + CHUNK, :], preferred_element_type=F32
            )
        dq_out[ys] = dqt


def key_terms(out, half, p, g, qf, at16):
    for ch in range(4):
        dk = jnp.zeros((256, HEAD_WIDTH), F32)
        dv = jnp.zeros((256, HEAD_WIDTH), F32)
        for ys in range(4):
            if ch in CHUNKS[ys]:
                at = (P_AT[ys] + CHUNKS[ys].index(ch)) * CHUNK + half * 256
                dk = dk + times_t(g[at : at + 256, :], qf[ys])
                dv = dv + times_t(p[at : at + 256, :], at16[ys])
        both = jnp.concatenate([dk, dv], axis=1).astype(BF16)
        for z in range(2):
            for kx in range(4):
                row = z * BLOCK + kx * 32
                out[kx, ch, z] = both[row : row + 32]


def far_kernel(did, w, l0, l1, l2, l3, g0, g1, g2, g3, p, g, inv, qt, out, f_out, qf, at16, loss_out, lgs, labs):
    _, _, y, _, _ = coords(did)
    for k, ref in enumerate((l0, l1, l2, l3)):
        src = (y - k + 4) % 4
        for m in range(4):
            ys = (y - m + 4) % 4
            lgs[src, ys] = ref[(m - k) % 4]
    for k, ref in enumerate((g0, g1, g2, g3)):
        labs[(y - k + 4) % 4] = ref[BLOCK:, :256].astype(F32)[8:16, :]
    wt = jnp.concatenate([jnp.broadcast_to(head_diff(w, y, h), (BLOCK, HEAD_WIDTH)).T for h in range(GROUP)], axis=1)
    loss = jnp.zeros((1, BLOCK), F32)
    for ys in range(4):
        z = (lgs[0, ys] + lgs[1, ys] + lgs[2, ys] + lgs[3, ys])[0:1, :]
        one = labs[ys, 0:1, :BLOCK] > 0.5
        mask = labs[ys, 0:1, BLOCK:]
        a = jnp.where(one, z, -z)
        e = jnp.exp(-jnp.abs(a))
        loss = loss + mask * (jnp.maximum(a, 0.0) + jnp.log(1.0 + e))
        sig = jnp.where(a >= 0.0, 1.0, e) / (1.0 + e)
        d0 = mask * jnp.where(one, sig, -sig)
        f = jnp.concatenate([d0] * GROUP, axis=1) * inv[ys, 0:1, :]
        f_out[ys] = jnp.broadcast_to(f, (8, WIDE))
        at16[ys] = (wt * f).astype(BF16)
        qf[ys] = (qt[ys].astype(F32) * (f * SCALE)).astype(BF16)
    loss_out[...] = jnp.broadcast_to(loss, (8, BLOCK))
    key_terms(out, 1, p, g, qf, at16)


def own_kernel(did, p, g, qf, at16, f, loss, kv, dqt, out, hg_out, d0, d1, d2, d3, dqb, ct):
    _, _, y, _, _ = coords(did)
    key_terms(out, 0, p, g, qf, at16)
    head_of = lax.broadcasted_iota(jnp.int32, (8, WIDE), 1) // BLOCK
    head_at = lax.broadcasted_iota(jnp.int32, (8, WIDE), 0)
    seen = set()
    for ys in range(4):
        fm = on_both(jnp.where(head_of == head_at, f[ys, 0:1, :], 0.0))
        for i, ch in enumerate(CHUNKS[ys]):
            at = (P_AT[ys] + i) * CHUNK
            rows = slice(ch * CHUNK, (ch + 1) * CHUNK)
            cs = times_t(fm, p[at : at + CHUNK, :])
            cs = cs[:8] + cs[8:]
            ct[:, rows] = ct[:, rows] + cs if ch in seen else cs
            seen.add(ch)
        dqs = dqt[ys] * (f[ys, 0:1, :] * SCALE)
        slot = (y - ys + 4) % 4
        for h in range(GROUP):
            cols = slice(h * BLOCK, (h + 1) * BLOCK)
            dqb[slot, :, cols] = dqs[:, cols].T.astype(BF16)
    for k, ref in enumerate((d0, d1, d2, d3)):
        ref[...] = dqb[k]
    hg = jnp.dot(on_both(ct[...]), kv[:, HEAD_WIDTH:], preferred_element_type=F32)
    row8 = lax.broadcasted_iota(jnp.int32, (8, BLOCK), 0)
    hg_out[...] = jnp.where(row8 == GROUP, loss[...], hg[:8] + hg[8:])


def core_kernel(own, far, b0, b1, b2, b3):
    for kx, out in enumerate((b0, b1, b2, b3)):

        def add(ys, carry, kx=kx, out=out):
            out[ys] = (own[kx, ys].astype(F32) + far[kx, ys].astype(F32)).astype(BF16)
            return carry

        lax.fori_loop(0, 4, add, 0)


def x_kernel(b0, b1, b2, b3, hg, hg_far, out):
    high, low = halves(hg[...] + hg_far[...])
    tail = jnp.concatenate([high[:4], low[:4]], axis=0).astype(BF16)
    tail = jnp.broadcast_to(tail[None, None], (2, 4, 8, BLOCK))

    def add(ys, carry):
        v = b0[ys].astype(F32) + b1[ys].astype(F32) + b2[ys].astype(F32) + b3[ys].astype(F32)
        out[ys, :, :, :, :256] = v.reshape(2, 4, 8, 256).astype(BF16)
        out[ys, :, :, :, 256:] = tail
        return carry

    lax.fori_loop(0, 4, add, 0)


def finish_kernel(did, pieces, d0, d1, d2, d3, qg, gk, gv, hg, loss):
    zl, _, y, _, _ = coords(did)
    for g in range(4):
        v = jnp.zeros((8, 256), F32)
        for k in range(2):
            for z in range(4):
                v = v + pieces[g, k, z, :, :256].astype(F32)
        gk[:, g * HEAD_WIDTH : (g + 1) * HEAD_WIDTH] = v[:, :HEAD_WIDTH]
        gv[:, g * HEAD_WIDTH : (g + 1) * HEAD_WIDTH] = v[:, HEAD_WIDTH:]
        v = pieces[g, 0, zl, :, 256:].astype(F32)
        t = pieces[g, 1, zl, :, 256:].astype(F32)
        v = (v[:4] + v[4:]) + (t[:4] + t[4:])
        for h in range(GROUP):
            cols = slice(g * WIDE + h * HEAD_WIDTH, g * WIDE + (h + 1) * HEAD_WIDTH)
            hg[0:1, cols] = v[h : h + 1]
            hg[1:2, cols] = -v[h : h + 1]
        if g == 0:
            loss[0] = jnp.sum(v[GROUP : GROUP + 1]) * (1.0 / TOKENS)
    for k, d in enumerate((d0, d1, d2, d3)):
        wide = pl.ds(pl.multiple_of(((y + k) % 4) * WIDE, HEAD_WIDTH), WIDE)
        qg[:, wide] = d[...].astype(F32)


def shift(v, axis, size, k):
    return lax.ppermute(v, axis, [(i, (i + k) % size) for i in range(size)])


def like(shape, dtype):
    return jax.ShapeDtypeStruct(shape, dtype)


def in_hbm(v):
    return pltpu.with_memory_space_constraint(v, pltpu.HBM)


def call(kernel, out_shape, specs, out_specs=None, scratch=()):
    return pl.pallas_call(
        kernel,
        out_shape=out_shape,
        in_specs=specs,
        out_specs=out_specs or [VMEM] * len(out_shape),
        scratch_shapes=list(scratch),
        compiler_params=pltpu.CompilerParams(vmem_limit_bytes=20 << 20),
    )


def per_device(queries, keys, values, head, segments, label_mask, labels):
    did = lax.axis_index(("zl", "x", "y", "zh", "c")).astype(jnp.int32).reshape(1)
    (copies,) = call(
        keys_kernel,
        [like((4, 8, 8, 256), BF16)],
        [HBM] * 2,
        scratch=[pltpu.VMEM((8, 512), BF16), pltpu.VMEM((8, 512), BF16), pltpu.SemaphoreType.DMA((2,))],
    )(in_hbm(keys), in_hbm(values))
    own = lax.all_to_all(copies.reshape(32, 8, 256), YZ_AXES, 0, 0, tiled=True).reshape(4, 2, 32, 256)
    *packs, w, seg = call(
        queries_kernel,
        [like((BLOCK + 16, WIDE), BF16)] * 4 + [like((2, 4 * WIDE), F32), like((1, TOKENS), jnp.int32)],
        [SMEM] + [HBM] * 5,
        scratch=[
            pltpu.VMEM((1, BLOCK), jnp.int32),
            pltpu.VMEM((1, BLOCK), jnp.int32),
            pltpu.SemaphoreType.DMA((8,)),
        ],
    )(
        did,
        in_hbm(labels.reshape(1, BLOCK)),
        in_hbm(label_mask.reshape(1, BLOCK)),
        in_hbm(queries[0]),
        in_hbm(head[0].T),
        in_hbm(segments.reshape(1, TOKENS)),
    )
    over_x = [own]
    for k in range(1, 4):
        over_x.append(shift(own, "x", 4, k))
    over_c = [shift(a, "c", 2, 1) for a in over_x]
    for k in range(1, 4):
        packs[k] = shift(packs[k], "y", 4, k)
    plog, p, inv, delta, q, kv = call(
        forward_kernel,
        [
            like((4, 8, BLOCK), F32),
            like((7 * CHUNK, WIDE), BF16),
            like((4, 8, WIDE), F32),
            like((4, 8, WIDE), F32),
            like((4, WIDE, HEAD_WIDTH), BF16),
            like((TOKENS, 256), BF16),
        ],
        [SMEM] + [VMEM] * 14,
        scratch=[pltpu.VMEM((3 * CHUNK, WIDE), F32), pltpu.VMEM((16, TOKENS), BF16)],
    )(did, seg, w, *packs, *over_x, *over_c)
    logs = [plog] + [shift(plog, "y", 4, k) for k in range(1, 4)]
    g, dqt, qt = call(
        middle_kernel,
        [
            like((7 * CHUNK, WIDE), BF16),
            like((4, HEAD_WIDTH, WIDE), F32),
            like((4, HEAD_WIDTH, WIDE), BF16),
        ],
        [SMEM] + [VMEM] * 5,
        scratch=[pltpu.VMEM((HEAD_WIDTH, TOKENS), BF16), pltpu.VMEM((TOKENS, BLOCK), F32)],
    )(did, w, p, delta, q, kv)
    far_d, f, qf, at16, loss_rows = call(
        far_kernel,
        [
            like((4, 4, 2, 32, 256), BF16),
            like((4, 8, WIDE), F32),
            like((4, HEAD_WIDTH, WIDE), BF16),
            like((4, HEAD_WIDTH, WIDE), BF16),
            like((8, BLOCK), F32),
        ],
        [SMEM] + [VMEM] * 13,
        scratch=[pltpu.VMEM((4, 4, 8, BLOCK), F32), pltpu.VMEM((4, 8, 256), F32)],
    )(did, w, *logs, *packs, p, g, inv, qt)
    far = shift(far_d, "c", 2, 1)
    own_d, hg, *dq = call(
        own_kernel,
        [like((4, 4, 2, 32, 256), BF16), like((8, BLOCK), F32)] + [like((BLOCK, WIDE), BF16)] * 4,
        [SMEM] + [VMEM] * 8,
        scratch=[pltpu.VMEM((4, BLOCK, WIDE), BF16), pltpu.VMEM((8, TOKENS), F32)],
    )(did, p, g, qf, at16, f, loss_rows, kv, dqt)
    by_x = call(core_kernel, [like((4, 2, 32, 256), BF16)] * 4, [VMEM] * 2)(own_d, far)
    got = [by_x[0]] + [shift(by_x[k], "x", 4, -k) for k in range(1, 4)]
    hg_far = shift(hg, "c", 2, 1)
    (by_z,) = call(x_kernel, [like((4, 2, 4, 8, WIDE), BF16)], [VMEM] * 6)(*got, hg, hg_far)
    pieces = lax.all_to_all(by_z.reshape(32, 8, WIDE), YZ_AXES, 0, 0, tiled=True).reshape(4, 2, 4, 8, WIDE)
    back = [dq[0]]
    for k in range(1, 4):
        back.append(shift(dq[k], "y", 4, -k))
    query_gradient, grad_keys, grad_values, head_t, loss = call(
        finish_kernel,
        [
            like((BLOCK, 4 * WIDE), F32),
            like((8, 512), F32),
            like((8, 512), F32),
            like((2, 4 * WIDE), F32),
            like((1,), F32),
        ],
        [SMEM] + [VMEM] * 5,
        [VMEM] * 4 + [SMEM],
    )(did, pieces, *back)
    return loss, query_gradient[None], grad_keys, grad_values, head_t.T[None]


def solution(mesh):
    fine = Mesh(mesh.devices.reshape(4, 4, 4, 2, 2), ("zl", "x", "y", "zh", "c"))
    layer, ctx = ("zl", "x"), ("y", "zh", "c")
    return jax.shard_map(
        per_device,
        mesh=fine,
        in_specs=(
            P(layer, ctx, None),
            P(ctx + layer, None),
            P(ctx + layer, None),
            P(layer, None, None),
            P(),
            P(ctx),
            P(ctx),
        ),
        out_specs=(
            P(layer),
            P(layer, ctx, None),
            P(ctx + layer, None),
            P(ctx + layer, None),
            P(layer, None, None),
        ),
        check_vma=False,
    )
```

```python
import jax
import jax.numpy as jnp
from jax import lax
from jax.experimental import pallas as pl
from jax.experimental.pallas import tpu as pltpu
from jax.sharding import Mesh, PartitionSpec as P

HEAD_WIDTH = 128
GROUP = 3
WIDE = GROUP * HEAD_WIDTH
BLOCK = 128
CHUNK = 512
TOKENS = 2048
SCALE = HEAD_WIDTH ** -0.5
LOG2E = 1.4426950408889634
NEG = -1.0e30
F32 = jnp.float32
BF16 = jnp.bfloat16
HIGH = lax.Precision.HIGHEST
CHUNKS = ((0,), (0, 1), (0, 1, 2), (3,))
P_AT = (0, 1, 3, 6)
YZ_AXES = ("y", "zh", "zl")


VMEM = pl.BlockSpec(memory_space=pltpu.VMEM)
HBM = pl.BlockSpec(memory_space=pltpu.HBM)
SMEM = pl.BlockSpec(memory_space=pltpu.SMEM)


def coords(did_ref):
    d = did_ref[0]
    return d // 64, (d // 16) % 4, (d // 4) % 4, (d // 2) % 2, d % 2


def keys_kernel(keys, values, kv_out, kb, vb, sems):
    copies = [pltpu.make_async_copy(keys, kb, sems.at[0]), pltpu.make_async_copy(values, vb, sems.at[1])]
    for copy in copies:
        copy.start()
    for copy in copies:
        copy.wait()
    for g in range(4):
        cols = slice(g * HEAD_WIDTH, (g + 1) * HEAD_WIDTH)
        both = jnp.concatenate([kb[:, cols], vb[:, cols]], axis=1)
        for z in range(8):
            kv_out[g, z] = both


def queries_kernel(did, labels, mask, queries, w, seg, q0, q1, q2, q3, w_out, seg_out, lb, mb, sems):
    _, _, y, _, _ = coords(did)
    outs = (q0, q1, q2, q3)
    early = [pltpu.make_async_copy(labels, lb, sems.at[0]), pltpu.make_async_copy(mask, mb, sems.at[1])]
    late = [pltpu.make_async_copy(w, w_out, sems.at[2]), pltpu.make_async_copy(seg, seg_out, sems.at[3])]
    for k in range(4):
        g = pl.multiple_of(((y + k) % 4) * WIDE, HEAD_WIDTH)
        late.append(pltpu.make_async_copy(queries.at[:, pl.ds(g, WIDE)], outs[k].at[pl.ds(0, BLOCK)], sems.at[4 + k]))
    for copy in early + late:
        copy.start()
    for copy in early:
        copy.wait()
    lab = jnp.broadcast_to(lb[...].astype(F32), (16, BLOCK))
    msk = jnp.broadcast_to(mb[...].astype(F32), (16, BLOCK))
    tail = jnp.concatenate([lab, msk, lab], axis=1).astype(BF16)
    for k in range(4):
        outs[k][BLOCK:, :] = tail
    for copy in late:
        copy.wait()


def head_diff(w, y, h):
    at = pl.multiple_of(y * WIDE + h * HEAD_WIDTH, HEAD_WIDTH)
    return w[0:1, pl.ds(at, HEAD_WIDTH)] - w[1:2, pl.ds(at, HEAD_WIDTH)]


def halves(v):
    high = v.astype(BF16).astype(F32)
    return high, v - high


def stack8(rows):
    at = lax.broadcasted_iota(jnp.int32, (8, rows[0].shape[1]), 0)
    out = jnp.zeros((8, rows[0].shape[1]), F32)
    for r, row in enumerate(rows):
        out = jnp.where(at == r, row, out)
    return out


def on_both(v):
    high, low = halves(v)
    return jnp.concatenate([high, low], axis=0).astype(BF16)


NT = (((1,), (1,)), ((), ()))


def times_t(a, b):
    return lax.dot_general(a, b, NT, preferred_element_type=F32)


def forward_kernel(did, seg, w, q0, q1, q2, q3, *rest):
    kvs = rest[:8]
    plog, p_out, inv_out, delta_out, q_out, kv_out = rest[8:14]
    s_buf, u_rows = rest[14:]
    _, x, y, zh, c = coords(did)
    for cc in range(2):
        for kx in range(4):
            for ys in range(4):
                for z in range(2):
                    row = ys * CHUNK + cc * 256 + z * BLOCK + kx * 32
                    kv_out[row : row + 32, :] = kvs[cc * 4 + kx][ys, z]
    for k, ref in enumerate((q0, q1, q2, q3)):
        slot = (y - k + 4) % 4
        for h in range(GROUP):
            q_out[slot, h * BLOCK : (h + 1) * BLOCK, :] = ref[:BLOCK, h * HEAD_WIDTH : (h + 1) * HEAD_WIDTH]
    diffs16 = on_both(stack8([head_diff(w, y, h) for h in range(GROUP)]))
    ones = stack8([jnp.zeros((1, CHUNK), F32)] * GROUP + [jnp.ones((1, CHUNK), F32)])
    for ch in range(4):
        rows = slice(ch * CHUNK, (ch + 1) * CHUNK)
        part = times_t(diffs16, kv_out[rows, HEAD_WIDTH:])
        high, low = halves(part[:8] + part[8:])
        u_rows[:, rows] = jnp.concatenate([high + ones, low], axis=0).astype(BF16)
    j = zh * 2 + c
    r = lax.broadcasted_iota(jnp.int32, (BLOCK, BLOCK), 0)
    from_x = jnp.bitwise_and(x + 4 - jnp.right_shift(r, 5), 3)
    inner = jnp.bitwise_and(jnp.right_shift(r, 3), 3) * 32 + from_x * 8 + jnp.bitwise_and(r, 7)
    query_at = lax.broadcasted_iota(jnp.int32, (BLOCK, BLOCK), 1) + j * BLOCK
    last = seg[:, pl.ds(pl.multiple_of(3 * CHUNK + j * BLOCK, BLOCK), BLOCK)]
    start = jnp.zeros((1, BLOCK), F32)
    for b in range(4):
        row = 3 * CHUNK + b * BLOCK
        ids = jnp.broadcast_to(seg[:, row : row + BLOCK], (BLOCK, BLOCK)).T
        start = start + jnp.sum(jnp.where(ids < last, 1.0, 0.0), axis=0, keepdims=True)
    start = start.astype(jnp.int32)
    for ys in range(4):
        top = jnp.full((1, WIDE), NEG, F32)
        for i, ch in enumerate(CHUNKS[ys]):
            for b in range(CHUNK // BLOCK):
                row = ch * CHUNK + b * BLOCK
                s = times_t(kv_out[row : row + BLOCK, :HEAD_WIDTH], q_out[ys])
                if ch == ys:
                    key_at = inner + ((b % 2) * 256 + ((c + b // 2) % 2) * BLOCK)
                    ok = key_at <= query_at
                    if ys == 3:
                        ok = ok & (key_at >= start)
                    s = jnp.where(jnp.concatenate([ok] * GROUP, axis=1), s, NEG)
                top = jnp.maximum(top, jnp.max(s, axis=0, keepdims=True))
                at = i * CHUNK + b * BLOCK
                s_buf[at : at + BLOCK, :] = s
        sums = jnp.zeros((16, WIDE), F32)
        for i, ch in enumerate(CHUNKS[ys]):
            at_p = (P_AT[ys] + i) * CHUNK
            for b in range(CHUNK // BLOCK):
                at = i * CHUNK + b * BLOCK
                p = jnp.exp2((s_buf[at : at + BLOCK, :] - top) * (SCALE * LOG2E))
                p_out[at_p + b * BLOCK : at_p + (b + 1) * BLOCK, :] = p.astype(BF16)
            sums = sums + jnp.dot(
                u_rows[:, ch * CHUNK : (ch + 1) * CHUNK], p_out[at_p : at_p + CHUNK, :], preferred_element_type=F32
            )
        inv = 1.0 / sums[GROUP : GROUP + 1, :]
        both = (sums[:8] + sums[8:]) * inv
        delta = jnp.concatenate([both[h : h + 1, h * BLOCK : (h + 1) * BLOCK] for h in range(GROUP)], axis=1)
        inv_out[ys] = jnp.broadcast_to(inv, (8, WIDE))
        delta_out[ys] = jnp.broadcast_to(delta, (8, WIDE))
        lg = delta[:, :BLOCK] + delta[:, BLOCK : 2 * BLOCK] + delta[:, 2 * BLOCK :]
        plog[(y - ys + 4) % 4] = jnp.broadcast_to(lg, (8, BLOCK))


def middle_kernel(did, w, p, delta, q, kv, g_out, dq_out, qt_out, pv_out, kt, vt, u):
    _, _, y, _, _ = coords(did)
    eye = jnp.where(
        lax.broadcasted_iota(jnp.int32, (BLOCK, BLOCK), 0) == lax.broadcasted_iota(jnp.int32, (BLOCK, BLOCK), 1), 1.0, 0.0
    ).astype(BF16)
    pad = jnp.zeros((BLOCK - 8, HEAD_WIDTH), F32)
    high, low = halves(jnp.concatenate([stack8([head_diff(w, y, h) for h in range(GROUP)]), pad], axis=0))
    high, low = high.astype(BF16), low.astype(BF16)
    for ch in range(4):
        rows = slice(ch * CHUNK, (ch + 1) * CHUNK)
        kt[:, rows] = times_t(eye, kv[rows, :HEAD_WIDTH]).astype(BF16)
        vt[:, rows] = times_t(eye, kv[rows, HEAD_WIDTH:]).astype(BF16)
        u[rows, :] = times_t(kv[rows, HEAD_WIDTH:], high) + times_t(kv[rows, HEAD_WIDTH:], low)
    for ys in range(4):
        qt_out[ys] = times_t(eye, q[ys]).astype(BF16)
        dqt = jnp.zeros((HEAD_WIDTH, WIDE), F32)
        pv = jnp.zeros((HEAD_WIDTH, WIDE), F32)
        for i, ch in enumerate(CHUNKS[ys]):
            at_p = (P_AT[ys] + i) * CHUNK
            pv = pv + jnp.dot(
                vt[:, ch * CHUNK : (ch + 1) * CHUNK], p[at_p : at_p + CHUNK, :], preferred_element_type=F32
            )
            for b in range(CHUNK // BLOCK):
                row = ch * CHUNK + b * BLOCK
                at = slice(at_p + b * BLOCK, at_p + (b + 1) * BLOCK)
                ub = jnp.concatenate(
                    [jnp.broadcast_to(u[row : row + BLOCK, h : h + 1], (BLOCK, BLOCK)) for h in range(GROUP)], axis=1
                )
                g_out[at, :] = (p[at, :].astype(F32) * (ub - delta[ys, 0:1, :])).astype(BF16)
            dqt = dqt + jnp.dot(
                kt[:, ch * CHUNK : (ch + 1) * CHUNK], g_out[at_p : at_p + CHUNK, :], preferred_element_type=F32
            )
        dq_out[ys] = dqt
        pv_out[ys] = pv


def key_terms(out, half, p, g, qf, at16):
    for ch in range(4):
        dk = jnp.zeros((256, HEAD_WIDTH), F32)
        dv = jnp.zeros((256, HEAD_WIDTH), F32)
        for ys in range(4):
            if ch in CHUNKS[ys]:
                at = (P_AT[ys] + CHUNKS[ys].index(ch)) * CHUNK + half * 256
                dk = dk + times_t(g[at : at + 256, :], qf[ys])
                dv = dv + times_t(p[at : at + 256, :], at16[ys])
        both = jnp.concatenate([dk, dv], axis=1).astype(BF16)
        for z in range(2):
            for kx in range(4):
                row = z * BLOCK + kx * 32
                out[kx * 8 + ch * 2 + z] = both[row : row + 32]


def far_kernel(did, w, l0, l1, l2, l3, g0, g1, g2, g3, p, g, inv, qt, pv, out, f_out, qf, at16, hg_out, lgs, labs):
    _, _, y, _, _ = coords(did)
    for k, ref in enumerate((l0, l1, l2, l3)):
        src = (y - k + 4) % 4
        for m in range(4):
            ys = (y - m + 4) % 4
            lgs[src, ys] = ref[(m - k) % 4]
    for k, ref in enumerate((g0, g1, g2, g3)):
        labs[(y - k + 4) % 4] = ref[BLOCK:, :256].astype(F32)[8:16, :]
    wt = jnp.concatenate([jnp.broadcast_to(head_diff(w, y, h), (BLOCK, HEAD_WIDTH)).T for h in range(GROUP)], axis=1)
    head_of = lax.broadcasted_iota(jnp.int32, (8, WIDE), 1) // BLOCK
    head_at = lax.broadcasted_iota(jnp.int32, (8, WIDE), 0)
    loss = jnp.zeros((1, BLOCK), F32)
    hg = jnp.zeros((8, HEAD_WIDTH), F32)
    for ys in range(4):
        z = (lgs[0, ys] + lgs[1, ys] + lgs[2, ys] + lgs[3, ys])[0:1, :]
        one = labs[ys, 0:1, :BLOCK] > 0.5
        mask = labs[ys, 0:1, BLOCK:]
        a = jnp.where(one, z, -z)
        e = jnp.exp(-jnp.abs(a))
        loss = loss + mask * (jnp.maximum(a, 0.0) + jnp.log(1.0 + e))
        sig = jnp.where(a >= 0.0, 1.0, e) / (1.0 + e)
        d0 = mask * jnp.where(one, sig, -sig)
        f = jnp.concatenate([d0] * GROUP, axis=1) * inv[ys, 0:1, :]
        f_out[ys] = jnp.broadcast_to(f, (8, WIDE))
        at16[ys] = (wt * f).astype(BF16)
        qf[ys] = (qt[ys].astype(F32) * (f * SCALE)).astype(BF16)
        hg = hg + lax.dot_general(
            jnp.where(head_of == head_at, f, 0.0), pv[ys], NT, precision=HIGH, preferred_element_type=F32
        )
    row8 = lax.broadcasted_iota(jnp.int32, (8, BLOCK), 0)
    high, low = halves(jnp.where(row8 == GROUP, loss, hg))
    hg_out[...] = high + low
    tail = jnp.concatenate([high, low], axis=1)
    out[32] = jnp.concatenate([tail] * 4, axis=0).astype(BF16)
    key_terms(out, 1, p, g, qf, at16)


def own_kernel(did, p, g, qf, at16, f, dqt, out, d0, d1, d2, d3, dqb):
    _, _, y, _, _ = coords(did)
    key_terms(out, 0, p, g, qf, at16)
    for ys in range(4):
        dqs = dqt[ys] * (f[ys, 0:1, :] * SCALE)
        slot = (y - ys + 4) % 4
        for h in range(GROUP):
            cols = slice(h * BLOCK, (h + 1) * BLOCK)
            dqb[slot, :, cols] = dqs[:, cols].T.astype(BF16)
    for k, ref in enumerate((d0, d1, d2, d3)):
        ref[...] = dqb[k]


def core_kernel(own, far, hg, b0, b1, b2, b3, hg_out):
    for kx, out in enumerate((b0, b1, b2, b3)):

        def add(ys, carry, kx=kx, out=out):
            for z in range(2):
                at = kx * 8 + ys * 2 + z
                out[ys, z] = (own[at].astype(F32) + far[at].astype(F32)).astype(BF16)
            return carry

        lax.fori_loop(0, 4, add, 0)
    v = far[32].astype(F32)[:8]
    hg_out[...] = hg[...] + (v[:, :BLOCK] + v[:, BLOCK:])


def x_kernel(b0, b1, b2, b3, hg, out):
    high, low = halves(hg[...])
    tail = jnp.concatenate([high[:4], low[:4]], axis=0).astype(BF16)
    tail = jnp.broadcast_to(tail[None, None], (2, 4, 8, BLOCK))

    def add(ys, carry):
        v = b0[ys].astype(F32) + b1[ys].astype(F32) + b2[ys].astype(F32) + b3[ys].astype(F32)
        out[ys, :, :, :, :256] = v.reshape(2, 4, 8, 256).astype(BF16)
        out[ys, :, :, :, 256:] = tail
        return carry

    lax.fori_loop(0, 4, add, 0)


def rows_kernel(did, d0, d1, d2, d3, qg):
    _, _, y, _, _ = coords(did)
    for k, d in enumerate((d0, d1, d2, d3)):
        wide = pl.ds(pl.multiple_of(((y + k) % 4) * WIDE, HEAD_WIDTH), WIDE)
        qg[:, wide] = d[...].astype(F32)


def finish_kernel(did, pieces, gk, gv, hg, loss):
    zl, _, _, _, _ = coords(did)
    for g in range(4):
        v = jnp.zeros((8, 256), F32)
        for k in range(2):
            for z in range(4):
                v = v + pieces[g, k, z, :, :256].astype(F32)
        gk[:, g * HEAD_WIDTH : (g + 1) * HEAD_WIDTH] = v[:, :HEAD_WIDTH]
        gv[:, g * HEAD_WIDTH : (g + 1) * HEAD_WIDTH] = v[:, HEAD_WIDTH:]
        v = pieces[g, 0, zl, :, 256:].astype(F32)
        t = pieces[g, 1, zl, :, 256:].astype(F32)
        v = (v[:4] + v[4:]) + (t[:4] + t[4:])
        for h in range(GROUP):
            cols = slice(g * WIDE + h * HEAD_WIDTH, g * WIDE + (h + 1) * HEAD_WIDTH)
            hg[0:1, cols] = v[h : h + 1]
            hg[1:2, cols] = -v[h : h + 1]
        if g == 0:
            loss[0] = jnp.sum(v[GROUP : GROUP + 1]) * (1.0 / TOKENS)


def shift(v, axis, size, k):
    return lax.ppermute(v, axis, [(i, (i + k) % size) for i in range(size)])


def like(shape, dtype):
    return jax.ShapeDtypeStruct(shape, dtype)


def in_hbm(v):
    return pltpu.with_memory_space_constraint(v, pltpu.HBM)


def call(kernel, out_shape, specs, out_specs=None, scratch=()):
    return pl.pallas_call(
        kernel,
        out_shape=out_shape,
        in_specs=specs,
        out_specs=out_specs or [VMEM] * len(out_shape),
        scratch_shapes=list(scratch),
        compiler_params=pltpu.CompilerParams(vmem_limit_bytes=20 << 20),
    )


def per_device(queries, keys, values, head, segments, label_mask, labels):
    did = lax.axis_index(("zl", "x", "y", "zh", "c")).astype(jnp.int32).reshape(1)
    (copies,) = call(
        keys_kernel,
        [pltpu.VMEM((4, 8, 8, 256), BF16)],
        [HBM] * 2,
        scratch=[pltpu.VMEM((8, 512), BF16), pltpu.VMEM((8, 512), BF16), pltpu.SemaphoreType.DMA((2,))],
    )(in_hbm(keys), in_hbm(values))
    own = lax.all_to_all(copies.reshape(32, 8, 256), YZ_AXES, 0, 0, tiled=True).reshape(4, 2, 32, 256)
    *packs, w, seg = call(
        queries_kernel,
        [like((BLOCK + 16, WIDE), BF16)] * 4 + [like((2, 4 * WIDE), F32), like((1, TOKENS), jnp.int32)],
        [SMEM] + [HBM] * 5,
        scratch=[
            pltpu.VMEM((1, BLOCK), jnp.int32),
            pltpu.VMEM((1, BLOCK), jnp.int32),
            pltpu.SemaphoreType.DMA((8,)),
        ],
    )(
        did,
        in_hbm(labels.reshape(1, BLOCK)),
        in_hbm(label_mask.reshape(1, BLOCK)),
        in_hbm(queries[0]),
        in_hbm(head[0].T),
        in_hbm(segments.reshape(1, TOKENS)),
    )
    over_x = [own]
    for k in range(1, 4):
        over_x.append(shift(own, "x", 4, k))
    over_c = [shift(a, "c", 2, 1) for a in over_x]
    for k in range(1, 4):
        packs[k] = shift(packs[k], "y", 4, k)
    plog, p, inv, delta, q, kv = call(
        forward_kernel,
        [
            like((4, 8, BLOCK), F32),
            like((7 * CHUNK, WIDE), BF16),
            like((4, 8, WIDE), F32),
            like((4, 8, WIDE), F32),
            like((4, WIDE, HEAD_WIDTH), BF16),
            like((TOKENS, 256), BF16),
        ],
        [SMEM] + [VMEM] * 14,
        scratch=[pltpu.VMEM((3 * CHUNK, WIDE), F32), pltpu.VMEM((16, TOKENS), BF16)],
    )(did, seg, w, *packs, *over_x, *over_c)
    logs = [plog] + [shift(plog, "y", 4, k) for k in range(1, 4)]
    g, dqt, qt, pv = call(
        middle_kernel,
        [
            like((7 * CHUNK, WIDE), BF16),
            like((4, HEAD_WIDTH, WIDE), F32),
            like((4, HEAD_WIDTH, WIDE), BF16),
            like((4, HEAD_WIDTH, WIDE), F32),
        ],
        [SMEM] + [VMEM] * 5,
        scratch=[
            pltpu.VMEM((HEAD_WIDTH, TOKENS), BF16),
            pltpu.VMEM((HEAD_WIDTH, TOKENS), BF16),
            pltpu.VMEM((TOKENS, BLOCK), F32),
        ],
    )(did, w, p, delta, q, kv)
    far_d, f, qf, at16, hg = call(
        far_kernel,
        [
            like((33, 32, 256), BF16),
            like((4, 8, WIDE), F32),
            like((4, HEAD_WIDTH, WIDE), BF16),
            like((4, HEAD_WIDTH, WIDE), BF16),
            like((8, BLOCK), F32),
        ],
        [SMEM] + [VMEM] * 14,
        scratch=[pltpu.VMEM((4, 4, 8, BLOCK), F32), pltpu.VMEM((4, 8, 256), F32)],
    )(did, w, *logs, *packs, p, g, inv, qt, pv)
    far = shift(far_d, "c", 2, 1)
    own_d, *dq = call(
        own_kernel,
        [like((32, 32, 256), BF16)] + [like((BLOCK, WIDE), BF16)] * 4,
        [SMEM] + [VMEM] * 6,
        scratch=[pltpu.VMEM((4, BLOCK, WIDE), BF16)],
    )(did, p, g, qf, at16, f, dqt)
    *by_x, hg = call(core_kernel, [like((4, 2, 32, 256), BF16)] * 4 + [like((8, BLOCK), F32)], [VMEM] * 3)(
        own_d, far, hg
    )
    got = [by_x[0]] + [shift(by_x[k], "x", 4, -k) for k in range(1, 4)]
    (by_z,) = call(x_kernel, [pltpu.VMEM((4, 2, 4, 8, WIDE), BF16)], [VMEM] * 5)(*got, hg)
    pieces = lax.all_to_all(by_z.reshape(32, 8, WIDE), YZ_AXES, 0, 0, tiled=True).reshape(4, 2, 4, 8, WIDE)
    back = [dq[0]]
    for k in range(1, 4):
        back.append(shift(dq[k], "y", 4, -k))
    (query_gradient,) = call(rows_kernel, [like((BLOCK, 4 * WIDE), F32)], [SMEM] + [VMEM] * 4)(did, *back)
    grad_keys, grad_values, head_t, loss = call(
        finish_kernel,
        [like((8, 512), F32), like((8, 512), F32), like((2, 4 * WIDE), F32), like((1,), F32)],
        [SMEM, VMEM],
        [VMEM] * 3 + [SMEM],
    )(did, pieces)
    return loss, query_gradient[None], grad_keys, grad_values, head_t.T[None]


def solution(mesh):
    fine = Mesh(mesh.devices.reshape(4, 4, 4, 2, 2), ("zl", "x", "y", "zh", "c"))
    layer, ctx = ("zl", "x"), ("y", "zh", "c")
    return jax.shard_map(
        per_device,
        mesh=fine,
        in_specs=(
            P(layer, ctx, None),
            P(ctx + layer, None),
            P(ctx + layer, None),
            P(layer, None, None),
            P(),
            P(ctx),
            P(ctx),
        ),
        out_specs=(
            P(layer),
            P(layer, ctx, None),
            P(ctx + layer, None),
            P(ctx + layer, None),
            P(layer, None, None),
        ),
        check_vma=False,
    )
```

```python
import jax
import jax.numpy as jnp
from jax import lax
from jax.experimental import pallas as pl
from jax.experimental.pallas import tpu as pltpu
from jax.sharding import Mesh, PartitionSpec as P

HEAD_WIDTH = 128
GROUP = 3
WIDE = GROUP * HEAD_WIDTH
BLOCK = 128
CHUNK = 512
TOKENS = 2048
SCALE = HEAD_WIDTH ** -0.5
LOG2E = 1.4426950408889634
NEG = -1.0e30
F32 = jnp.float32
BF16 = jnp.bfloat16
CHUNKS = ((0,), (0, 1), (0, 1, 2), (3,))
P_AT = (0, 1, 3, 6)
YZ_AXES = ("y", "zh", "zl")


VMEM = pl.BlockSpec(memory_space=pltpu.VMEM)
HBM = pl.BlockSpec(memory_space=pltpu.HBM)
SMEM = pl.BlockSpec(memory_space=pltpu.SMEM)


def coords(did_ref):
    d = did_ref[0]
    return d // 64, (d // 16) % 4, (d // 4) % 4, (d // 2) % 2, d % 2


def keys_kernel(keys, values, kv_out, sems):
    copies = []
    for g in range(4):
        cols = pl.ds(g * HEAD_WIDTH, HEAD_WIDTH)
        for z in range(8):
            for part, src in enumerate((keys, values)):
                to = kv_out.at[g, z, :, pl.ds(part * HEAD_WIDTH, HEAD_WIDTH)]
                copies.append(pltpu.make_async_copy(src.at[:, cols], to, sems.at[len(copies)]))
    for copy in copies:
        copy.start()
    for copy in copies:
        copy.wait()


def queries_kernel(did, labels, mask, queries, w, seg, q0, q1, q2, q3, w_out, seg_out, lb, mb, sems):
    _, _, y, _, _ = coords(did)
    outs = (q0, q1, q2, q3)
    early = [pltpu.make_async_copy(labels, lb, sems.at[0]), pltpu.make_async_copy(mask, mb, sems.at[1])]
    late = [pltpu.make_async_copy(w, w_out, sems.at[2]), pltpu.make_async_copy(seg, seg_out, sems.at[3])]
    for k in range(4):
        g = pl.multiple_of(((y + k) % 4) * WIDE, HEAD_WIDTH)
        late.append(pltpu.make_async_copy(queries.at[:, pl.ds(g, WIDE)], outs[k].at[pl.ds(0, BLOCK)], sems.at[4 + k]))
    for copy in early + late:
        copy.start()
    for copy in early:
        copy.wait()
    lab = jnp.broadcast_to(lb[...].astype(F32), (16, BLOCK))
    msk = jnp.broadcast_to(mb[...].astype(F32), (16, BLOCK))
    tail = jnp.concatenate([lab, msk, lab], axis=1).astype(BF16)
    for k in range(4):
        outs[k][BLOCK:, :] = tail
    for copy in late:
        copy.wait()


def head_diff(w, y, h):
    at = pl.multiple_of(y * WIDE + h * HEAD_WIDTH, HEAD_WIDTH)
    return w[0:1, pl.ds(at, HEAD_WIDTH)] - w[1:2, pl.ds(at, HEAD_WIDTH)]


def halves(v):
    high = v.astype(BF16).astype(F32)
    return high, v - high


def stack8(rows):
    at = lax.broadcasted_iota(jnp.int32, (8, rows[0].shape[1]), 0)
    out = jnp.zeros((8, rows[0].shape[1]), F32)
    for r, row in enumerate(rows):
        out = jnp.where(at == r, row, out)
    return out


def on_both(v):
    high, low = halves(v)
    return jnp.concatenate([high, low], axis=0).astype(BF16)


NT = (((1,), (1,)), ((), ()))


def times_t(a, b):
    return lax.dot_general(a, b, NT, preferred_element_type=F32)


def forward_kernel(did, seg, w, q0, q1, q2, q3, *rest):
    kvs = rest[:8]
    plog, p_out, inv_out, delta_out, q_out, kv_out = rest[8:14]
    s_buf, u_rows = rest[14:]
    _, x, y, zh, c = coords(did)
    for cc in range(2):
        for kx in range(4):
            for ys in range(4):
                for z in range(2):
                    row = ys * CHUNK + cc * 256 + z * BLOCK + kx * 32
                    kv_out[row : row + 32, :] = kvs[cc * 4 + kx][ys, z]
    for k, ref in enumerate((q0, q1, q2, q3)):
        slot = (y - k + 4) % 4
        for h in range(GROUP):
            q_out[slot, h * BLOCK : (h + 1) * BLOCK, :] = ref[:BLOCK, h * HEAD_WIDTH : (h + 1) * HEAD_WIDTH]
    diffs16 = on_both(stack8([head_diff(w, y, h) for h in range(GROUP)]))
    ones = stack8([jnp.zeros((1, CHUNK), F32)] * GROUP + [jnp.ones((1, CHUNK), F32)])
    for ch in range(4):
        rows = slice(ch * CHUNK, (ch + 1) * CHUNK)
        part = times_t(diffs16, kv_out[rows, HEAD_WIDTH:])
        high, low = halves(part[:8] + part[8:])
        u_rows[:, rows] = jnp.concatenate([high + ones, low], axis=0).astype(BF16)
    plog[...] = jnp.zeros_like(plog)
    j = zh * 2 + c
    r = lax.broadcasted_iota(jnp.int32, (BLOCK, BLOCK), 0)
    from_x = jnp.bitwise_and(x + 4 - jnp.right_shift(r, 5), 3)
    inner = jnp.bitwise_and(jnp.right_shift(r, 3), 3) * 32 + from_x * 8 + jnp.bitwise_and(r, 7)
    query_at = lax.broadcasted_iota(jnp.int32, (BLOCK, BLOCK), 1) + j * BLOCK
    last = seg[:, pl.ds(pl.multiple_of(3 * CHUNK + j * BLOCK, BLOCK), BLOCK)]
    start = jnp.zeros((1, BLOCK), F32)
    for b in range(4):
        row = 3 * CHUNK + b * BLOCK
        ids = jnp.broadcast_to(seg[:, row : row + BLOCK], (BLOCK, BLOCK)).T
        start = start + jnp.sum(jnp.where(ids < last, 1.0, 0.0), axis=0, keepdims=True)
    start = start.astype(jnp.int32)
    for ys in range(4):
        top = jnp.full((1, WIDE), NEG, F32)
        for i, ch in enumerate(CHUNKS[ys]):
            for b in range(CHUNK // BLOCK):
                row = ch * CHUNK + b * BLOCK
                s = times_t(kv_out[row : row + BLOCK, :HEAD_WIDTH], q_out[ys])
                if ch == ys:
                    key_at = inner + ((b % 2) * 256 + ((c + b // 2) % 2) * BLOCK)
                    ok = key_at <= query_at
                    if ys == 3:
                        ok = ok & (key_at >= start)
                    s = jnp.where(jnp.concatenate([ok] * GROUP, axis=1), s, NEG)
                top = jnp.maximum(top, jnp.max(s, axis=0, keepdims=True))
                at = i * CHUNK + b * BLOCK
                s_buf[at : at + BLOCK, :] = s
        sums = jnp.zeros((16, WIDE), F32)
        for i, ch in enumerate(CHUNKS[ys]):
            at_p = (P_AT[ys] + i) * CHUNK
            for b in range(CHUNK // BLOCK):
                at = i * CHUNK + b * BLOCK
                p = jnp.exp2((s_buf[at : at + BLOCK, :] - top) * (SCALE * LOG2E))
                p_out[at_p + b * BLOCK : at_p + (b + 1) * BLOCK, :] = p.astype(BF16)
            sums = sums + jnp.dot(
                u_rows[:, ch * CHUNK : (ch + 1) * CHUNK], p_out[at_p : at_p + CHUNK, :], preferred_element_type=F32
            )
        inv = 1.0 / sums[GROUP : GROUP + 1, :]
        both = (sums[:8] + sums[8:]) * inv
        delta = jnp.concatenate([both[h : h + 1, h * BLOCK : (h + 1) * BLOCK] for h in range(GROUP)], axis=1)
        inv_out[ys] = jnp.broadcast_to(inv, (8, WIDE))
        delta_out[ys] = jnp.broadcast_to(delta, (8, WIDE))
        lg = delta[:, :BLOCK] + delta[:, BLOCK : 2 * BLOCK] + delta[:, 2 * BLOCK :]
        plog[pl.ds((y - ys + 4) % 4, 1), :] = lg


def middle_kernel(did, w, p, delta, q, kv, g_out, dq_out, qt_out, kt, u):
    _, _, y, _, _ = coords(did)
    eye = jnp.where(
        lax.broadcasted_iota(jnp.int32, (BLOCK, BLOCK), 0) == lax.broadcasted_iota(jnp.int32, (BLOCK, BLOCK), 1), 1.0, 0.0
    ).astype(BF16)
    pad = jnp.zeros((BLOCK - 8, HEAD_WIDTH), F32)
    high, low = halves(jnp.concatenate([stack8([head_diff(w, y, h) for h in range(GROUP)]), pad], axis=0))
    high, low = high.astype(BF16), low.astype(BF16)
    for ch in range(4):
        rows = slice(ch * CHUNK, (ch + 1) * CHUNK)
        kt[:, rows] = times_t(eye, kv[rows, :HEAD_WIDTH]).astype(BF16)
        u[rows, :] = times_t(kv[rows, HEAD_WIDTH:], high) + times_t(kv[rows, HEAD_WIDTH:], low)
    for ys in range(4):
        qt_out[ys] = times_t(eye, q[ys]).astype(BF16)
        dqt = jnp.zeros((HEAD_WIDTH, WIDE), F32)
        for i, ch in enumerate(CHUNKS[ys]):
            at_p = (P_AT[ys] + i) * CHUNK
            for b in range(CHUNK // BLOCK):
                row = ch * CHUNK + b * BLOCK
                at = slice(at_p + b * BLOCK, at_p + (b + 1) * BLOCK)
                ub = jnp.concatenate(
                    [jnp.broadcast_to(u[row : row + BLOCK, h : h + 1], (BLOCK, BLOCK)) for h in range(GROUP)], axis=1
                )
                g_out[at, :] = (p[at, :].astype(F32) * (ub - delta[ys, 0:1, :])).astype(BF16)
            dqt = dqt + jnp.dot(
                kt[:, ch * CHUNK : (ch + 1) * CHUNK], g_out[at_p : at_p + CHUNK, :], preferred_element_type=F32
            )
        dq_out[ys] = dqt


def key_terms(out, half, p, g, qf, at16):
    for ch in range(4):
        dk = jnp.zeros((256, HEAD_WIDTH), F32)
        dv = jnp.zeros((256, HEAD_WIDTH), F32)
        for ys in range(4):
            if ch in CHUNKS[ys]:
                at = (P_AT[ys] + CHUNKS[ys].index(ch)) * CHUNK + half * 256
                dk = dk + times_t(g[at : at + 256, :], qf[ys])
                dv = dv + times_t(p[at : at + 256, :], at16[ys])
        both = jnp.concatenate([dk, dv], axis=1).astype(BF16)
        for z in range(2):
            for kx in range(4):
                row = z * BLOCK + kx * 32
                out[kx, ch, z] = both[row : row + 32]


def far_kernel(did, w, l0, l1, l2, l3, g0, g1, g2, g3, p, g, inv, qt, out, f_out, qf, at16, loss_out, lgs, labs):
    _, _, y, _, _ = coords(did)
    for k, ref in enumerate((l0, l1, l2, l3)):
        src = (y - k + 4) % 4
        for m in range(4):
            ys = (y - m + 4) % 4
            lgs[src, ys] = jnp.broadcast_to(ref[(m - k) % 4 : (m - k) % 4 + 1, :], (8, BLOCK))
    for k, ref in enumerate((g0, g1, g2, g3)):
        labs[(y - k + 4) % 4] = ref[BLOCK:, :256].astype(F32)[8:16, :]
    wt = jnp.concatenate([jnp.broadcast_to(head_diff(w, y, h), (BLOCK, HEAD_WIDTH)).T for h in range(GROUP)], axis=1)
    loss = jnp.zeros((1, BLOCK), F32)
    for ys in range(4):
        z = (lgs[0, ys] + lgs[1, ys] + lgs[2, ys] + lgs[3, ys])[0:1, :]
        one = labs[ys, 0:1, :BLOCK] > 0.5
        mask = labs[ys, 0:1, BLOCK:]
        a = jnp.where(one, z, -z)
        e = jnp.exp(-jnp.abs(a))
        loss = loss + mask * (jnp.maximum(a, 0.0) + jnp.log(1.0 + e))
        sig = jnp.where(a >= 0.0, 1.0, e) / (1.0 + e)
        d0 = mask * jnp.where(one, sig, -sig)
        f = jnp.concatenate([d0] * GROUP, axis=1) * inv[ys, 0:1, :]
        f_out[ys] = jnp.broadcast_to(f, (8, WIDE))
        at16[ys] = (wt * f).astype(BF16)
        qf[ys] = (qt[ys].astype(F32) * (f * SCALE)).astype(BF16)
    loss_out[...] = jnp.broadcast_to(loss, (8, BLOCK))
    key_terms(out, 1, p, g, qf, at16)


def own_kernel(did, p, g, qf, at16, f, loss, kv, dqt, out, hg_out, d0, d1, d2, d3, dqb, ct):
    _, _, y, _, _ = coords(did)
    key_terms(out, 0, p, g, qf, at16)
    head_of = lax.broadcasted_iota(jnp.int32, (8, WIDE), 1) // BLOCK
    head_at = lax.broadcasted_iota(jnp.int32, (8, WIDE), 0)
    seen = set()
    for ys in range(4):
        fm = on_both(jnp.where(head_of == head_at, f[ys, 0:1, :], 0.0))
        for i, ch in enumerate(CHUNKS[ys]):
            at = (P_AT[ys] + i) * CHUNK
            rows = slice(ch * CHUNK, (ch + 1) * CHUNK)
            cs = times_t(fm, p[at : at + CHUNK, :])
            cs = cs[:8] + cs[8:]
            ct[:, rows] = ct[:, rows] + cs if ch in seen else cs
            seen.add(ch)
        dqs = dqt[ys] * (f[ys, 0:1, :] * SCALE)
        slot = (y - ys + 4) % 4
        for h in range(GROUP):
            cols = slice(h * BLOCK, (h + 1) * BLOCK)
            dqb[slot, :, cols] = dqs[:, cols].T.astype(BF16)
    for k, ref in enumerate((d0, d1, d2, d3)):
        ref[...] = dqb[k]
    hg = jnp.dot(on_both(ct[...]), kv[:, HEAD_WIDTH:], preferred_element_type=F32)
    row8 = lax.broadcasted_iota(jnp.int32, (8, BLOCK), 0)
    hg_out[...] = jnp.where(row8 == GROUP, loss[...], hg[:8] + hg[8:])


def core_kernel(own, far, b0, b1, b2, b3):
    for kx, out in enumerate((b0, b1, b2, b3)):

        def add(ys, carry, kx=kx, out=out):
            out[ys] = (own[kx, ys].astype(F32) + far[kx, ys].astype(F32)).astype(BF16)
            return carry

        lax.fori_loop(0, 4, add, 0)


def x_kernel(b0, b1, b2, b3, hg, hg_far, out):
    high, low = halves(hg[...] + hg_far[...])
    tail = jnp.concatenate([high[:4], low[:4]], axis=0).astype(BF16)
    tail = jnp.broadcast_to(tail[None, None], (2, 4, 8, BLOCK))

    def add(ys, carry):
        v = b0[ys].astype(F32) + b1[ys].astype(F32) + b2[ys].astype(F32) + b3[ys].astype(F32)
        out[ys, :, :, :, :256] = v.reshape(2, 4, 8, 256).astype(BF16)
        out[ys, :, :, :, 256:] = tail
        return carry

    lax.fori_loop(0, 4, add, 0)


def rows_kernel(did, d0, d1, d2, d3, qg):
    _, _, y, _, _ = coords(did)
    for k, d in enumerate((d0, d1, d2, d3)):
        wide = pl.ds(pl.multiple_of(((y + k) % 4) * WIDE, HEAD_WIDTH), WIDE)
        qg[:, wide] = d[...].astype(F32)


def finish_kernel(did, pieces, gk, gv, hg, loss):
    zl, _, _, _, _ = coords(did)
    for g in range(4):
        v = jnp.zeros((8, 256), F32)
        for k in range(2):
            for z in range(4):
                v = v + pieces[g, k, z, :, :256].astype(F32)
        gk[:, g * HEAD_WIDTH : (g + 1) * HEAD_WIDTH] = v[:, :HEAD_WIDTH]
        gv[:, g * HEAD_WIDTH : (g + 1) * HEAD_WIDTH] = v[:, HEAD_WIDTH:]
        v = pieces[g, 0, zl, :, 256:].astype(F32)
        t = pieces[g, 1, zl, :, 256:].astype(F32)
        v = (v[:4] + v[4:]) + (t[:4] + t[4:])
        for h in range(GROUP):
            cols = slice(g * WIDE + h * HEAD_WIDTH, g * WIDE + (h + 1) * HEAD_WIDTH)
            hg[0:1, cols] = v[h : h + 1]
            hg[1:2, cols] = -v[h : h + 1]
        if g == 0:
            loss[0] = jnp.sum(v[GROUP : GROUP + 1]) * (1.0 / TOKENS)


def shift(v, axis, size, k):
    return lax.ppermute(v, axis, [(i, (i + k) % size) for i in range(size)])


def like(shape, dtype):
    return jax.ShapeDtypeStruct(shape, dtype)


def in_hbm(v):
    return pltpu.with_memory_space_constraint(v, pltpu.HBM)


def call(kernel, out_shape, specs, out_specs=None, scratch=()):
    return pl.pallas_call(
        kernel,
        out_shape=out_shape,
        in_specs=specs,
        out_specs=out_specs or [VMEM] * len(out_shape),
        scratch_shapes=list(scratch),
        compiler_params=pltpu.CompilerParams(vmem_limit_bytes=20 << 20),
    )


def per_device(queries, keys, values, head, segments, label_mask, labels):
    did = lax.axis_index(("zl", "x", "y", "zh", "c")).astype(jnp.int32).reshape(1)
    (copies,) = call(
        keys_kernel, [like((4, 8, 8, 256), BF16)], [HBM] * 2, [HBM], scratch=[pltpu.SemaphoreType.DMA((64,))]
    )(in_hbm(keys), in_hbm(values))
    own = lax.all_to_all(copies.reshape(32, 8, 256), YZ_AXES, 0, 0, tiled=True).reshape(4, 2, 32, 256)
    *packs, w, seg = call(
        queries_kernel,
        [like((BLOCK + 16, WIDE), BF16)] * 4 + [like((2, 4 * WIDE), F32), like((1, TOKENS), jnp.int32)],
        [SMEM] + [HBM] * 5,
        scratch=[
            pltpu.VMEM((1, BLOCK), jnp.int32),
            pltpu.VMEM((1, BLOCK), jnp.int32),
            pltpu.SemaphoreType.DMA((8,)),
        ],
    )(
        did,
        in_hbm(labels.reshape(1, BLOCK)),
        in_hbm(label_mask.reshape(1, BLOCK)),
        in_hbm(queries[0]),
        in_hbm(head[0].T),
        in_hbm(segments.reshape(1, TOKENS)),
    )
    over_x = [own]
    for k in range(1, 4):
        over_x.append(shift(own, "x", 4, k))
    over_c = [shift(a, "c", 2, 1) for a in over_x]
    for k in range(1, 4):
        packs[k] = shift(packs[k], "y", 4, k)
    plog, p, inv, delta, q, kv = call(
        forward_kernel,
        [
            like((8, BLOCK), F32),
            like((7 * CHUNK, WIDE), BF16),
            like((4, 8, WIDE), F32),
            like((4, 8, WIDE), F32),
            like((4, WIDE, HEAD_WIDTH), BF16),
            like((TOKENS, 256), BF16),
        ],
        [SMEM] + [VMEM] * 14,
        scratch=[pltpu.VMEM((3 * CHUNK, WIDE), F32), pltpu.VMEM((16, TOKENS), BF16)],
    )(did, seg, w, *packs, *over_x, *over_c)
    logs = [plog]
    for k in range(1, 4):
        logs.append(shift(plog, "y", 4, k))
    g, dqt, qt = call(
        middle_kernel,
        [
            like((7 * CHUNK, WIDE), BF16),
            like((4, HEAD_WIDTH, WIDE), F32),
            like((4, HEAD_WIDTH, WIDE), BF16),
        ],
        [SMEM] + [VMEM] * 5,
        scratch=[pltpu.VMEM((HEAD_WIDTH, TOKENS), BF16), pltpu.VMEM((TOKENS, BLOCK), F32)],
    )(did, w, p, delta, q, kv)
    far_d, f, qf, at16, loss_rows = call(
        far_kernel,
        [
            like((4, 4, 2, 32, 256), BF16),
            like((4, 8, WIDE), F32),
            like((4, HEAD_WIDTH, WIDE), BF16),
            like((4, HEAD_WIDTH, WIDE), BF16),
            like((8, BLOCK), F32),
        ],
        [SMEM] + [VMEM] * 13,
        scratch=[pltpu.VMEM((4, 4, 8, BLOCK), F32), pltpu.VMEM((4, 8, 256), F32)],
    )(did, w, *logs, *packs, p, g, inv, qt)
    far = shift(far_d, "c", 2, 1)
    own_d, hg, *dq = call(
        own_kernel,
        [like((4, 4, 2, 32, 256), BF16), like((8, BLOCK), F32)] + [like((BLOCK, WIDE), BF16)] * 4,
        [SMEM] + [VMEM] * 8,
        scratch=[pltpu.VMEM((4, BLOCK, WIDE), BF16), pltpu.VMEM((8, TOKENS), F32)],
    )(did, p, g, qf, at16, f, loss_rows, kv, dqt)
    by_x = call(core_kernel, [like((4, 2, 32, 256), BF16)] * 4, [VMEM] * 2)(own_d, far)
    got = [by_x[0]]
    for k in range(1, 4):
        got.append(shift(by_x[k], "x", 4, -k))
    hg_far = shift(hg, "c", 2, 1)
    (by_z,) = call(x_kernel, [like((4, 2, 4, 8, WIDE), BF16)], [VMEM] * 6)(*got, hg, hg_far)
    pieces = lax.all_to_all(by_z.reshape(32, 8, WIDE), YZ_AXES, 0, 0, tiled=True).reshape(4, 2, 4, 8, WIDE)
    back = [dq[0]]
    for k in range(1, 4):
        back.append(shift(dq[k], "y", 4, -k))
    (query_gradient,) = call(rows_kernel, [like((BLOCK, 4 * WIDE), F32)], [SMEM] + [VMEM] * 4)(did, *back)
    grad_keys, grad_values, head_t, loss = call(
        finish_kernel,
        [like((8, 512), F32), like((8, 512), F32), like((2, 4 * WIDE), F32), like((1,), F32)],
        [SMEM, VMEM],
        [VMEM] * 3 + [SMEM],
    )(did, pieces)
    return loss, query_gradient[None], grad_keys, grad_values, head_t.T[None]


def solution(mesh):
    fine = Mesh(mesh.devices.reshape(4, 4, 4, 2, 2), ("zl", "x", "y", "zh", "c"))
    layer, ctx = ("zl", "x"), ("y", "zh", "c")
    return jax.shard_map(
        per_device,
        mesh=fine,
        in_specs=(
            P(layer, ctx, None),
            P(ctx + layer, None),
            P(ctx + layer, None),
            P(layer, None, None),
            P(),
            P(ctx),
            P(ctx),
        ),
        out_specs=(
            P(layer),
            P(layer, ctx, None),
            P(ctx + layer, None),
            P(ctx + layer, None),
            P(layer, None, None),
        ),
        check_vma=False,
    )
```

```python
import jax
import jax.numpy as jnp
from jax import lax
from jax.experimental import pallas as pl
from jax.experimental.pallas import tpu as pltpu
from jax.sharding import Mesh, PartitionSpec as P

HEAD_WIDTH = 128
GROUP = 3
WIDE = GROUP * HEAD_WIDTH
BLOCK = 128
CHUNK = 512
HALF = 256
TOKENS = 2048
SCALE = HEAD_WIDTH ** -0.5
LOG2E = 1.4426950408889634
NEG = -1.0e30
F32 = jnp.float32
BF16 = jnp.bfloat16
CHUNKS = ((0,), (0, 1), (0, 1, 2), (3,))
P_AT = (0, 1, 3, 6)
YZ_AXES = ("y", "zh", "zl")


VMEM = pl.BlockSpec(memory_space=pltpu.VMEM)
HBM = pl.BlockSpec(memory_space=pltpu.HBM)
SMEM = pl.BlockSpec(memory_space=pltpu.SMEM)


def coords(did_ref):
    d = did_ref[0]
    return d // 64, (d // 16) % 4, (d // 4) % 4, (d // 2) % 2, d % 2


def keys_kernel(keys, values, kv_out, kb, vb, sems):
    copies = [pltpu.make_async_copy(keys, kb, sems.at[0]), pltpu.make_async_copy(values, vb, sems.at[1])]
    for copy in copies:
        copy.start()
    for copy in copies:
        copy.wait()
    for g in range(4):
        cols = slice(g * HEAD_WIDTH, (g + 1) * HEAD_WIDTH)
        both = jnp.concatenate([kb[:, cols], vb[:, cols]], axis=1)
        for z in range(8):
            kv_out[g, z] = both


def queries_kernel(did, labels, mask, queries, w, seg, q0, q1, q2, q3, w_out, seg_out, lb, mb, sems):
    _, _, y, _, _ = coords(did)
    outs = (q0, q1, q2, q3)
    early = [pltpu.make_async_copy(labels, lb, sems.at[0]), pltpu.make_async_copy(mask, mb, sems.at[1])]
    late = [pltpu.make_async_copy(w, w_out, sems.at[2]), pltpu.make_async_copy(seg, seg_out, sems.at[3])]
    for k in range(4):
        g = pl.multiple_of(((y + k) % 4) * WIDE, HEAD_WIDTH)
        late.append(pltpu.make_async_copy(queries.at[:, pl.ds(g, WIDE)], outs[k].at[pl.ds(0, BLOCK)], sems.at[4 + k]))
    for copy in early + late:
        copy.start()
    for copy in early:
        copy.wait()
    lab = jnp.broadcast_to(lb[...].astype(F32), (16, BLOCK))
    msk = jnp.broadcast_to(mb[...].astype(F32), (16, BLOCK))
    tail = jnp.concatenate([lab, msk, lab], axis=1).astype(BF16)
    for k in range(4):
        outs[k][BLOCK:, :] = tail
    for copy in late:
        copy.wait()


def head_diff(w, y, h):
    at = pl.multiple_of(y * WIDE + h * HEAD_WIDTH, HEAD_WIDTH)
    return w[0:1, pl.ds(at, HEAD_WIDTH)] - w[1:2, pl.ds(at, HEAD_WIDTH)]


def halves(v):
    high = v.astype(BF16).astype(F32)
    return high, v - high


def stack8(rows):
    at = lax.broadcasted_iota(jnp.int32, (8, rows[0].shape[1]), 0)
    out = jnp.zeros((8, rows[0].shape[1]), F32)
    for r, row in enumerate(rows):
        out = jnp.where(at == r, row, out)
    return out


def on_both(v):
    high, low = halves(v)
    return jnp.concatenate([high, low], axis=0).astype(BF16)


NT = (((1,), (1,)), ((), ()))


def times_t(a, b):
    return lax.dot_general(a, b, NT, preferred_element_type=F32)


def scores_half(cc, place, q, seg, w, kvs, kv_out, p_out, top_out, sums_out, s_buf, u_rows):
    _, x, y, zh, c = place
    for kx in range(4):
        for ys in range(4):
            for z in range(2):
                row = ys * HALF + z * BLOCK + kx * 32
                kv_out[row : row + 32, :] = kvs[kx][ys, z]
    diffs16 = on_both(stack8([head_diff(w, y, h) for h in range(GROUP)]))
    ones = stack8([jnp.zeros((1, 2 * HALF), F32)] * GROUP + [jnp.ones((1, 2 * HALF), F32)])
    for n in range(2):
        rows = slice(n * 2 * HALF, (n + 1) * 2 * HALF)
        part = times_t(diffs16, kv_out[rows, HEAD_WIDTH:])
        high, low = halves(part[:8] + part[8:])
        u_rows[:, rows] = jnp.concatenate([high + ones, low], axis=0).astype(BF16)
    j = zh * 2 + c
    r = lax.broadcasted_iota(jnp.int32, (BLOCK, BLOCK), 0)
    from_x = jnp.bitwise_and(x + 4 - jnp.right_shift(r, 5), 3)
    inner = jnp.bitwise_and(jnp.right_shift(r, 3), 3) * 32 + from_x * 8 + jnp.bitwise_and(r, 7)
    inner = inner + ((c + cc) % 2) * BLOCK
    query_at = lax.broadcasted_iota(jnp.int32, (BLOCK, BLOCK), 1) + j * BLOCK
    last = seg[:, pl.ds(pl.multiple_of(3 * CHUNK + j * BLOCK, BLOCK), BLOCK)]
    start = jnp.zeros((1, BLOCK), F32)
    for b in range(4):
        row = 3 * CHUNK + b * BLOCK
        ids = jnp.broadcast_to(seg[:, row : row + BLOCK], (BLOCK, BLOCK)).T
        start = start + jnp.sum(jnp.where(ids < last, 1.0, 0.0), axis=0, keepdims=True)
    start = start.astype(jnp.int32)
    for ys in range(4):
        top = jnp.full((1, WIDE), NEG, F32)
        for i, ch in enumerate(CHUNKS[ys]):
            for z in range(2):
                row = ch * HALF + z * BLOCK
                s = times_t(kv_out[row : row + BLOCK, :HEAD_WIDTH], q[ys])
                if ch == ys:
                    key_at = inner + z * 256
                    ok = key_at <= query_at
                    if ys == 3:
                        ok = ok & (key_at >= start)
                    s = jnp.where(jnp.concatenate([ok] * GROUP, axis=1), s, NEG)
                top = jnp.maximum(top, jnp.max(s, axis=0, keepdims=True))
                at = i * HALF + z * BLOCK
                s_buf[at : at + BLOCK, :] = s
        sums = jnp.zeros((16, WIDE), F32)
        for i, ch in enumerate(CHUNKS[ys]):
            at_p = (P_AT[ys] + i) * HALF
            for z in range(2):
                at = i * HALF + z * BLOCK
                p = jnp.exp2((s_buf[at : at + BLOCK, :] - top) * (SCALE * LOG2E))
                p_out[at_p + z * BLOCK : at_p + (z + 1) * BLOCK, :] = p.astype(BF16)
            sums = sums + jnp.dot(
                u_rows[:, ch * HALF : (ch + 1) * HALF], p_out[at_p : at_p + HALF, :], preferred_element_type=F32
            )
        top_out[ys] = jnp.broadcast_to(top, (8, WIDE))
        sums_out[ys] = sums


def near_kernel(did, seg, w, q0, q1, q2, q3, k0, k1, k2, k3, q_out, kv_out, p_out, top_out, sums_out, s_buf, u_rows):
    place = coords(did)
    y = place[2]
    for k, ref in enumerate((q0, q1, q2, q3)):
        slot = (y - k + 4) % 4
        for h in range(GROUP):
            q_out[slot, h * BLOCK : (h + 1) * BLOCK, :] = ref[:BLOCK, h * HEAD_WIDTH : (h + 1) * HEAD_WIDTH]
    scores_half(0, place, q_out, seg, w, (k0, k1, k2, k3), kv_out, p_out, top_out, sums_out, s_buf, u_rows)


def rest_kernel(
    did, seg, w, q, top0, sums0, k0, k1, k2, k3, plog, inv_out, delta_out, alpha_out, kv_out, p_out, top, sums, s_buf, u_rows
):
    place = coords(did)
    y = place[2]
    scores_half(1, place, q, seg, w, (k0, k1, k2, k3), kv_out, p_out, top, sums, s_buf, u_rows)
    plog[...] = jnp.zeros_like(plog)
    row8 = lax.broadcasted_iota(jnp.int32, (8, WIDE), 0)
    for ys in range(4):
        a, b = top0[ys, 0:1, :], top[ys, 0:1, :]
        both = jnp.maximum(a, b)
        a = jnp.exp2((a - both) * (SCALE * LOG2E))
        b = jnp.exp2((b - both) * (SCALE * LOG2E))
        total = sums0[ys] * a + sums[ys] * b
        inv = 1.0 / total[GROUP : GROUP + 1, :]
        e = (total[:8] + total[8:]) * inv
        delta = jnp.concatenate([e[h : h + 1, h * BLOCK : (h + 1) * BLOCK] for h in range(GROUP)], axis=1)
        inv_out[ys] = jnp.broadcast_to(inv, (8, WIDE))
        delta_out[ys] = jnp.broadcast_to(delta, (8, WIDE))
        alpha_out[ys] = jnp.where(row8 == 0, a, b)
        lg = delta[:, :BLOCK] + delta[:, BLOCK : 2 * BLOCK] + delta[:, 2 * BLOCK :]
        plog[pl.ds((y - ys + 4) % 4, 1), :] = lg


def middle_kernel(did, w, p0, p1, delta, alpha, q, kv0, kv1, g0, g1, dq_out, qt_out, kt, u):
    _, _, y, _, _ = coords(did)
    eye = jnp.where(
        lax.broadcasted_iota(jnp.int32, (BLOCK, BLOCK), 0) == lax.broadcasted_iota(jnp.int32, (BLOCK, BLOCK), 1), 1.0, 0.0
    ).astype(BF16)
    pad = jnp.zeros((BLOCK - 8, HEAD_WIDTH), F32)
    high, low = halves(jnp.concatenate([stack8([head_diff(w, y, h) for h in range(GROUP)]), pad], axis=0))
    high, low = high.astype(BF16), low.astype(BF16)
    for half, kv in enumerate((kv0, kv1)):
        for n in range(2):
            rows = slice(n * 2 * HALF, (n + 1) * 2 * HALF)
            kt[half, :, rows] = times_t(eye, kv[rows, :HEAD_WIDTH]).astype(BF16)
            u[half, rows, :] = times_t(kv[rows, HEAD_WIDTH:], high) + times_t(kv[rows, HEAD_WIDTH:], low)
    for ys in range(4):
        qt_out[ys] = times_t(eye, q[ys]).astype(BF16)
        total = jnp.zeros((HEAD_WIDTH, WIDE), F32)
        for half, (p, g) in enumerate(((p0, g0), (p1, g1))):
            dqt = jnp.zeros((HEAD_WIDTH, WIDE), F32)
            for i, ch in enumerate(CHUNKS[ys]):
                at_p = (P_AT[ys] + i) * HALF
                for z in range(2):
                    row = ch * HALF + z * BLOCK
                    at = slice(at_p + z * BLOCK, at_p + (z + 1) * BLOCK)
                    ub = jnp.concatenate(
                        [jnp.broadcast_to(u[half, row : row + BLOCK, h : h + 1], (BLOCK, BLOCK)) for h in range(GROUP)],
                        axis=1,
                    )
                    g[at, :] = (p[at, :].astype(F32) * (ub - delta[ys, 0:1, :])).astype(BF16)
                dqt = dqt + jnp.dot(
                    kt[half, :, ch * HALF : (ch + 1) * HALF], g[at_p : at_p + HALF, :], preferred_element_type=F32
                )
            total = total + dqt * alpha[ys, half : half + 1, :]
        dq_out[ys] = total


def key_terms(out, half, p, g, qt, wt, f, alpha, qf, at16):
    for ys in range(4):
        fa = f[ys, 0:1, :] * alpha[ys, half : half + 1, :]
        at16[ys] = (wt[...] * fa).astype(BF16)
        qf[ys] = (qt[ys].astype(F32) * (fa * SCALE)).astype(BF16)
    for ch in range(4):
        dk = jnp.zeros((HALF, HEAD_WIDTH), F32)
        dv = jnp.zeros((HALF, HEAD_WIDTH), F32)
        for ys in range(4):
            if ch in CHUNKS[ys]:
                at = (P_AT[ys] + CHUNKS[ys].index(ch)) * HALF
                dk = dk + times_t(g[at : at + HALF, :], qf[ys])
                dv = dv + times_t(p[at : at + HALF, :], at16[ys])
        both = jnp.concatenate([dk, dv], axis=1).astype(BF16)
        for z in range(2):
            for kx in range(4):
                row = z * BLOCK + kx * 32
                out[kx, ch, z] = both[row : row + 32]


def far_kernel(did, w, l0, l1, l2, l3, g0, g1, g2, g3, p, g, inv, alpha, qt, out, f_out, wt, loss_out, lgs, labs, qf, at16):
    _, _, y, _, _ = coords(did)
    for k, ref in enumerate((l0, l1, l2, l3)):
        src = (y - k + 4) % 4
        for m in range(4):
            ys = (y - m + 4) % 4
            lgs[src, ys] = jnp.broadcast_to(ref[(m - k) % 4 : (m - k) % 4 + 1, :], (8, BLOCK))
    for k, ref in enumerate((g0, g1, g2, g3)):
        labs[(y - k + 4) % 4] = ref[BLOCK:, :256].astype(F32)[8:16, :]
    wt[...] = jnp.concatenate([jnp.broadcast_to(head_diff(w, y, h), (BLOCK, HEAD_WIDTH)).T for h in range(GROUP)], axis=1)
    loss = jnp.zeros((1, BLOCK), F32)
    for ys in range(4):
        z = (lgs[0, ys] + lgs[1, ys] + lgs[2, ys] + lgs[3, ys])[0:1, :]
        one = labs[ys, 0:1, :BLOCK] > 0.5
        mask = labs[ys, 0:1, BLOCK:]
        a = jnp.where(one, z, -z)
        e = jnp.exp(-jnp.abs(a))
        loss = loss + mask * (jnp.maximum(a, 0.0) + jnp.log(1.0 + e))
        sig = jnp.where(a >= 0.0, 1.0, e) / (1.0 + e)
        d0 = mask * jnp.where(one, sig, -sig)
        f_out[ys] = jnp.broadcast_to(jnp.concatenate([d0] * GROUP, axis=1) * inv[ys, 0:1, :], (8, WIDE))
    loss_out[...] = jnp.broadcast_to(loss, (8, BLOCK))
    key_terms(out, 1, p, g, qt, wt, f_out, alpha, qf, at16)


def own_kernel(
    did, p0, p1, g, qt, wt, f, alpha, loss, kv0, kv1, dqt, out, hg_out, d0, d1, d2, d3, dqb, ct, qf, at16
):
    _, _, y, _, _ = coords(did)
    key_terms(out, 0, p0, g, qt, wt, f, alpha, qf, at16)
    head_of = lax.broadcasted_iota(jnp.int32, (8, WIDE), 1) // BLOCK
    head_at = lax.broadcasted_iota(jnp.int32, (8, WIDE), 0)
    hg = jnp.zeros((16, HEAD_WIDTH), F32)
    for half, (p, kv) in enumerate(((p0, kv0), (p1, kv1))):
        seen = set()
        for ys in range(4):
            fa = f[ys, 0:1, :] * alpha[ys, half : half + 1, :]
            fm = on_both(jnp.where(head_of == head_at, fa, 0.0))
            for i, ch in enumerate(CHUNKS[ys]):
                at = (P_AT[ys] + i) * HALF
                rows = slice(ch * HALF, (ch + 1) * HALF)
                cs = times_t(fm, p[at : at + HALF, :])
                cs = cs[:8] + cs[8:]
                ct[:, rows] = ct[:, rows] + cs if ch in seen else cs
                seen.add(ch)
        hg = hg + jnp.dot(on_both(ct[...]), kv[:, HEAD_WIDTH:], preferred_element_type=F32)
    for ys in range(4):
        dqs = dqt[ys] * (f[ys, 0:1, :] * SCALE)
        slot = (y - ys + 4) % 4
        for h in range(GROUP):
            cols = slice(h * BLOCK, (h + 1) * BLOCK)
            dqb[slot, :, cols] = dqs[:, cols].T.astype(BF16)
    for k, ref in enumerate((d0, d1, d2, d3)):
        ref[...] = dqb[k]
    row8 = lax.broadcasted_iota(jnp.int32, (8, BLOCK), 0)
    hg_out[...] = jnp.where(row8 == GROUP, loss[...], hg[:8] + hg[8:])


def core_kernel(own, far, b0, b1, b2, b3):
    for kx, out in enumerate((b0, b1, b2, b3)):

        def add(ys, carry, kx=kx, out=out):
            out[ys] = (own[kx, ys].astype(F32) + far[kx, ys].astype(F32)).astype(BF16)
            return carry

        lax.fori_loop(0, 4, add, 0)


def x_kernel(b0, b1, b2, b3, hg, hg_far, out):
    high, low = halves(hg[...] + hg_far[...])
    tail = jnp.concatenate([high[:4], low[:4]], axis=0).astype(BF16)
    tail = jnp.broadcast_to(tail[None, None], (2, 4, 8, BLOCK))

    def add(ys, carry):
        v = b0[ys].astype(F32) + b1[ys].astype(F32) + b2[ys].astype(F32) + b3[ys].astype(F32)
        out[ys, :, :, :, :256] = v.reshape(2, 4, 8, 256).astype(BF16)
        out[ys, :, :, :, 256:] = tail
        return carry

    lax.fori_loop(0, 4, add, 0)


def rows_kernel(did, d0, d1, d2, d3, qg):
    _, _, y, _, _ = coords(did)
    for k, d in enumerate((d0, d1, d2, d3)):
        wide = pl.ds(pl.multiple_of(((y + k) % 4) * WIDE, HEAD_WIDTH), WIDE)
        qg[:, wide] = d[...].astype(F32)


def finish_kernel(did, pieces, gk, gv, hg, loss):
    zl, _, _, _, _ = coords(did)
    for g in range(4):
        v = jnp.zeros((8, 256), F32)
        for k in range(2):
            for z in range(4):
                v = v + pieces[g, k, z, :, :256].astype(F32)
        gk[:, g * HEAD_WIDTH : (g + 1) * HEAD_WIDTH] = v[:, :HEAD_WIDTH]
        gv[:, g * HEAD_WIDTH : (g + 1) * HEAD_WIDTH] = v[:, HEAD_WIDTH:]
        v = pieces[g, 0, zl, :, 256:].astype(F32)
        t = pieces[g, 1, zl, :, 256:].astype(F32)
        v = (v[:4] + v[4:]) + (t[:4] + t[4:])
        for h in range(GROUP):
            cols = slice(g * WIDE + h * HEAD_WIDTH, g * WIDE + (h + 1) * HEAD_WIDTH)
            hg[0:1, cols] = v[h : h + 1]
            hg[1:2, cols] = -v[h : h + 1]
        if g == 0:
            loss[0] = jnp.sum(v[GROUP : GROUP + 1]) * (1.0 / TOKENS)


def shift(v, axis, size, k):
    return lax.ppermute(v, axis, [(i, (i + k) % size) for i in range(size)])


def like(shape, dtype):
    return jax.ShapeDtypeStruct(shape, dtype)


def in_hbm(v):
    return pltpu.with_memory_space_constraint(v, pltpu.HBM)


def call(kernel, out_shape, specs, out_specs=None, scratch=()):
    return pl.pallas_call(
        kernel,
        out_shape=out_shape,
        in_specs=specs,
        out_specs=out_specs or [VMEM] * len(out_shape),
        scratch_shapes=list(scratch),
        compiler_params=pltpu.CompilerParams(vmem_limit_bytes=20 << 20),
    )


def per_device(queries, keys, values, head, segments, label_mask, labels):
    did = lax.axis_index(("zl", "x", "y", "zh", "c")).astype(jnp.int32).reshape(1)
    (copies,) = call(
        keys_kernel,
        [like((4, 8, 8, 256), BF16)],
        [HBM] * 2,
        scratch=[pltpu.VMEM((8, 512), BF16), pltpu.VMEM((8, 512), BF16), pltpu.SemaphoreType.DMA((2,))],
    )(in_hbm(keys), in_hbm(values))
    own = lax.all_to_all(copies.reshape(32, 8, 256), YZ_AXES, 0, 0, tiled=True).reshape(4, 2, 32, 256)
    *packs, w, seg = call(
        queries_kernel,
        [like((BLOCK + 16, WIDE), BF16)] * 4 + [like((2, 4 * WIDE), F32), like((1, TOKENS), jnp.int32)],
        [SMEM] + [HBM] * 5,
        scratch=[
            pltpu.VMEM((1, BLOCK), jnp.int32),
            pltpu.VMEM((1, BLOCK), jnp.int32),
            pltpu.SemaphoreType.DMA((8,)),
        ],
    )(
        did,
        in_hbm(labels.reshape(1, BLOCK)),
        in_hbm(label_mask.reshape(1, BLOCK)),
        in_hbm(queries[0]),
        in_hbm(head[0].T),
        in_hbm(segments.reshape(1, TOKENS)),
    )
    over_x = [own]
    for k in range(1, 4):
        over_x.append(shift(own, "x", 4, k))
    over_c = [shift(a, "c", 2, 1) for a in over_x]
    for k in range(1, 4):
        packs[k] = shift(packs[k], "y", 4, k)
    half_p = like((7 * HALF, WIDE), BF16)
    half_kv = like((4 * HALF, 256), BF16)
    row_set = like((4, 8, WIDE), F32)
    wide_set = like((4, HEAD_WIDTH, WIDE), BF16)
    half_scratch = [pltpu.VMEM((3 * HALF, WIDE), F32), pltpu.VMEM((16, 4 * HALF), BF16)]
    q, kv0, p0, top0, sums0 = call(
        near_kernel,
        [like((4, WIDE, HEAD_WIDTH), BF16), half_kv, half_p, row_set, like((4, 16, WIDE), F32)],
        [SMEM] + [VMEM] * 10,
        scratch=half_scratch,
    )(did, seg, w, *packs, *over_x)
    plog, inv, delta, alpha, kv1, p1 = call(
        rest_kernel,
        [like((8, BLOCK), F32), row_set, row_set, row_set, half_kv, half_p],
        [SMEM] + [VMEM] * 9,
        scratch=[pltpu.VMEM((4, 8, WIDE), F32), pltpu.VMEM((4, 16, WIDE), F32)] + half_scratch,
    )(did, seg, w, q, top0, sums0, *over_c)
    logs = [plog]
    for k in range(1, 4):
        logs.append(shift(plog, "y", 4, k))
    g0, g1, dqt, qt = call(
        middle_kernel,
        [half_p, half_p, like((4, HEAD_WIDTH, WIDE), F32), wide_set],
        [SMEM] + [VMEM] * 8,
        scratch=[pltpu.VMEM((2, HEAD_WIDTH, 4 * HALF), BF16), pltpu.VMEM((2, 4 * HALF, BLOCK), F32)],
    )(did, w, p0, p1, delta, alpha, q, kv0, kv1)
    factor_scratch = [pltpu.VMEM((4, HEAD_WIDTH, WIDE), BF16), pltpu.VMEM((4, HEAD_WIDTH, WIDE), BF16)]
    far_d, f, wt, loss_rows = call(
        far_kernel,
        [like((4, 4, 2, 32, 256), BF16), row_set, like((HEAD_WIDTH, WIDE), F32), like((8, BLOCK), F32)],
        [SMEM] + [VMEM] * 14,
        scratch=[pltpu.VMEM((4, 4, 8, BLOCK), F32), pltpu.VMEM((4, 8, 256), F32)] + factor_scratch,
    )(did, w, *logs, *packs, p1, g1, inv, alpha, qt)
    far = shift(far_d, "c", 2, 1)
    own_d, hg, *dq = call(
        own_kernel,
        [like((4, 4, 2, 32, 256), BF16), like((8, BLOCK), F32)] + [like((BLOCK, WIDE), BF16)] * 4,
        [SMEM] + [VMEM] * 11,
        scratch=[pltpu.VMEM((4, BLOCK, WIDE), BF16), pltpu.VMEM((8, 4 * HALF), F32)] + factor_scratch,
    )(did, p0, p1, g0, qt, wt, f, alpha, loss_rows, kv0, kv1, dqt)
    by_x = call(core_kernel, [like((4, 2, 32, 256), BF16)] * 4, [VMEM] * 2)(own_d, far)
    got = [by_x[0]]
    for k in range(1, 4):
        got.append(shift(by_x[k], "x", 4, -k))
    hg_far = shift(hg, "c", 2, 1)
    (by_z,) = call(x_kernel, [like((4, 2, 4, 8, WIDE), BF16)], [VMEM] * 6)(*got, hg, hg_far)
    pieces = lax.all_to_all(by_z.reshape(32, 8, WIDE), YZ_AXES, 0, 0, tiled=True).reshape(4, 2, 4, 8, WIDE)
    back = [dq[0]]
    for k in range(1, 4):
        back.append(shift(dq[k], "y", 4, -k))
    (query_gradient,) = call(rows_kernel, [like((BLOCK, 4 * WIDE), F32)], [SMEM] + [VMEM] * 4)(did, *back)
    grad_keys, grad_values, head_t, loss = call(
        finish_kernel,
        [like((8, 512), F32), like((8, 512), F32), like((2, 4 * WIDE), F32), like((1,), F32)],
        [SMEM, VMEM],
        [VMEM] * 3 + [SMEM],
    )(did, pieces)
    return loss, query_gradient[None], grad_keys, grad_values, head_t.T[None]


def solution(mesh):
    fine = Mesh(mesh.devices.reshape(4, 4, 4, 2, 2), ("zl", "x", "y", "zh", "c"))
    layer, ctx = ("zl", "x"), ("y", "zh", "c")
    return jax.shard_map(
        per_device,
        mesh=fine,
        in_specs=(
            P(layer, ctx, None),
            P(ctx + layer, None),
            P(ctx + layer, None),
            P(layer, None, None),
            P(),
            P(ctx),
            P(ctx),
        ),
        out_specs=(
            P(layer),
            P(layer, ctx, None),
            P(ctx + layer, None),
            P(ctx + layer, None),
            P(layer, None, None),
        ),
        check_vma=False,
    )
```

```python
import jax
import jax.numpy as jnp
from jax import lax
from jax.experimental import pallas as pl
from jax.experimental.pallas import tpu as pltpu
from jax.sharding import Mesh, PartitionSpec as P

HEAD_WIDTH = 128
GROUP = 3
WIDE = GROUP * HEAD_WIDTH
BLOCK = 128
CHUNK = 512
HALF = 256
TOKENS = 2048
SCALE = HEAD_WIDTH ** -0.5
LOG2E = 1.4426950408889634
NEG = -1.0e30
F32 = jnp.float32
BF16 = jnp.bfloat16
CHUNKS = ((0,), (0, 1), (0, 1, 2), (3,))
P_AT = (0, 1, 3, 6)
YZ_AXES = ("y", "zh", "zl")


VMEM = pl.BlockSpec(memory_space=pltpu.VMEM)
HBM = pl.BlockSpec(memory_space=pltpu.HBM)
SMEM = pl.BlockSpec(memory_space=pltpu.SMEM)


def coords(did_ref):
    d = did_ref[0]
    return d // 64, (d // 16) % 4, (d // 4) % 4, (d // 2) % 2, d % 2


def keys_kernel(keys, values, kv_out, kb, vb, sems):
    copies = [pltpu.make_async_copy(keys, kb, sems.at[0]), pltpu.make_async_copy(values, vb, sems.at[1])]
    for copy in copies:
        copy.start()
    for copy in copies:
        copy.wait()
    for g in range(4):
        cols = slice(g * HEAD_WIDTH, (g + 1) * HEAD_WIDTH)
        both = jnp.concatenate([kb[:, cols], vb[:, cols]], axis=1)
        for z in range(8):
            kv_out[g, z] = both


def queries_kernel(did, labels, mask, queries, w, seg, q0, q1, q2, q3, w_out, seg_out, lb, mb, sems):
    _, _, y, _, _ = coords(did)
    outs = (q0, q1, q2, q3)
    early = [pltpu.make_async_copy(labels, lb, sems.at[0]), pltpu.make_async_copy(mask, mb, sems.at[1])]
    late = [pltpu.make_async_copy(w, w_out, sems.at[2]), pltpu.make_async_copy(seg, seg_out, sems.at[3])]
    for k in range(4):
        g = pl.multiple_of(((y + k) % 4) * WIDE, HEAD_WIDTH)
        late.append(pltpu.make_async_copy(queries.at[:, pl.ds(g, WIDE)], outs[k].at[pl.ds(0, BLOCK)], sems.at[4 + k]))
    for copy in early + late:
        copy.start()
    for copy in early:
        copy.wait()
    lab = jnp.broadcast_to(lb[...].astype(F32), (16, BLOCK))
    msk = jnp.broadcast_to(mb[...].astype(F32), (16, BLOCK))
    tail = jnp.concatenate([lab, msk, lab], axis=1).astype(BF16)
    for k in range(4):
        outs[k][BLOCK:, :] = tail
    for copy in late:
        copy.wait()


def head_diff(w, y, h):
    at = pl.multiple_of(y * WIDE + h * HEAD_WIDTH, HEAD_WIDTH)
    return w[0:1, pl.ds(at, HEAD_WIDTH)] - w[1:2, pl.ds(at, HEAD_WIDTH)]


def halves(v):
    high = v.astype(BF16).astype(F32)
    return high, v - high


def stack8(rows):
    at = lax.broadcasted_iota(jnp.int32, (8, rows[0].shape[1]), 0)
    out = jnp.zeros((8, rows[0].shape[1]), F32)
    for r, row in enumerate(rows):
        out = jnp.where(at == r, row, out)
    return out


def on_both(v):
    high, low = halves(v)
    return jnp.concatenate([high, low], axis=0).astype(BF16)


NT = (((1,), (1,)), ((), ()))


def times_t(a, b):
    return lax.dot_general(a, b, NT, preferred_element_type=F32)


def place_kernel(k0, k1, k2, k3, kv_out):
    for kx, ref in enumerate((k0, k1, k2, k3)):
        for ys in range(4):
            for z in range(2):
                row = ys * HALF + z * BLOCK + kx * 32
                kv_out[row : row + 32, :] = ref[ys, z]


def eye_of():
    return jnp.where(
        lax.broadcasted_iota(jnp.int32, (BLOCK, BLOCK), 0) == lax.broadcasted_iota(jnp.int32, (BLOCK, BLOCK), 1), 1.0, 0.0
    ).astype(BF16)


def columns_half(w, y, kv, kt, u):
    eye = eye_of()
    pad = jnp.zeros((BLOCK - 8, HEAD_WIDTH), F32)
    high, low = halves(jnp.concatenate([stack8([head_diff(w, y, h) for h in range(GROUP)]), pad], axis=0))
    high, low = high.astype(BF16), low.astype(BF16)
    for n in range(2):
        rows = slice(n * 2 * HALF, (n + 1) * 2 * HALF)
        kt[:, rows] = times_t(eye, kv[rows, :HEAD_WIDTH]).astype(BF16)
        u[rows, :] = times_t(kv[rows, HEAD_WIDTH:], high) + times_t(kv[rows, HEAD_WIDTH:], low)


def scores_half(cc, place, q, seg, w, kv_out, p_out, top_out, sums_out, s_buf, u_rows):
    _, x, y, zh, c = place
    diffs16 = on_both(stack8([head_diff(w, y, h) for h in range(GROUP)]))
    ones = stack8([jnp.zeros((1, 2 * HALF), F32)] * GROUP + [jnp.ones((1, 2 * HALF), F32)])
    for n in range(2):
        rows = slice(n * 2 * HALF, (n + 1) * 2 * HALF)
        part = times_t(diffs16, kv_out[rows, HEAD_WIDTH:])
        high, low = halves(part[:8] + part[8:])
        u_rows[:, rows] = jnp.concatenate([high + ones, low], axis=0).astype(BF16)
    j = zh * 2 + c
    r = lax.broadcasted_iota(jnp.int32, (BLOCK, BLOCK), 0)
    from_x = jnp.bitwise_and(x + 4 - jnp.right_shift(r, 5), 3)
    inner = jnp.bitwise_and(jnp.right_shift(r, 3), 3) * 32 + from_x * 8 + jnp.bitwise_and(r, 7)
    inner = inner + ((c + cc) % 2) * BLOCK
    query_at = lax.broadcasted_iota(jnp.int32, (BLOCK, BLOCK), 1) + j * BLOCK
    last = seg[:, pl.ds(pl.multiple_of(3 * CHUNK + j * BLOCK, BLOCK), BLOCK)]
    start = jnp.zeros((1, BLOCK), F32)
    for b in range(4):
        row = 3 * CHUNK + b * BLOCK
        ids = jnp.broadcast_to(seg[:, row : row + BLOCK], (BLOCK, BLOCK)).T
        start = start + jnp.sum(jnp.where(ids < last, 1.0, 0.0), axis=0, keepdims=True)
    start = start.astype(jnp.int32)
    for ys in range(4):
        top = jnp.full((1, WIDE), NEG, F32)
        for i, ch in enumerate(CHUNKS[ys]):
            for z in range(2):
                row = ch * HALF + z * BLOCK
                s = times_t(kv_out[row : row + BLOCK, :HEAD_WIDTH], q[ys])
                if ch == ys:
                    key_at = inner + z * 256
                    ok = key_at <= query_at
                    if ys == 3:
                        ok = ok & (key_at >= start)
                    s = jnp.where(jnp.concatenate([ok] * GROUP, axis=1), s, NEG)
                top = jnp.maximum(top, jnp.max(s, axis=0, keepdims=True))
                at = i * HALF + z * BLOCK
                s_buf[at : at + BLOCK, :] = s
        sums = jnp.zeros((16, WIDE), F32)
        for i, ch in enumerate(CHUNKS[ys]):
            at_p = (P_AT[ys] + i) * HALF
            for z in range(2):
                at = i * HALF + z * BLOCK
                p = jnp.exp2((s_buf[at : at + BLOCK, :] - top) * (SCALE * LOG2E))
                p_out[at_p + z * BLOCK : at_p + (z + 1) * BLOCK, :] = p.astype(BF16)
            sums = sums + jnp.dot(
                u_rows[:, ch * HALF : (ch + 1) * HALF], p_out[at_p : at_p + HALF, :], preferred_element_type=F32
            )
        top_out[ys] = jnp.broadcast_to(top, (8, WIDE))
        sums_out[ys] = sums


def near_kernel(did, seg, w, q0, q1, q2, q3, kv, q_out, qt_out, kt, u, p_out, top_out, sums_out, s_buf, u_rows):
    place = coords(did)
    y = place[2]
    for k, ref in enumerate((q0, q1, q2, q3)):
        slot = (y - k + 4) % 4
        for h in range(GROUP):
            q_out[slot, h * BLOCK : (h + 1) * BLOCK, :] = ref[:BLOCK, h * HEAD_WIDTH : (h + 1) * HEAD_WIDTH]
    scores_half(0, place, q_out, seg, w, kv, p_out, top_out, sums_out, s_buf, u_rows)
    for ys in range(4):
        qt_out[ys] = times_t(eye_of(), q_out[ys]).astype(BF16)
    columns_half(w, y, kv, kt, u)


def rest_kernel(
    did, seg, w, q, top0, sums0, kv, plog, inv_out, delta_out, alpha_out, p_out, top, sums, s_buf, u_rows
):
    place = coords(did)
    y = place[2]
    scores_half(1, place, q, seg, w, kv, p_out, top, sums, s_buf, u_rows)
    plog[...] = jnp.zeros_like(plog)
    row8 = lax.broadcasted_iota(jnp.int32, (8, WIDE), 0)
    for ys in range(4):
        a, b = top0[ys, 0:1, :], top[ys, 0:1, :]
        both = jnp.maximum(a, b)
        a = jnp.exp2((a - both) * (SCALE * LOG2E))
        b = jnp.exp2((b - both) * (SCALE * LOG2E))
        total = sums0[ys] * a + sums[ys] * b
        inv = 1.0 / total[GROUP : GROUP + 1, :]
        e = (total[:8] + total[8:]) * inv
        delta = jnp.concatenate([e[h : h + 1, h * BLOCK : (h + 1) * BLOCK] for h in range(GROUP)], axis=1)
        inv_out[ys] = jnp.broadcast_to(inv, (8, WIDE))
        delta_out[ys] = jnp.broadcast_to(delta, (8, WIDE))
        alpha_out[ys] = jnp.where(row8 == 0, a, b)
        lg = delta[:, :BLOCK] + delta[:, BLOCK : 2 * BLOCK] + delta[:, 2 * BLOCK :]
        plog[pl.ds((y - ys + 4) % 4, 1), :] = lg


def middle_kernel(did, w, p0, p1, delta, alpha, kv1, kt0, u0, g0, g1, dq_out, kt1, u1):
    _, _, y, _, _ = coords(did)
    columns_half(w, y, kv1, kt1, u1)
    for ys in range(4):
        total = jnp.zeros((HEAD_WIDTH, WIDE), F32)
        for half, (p, g, kt, u) in enumerate(((p0, g0, kt0, u0), (p1, g1, kt1, u1))):
            dqt = jnp.zeros((HEAD_WIDTH, WIDE), F32)
            for i, ch in enumerate(CHUNKS[ys]):
                at_p = (P_AT[ys] + i) * HALF
                for z in range(2):
                    row = ch * HALF + z * BLOCK
                    at = slice(at_p + z * BLOCK, at_p + (z + 1) * BLOCK)
                    ub = jnp.concatenate(
                        [jnp.broadcast_to(u[row : row + BLOCK, h : h + 1], (BLOCK, BLOCK)) for h in range(GROUP)],
                        axis=1,
                    )
                    g[at, :] = (p[at, :].astype(F32) * (ub - delta[ys, 0:1, :])).astype(BF16)
                dqt = dqt + jnp.dot(
                    kt[:, ch * HALF : (ch + 1) * HALF], g[at_p : at_p + HALF, :], preferred_element_type=F32
                )
            total = total + dqt * alpha[ys, half : half + 1, :]
        dq_out[ys] = total


def key_terms(out, half, p, g, qt, wt, f, alpha, qf, at16):
    for ys in range(4):
        fa = f[ys, 0:1, :] * alpha[ys, half : half + 1, :]
        at16[ys] = (wt[...] * fa).astype(BF16)
        qf[ys] = (qt[ys].astype(F32) * (fa * SCALE)).astype(BF16)
    for ch in range(4):
        dk = jnp.zeros((HALF, HEAD_WIDTH), F32)
        dv = jnp.zeros((HALF, HEAD_WIDTH), F32)
        for ys in range(4):
            if ch in CHUNKS[ys]:
                at = (P_AT[ys] + CHUNKS[ys].index(ch)) * HALF
                dk = dk + times_t(g[at : at + HALF, :], qf[ys])
                dv = dv + times_t(p[at : at + HALF, :], at16[ys])
        both = jnp.concatenate([dk, dv], axis=1).astype(BF16)
        for z in range(2):
            for kx in range(4):
                row = z * BLOCK + kx * 32
                out[kx, ch, z] = both[row : row + 32]


def far_kernel(did, w, l0, l1, l2, l3, g0, g1, g2, g3, p, g, inv, alpha, qt, out, f_out, wt, loss_out, lgs, labs, qf, at16):
    _, _, y, _, _ = coords(did)
    for k, ref in enumerate((l0, l1, l2, l3)):
        src = (y - k + 4) % 4
        for m in range(4):
            ys = (y - m + 4) % 4
            lgs[src, ys] = jnp.broadcast_to(ref[(m - k) % 4 : (m - k) % 4 + 1, :], (8, BLOCK))
    for k, ref in enumerate((g0, g1, g2, g3)):
        labs[(y - k + 4) % 4] = ref[BLOCK:, :256].astype(F32)[8:16, :]
    wt[...] = jnp.concatenate([jnp.broadcast_to(head_diff(w, y, h), (BLOCK, HEAD_WIDTH)).T for h in range(GROUP)], axis=1)
    loss = jnp.zeros((1, BLOCK), F32)
    for ys in range(4):
        z = (lgs[0, ys] + lgs[1, ys] + lgs[2, ys] + lgs[3, ys])[0:1, :]
        one = labs[ys, 0:1, :BLOCK] > 0.5
        mask = labs[ys, 0:1, BLOCK:]
        a = jnp.where(one, z, -z)
        e = jnp.exp(-jnp.abs(a))
        loss = loss + mask * (jnp.maximum(a, 0.0) + jnp.log(1.0 + e))
        sig = jnp.where(a >= 0.0, 1.0, e) / (1.0 + e)
        d0 = mask * jnp.where(one, sig, -sig)
        f_out[ys] = jnp.broadcast_to(jnp.concatenate([d0] * GROUP, axis=1) * inv[ys, 0:1, :], (8, WIDE))
    loss_out[...] = jnp.broadcast_to(loss, (8, BLOCK))
    key_terms(out, 1, p, g, qt, wt, f_out, alpha, qf, at16)


def own_kernel(
    did, p0, p1, g, qt, wt, f, alpha, loss, kv0, kv1, dqt, out, hg_out, d0, d1, d2, d3, dqb, ct, qf, at16
):
    _, _, y, _, _ = coords(did)
    key_terms(out, 0, p0, g, qt, wt, f, alpha, qf, at16)
    head_of = lax.broadcasted_iota(jnp.int32, (8, WIDE), 1) // BLOCK
    head_at = lax.broadcasted_iota(jnp.int32, (8, WIDE), 0)
    hg = jnp.zeros((16, HEAD_WIDTH), F32)
    for half, (p, kv) in enumerate(((p0, kv0), (p1, kv1))):
        seen = set()
        for ys in range(4):
            fa = f[ys, 0:1, :] * alpha[ys, half : half + 1, :]
            fm = on_both(jnp.where(head_of == head_at, fa, 0.0))
            for i, ch in enumerate(CHUNKS[ys]):
                at = (P_AT[ys] + i) * HALF
                rows = slice(ch * HALF, (ch + 1) * HALF)
                cs = times_t(fm, p[at : at + HALF, :])
                cs = cs[:8] + cs[8:]
                ct[:, rows] = ct[:, rows] + cs if ch in seen else cs
                seen.add(ch)
        hg = hg + jnp.dot(on_both(ct[...]), kv[:, HEAD_WIDTH:], preferred_element_type=F32)
    for ys in range(4):
        dqs = dqt[ys] * (f[ys, 0:1, :] * SCALE)
        slot = (y - ys + 4) % 4
        for h in range(GROUP):
            cols = slice(h * BLOCK, (h + 1) * BLOCK)
            dqb[slot, :, cols] = dqs[:, cols].T.astype(BF16)
    for k, ref in enumerate((d0, d1, d2, d3)):
        ref[...] = dqb[k]
    row8 = lax.broadcasted_iota(jnp.int32, (8, BLOCK), 0)
    hg_out[...] = jnp.where(row8 == GROUP, loss[...], hg[:8] + hg[8:])


def core_kernel(own, far, b0, b1, b2, b3):
    for kx, out in enumerate((b0, b1, b2, b3)):

        def add(ys, carry, kx=kx, out=out):
            out[ys] = (own[kx, ys].astype(F32) + far[kx, ys].astype(F32)).astype(BF16)
            return carry

        lax.fori_loop(0, 4, add, 0)


def x_kernel(b0, b1, b2, b3, hg, hg_far, out):
    high, low = halves(hg[...] + hg_far[...])
    tail = jnp.concatenate([high[:4], low[:4]], axis=0).astype(BF16)
    tail = jnp.broadcast_to(tail[None, None], (2, 4, 8, BLOCK))

    def add(ys, carry):
        v = b0[ys].astype(F32) + b1[ys].astype(F32) + b2[ys].astype(F32) + b3[ys].astype(F32)
        out[ys, :, :, :, :256] = v.reshape(2, 4, 8, 256).astype(BF16)
        out[ys, :, :, :, 256:] = tail
        return carry

    lax.fori_loop(0, 4, add, 0)


def rows_kernel(did, d0, d1, d2, d3, qg):
    _, _, y, _, _ = coords(did)
    for k, d in enumerate((d0, d1, d2, d3)):
        wide = pl.ds(pl.multiple_of(((y + k) % 4) * WIDE, HEAD_WIDTH), WIDE)
        qg[:, wide] = d[...].astype(F32)


def finish_kernel(did, pieces, gk, gv, hg, loss):
    zl, _, _, _, _ = coords(did)
    for g in range(4):
        v = jnp.zeros((8, 256), F32)
        for k in range(2):
            for z in range(4):
                v = v + pieces[g, k, z, :, :256].astype(F32)
        gk[:, g * HEAD_WIDTH : (g + 1) * HEAD_WIDTH] = v[:, :HEAD_WIDTH]
        gv[:, g * HEAD_WIDTH : (g + 1) * HEAD_WIDTH] = v[:, HEAD_WIDTH:]
        v = pieces[g, 0, zl, :, 256:].astype(F32)
        t = pieces[g, 1, zl, :, 256:].astype(F32)
        v = (v[:4] + v[4:]) + (t[:4] + t[4:])
        for h in range(GROUP):
            cols = slice(g * WIDE + h * HEAD_WIDTH, g * WIDE + (h + 1) * HEAD_WIDTH)
            hg[0:1, cols] = v[h : h + 1]
            hg[1:2, cols] = -v[h : h + 1]
        if g == 0:
            loss[0] = jnp.sum(v[GROUP : GROUP + 1]) * (1.0 / TOKENS)


def shift(v, axis, size, k):
    return lax.ppermute(v, axis, [(i, (i + k) % size) for i in range(size)])


def like(shape, dtype):
    return jax.ShapeDtypeStruct(shape, dtype)


def in_hbm(v):
    return pltpu.with_memory_space_constraint(v, pltpu.HBM)


def call(kernel, out_shape, specs, out_specs=None, scratch=()):
    return pl.pallas_call(
        kernel,
        out_shape=out_shape,
        in_specs=specs,
        out_specs=out_specs or [VMEM] * len(out_shape),
        scratch_shapes=list(scratch),
        compiler_params=pltpu.CompilerParams(vmem_limit_bytes=20 << 20),
    )


def per_device(queries, keys, values, head, segments, label_mask, labels):
    did = lax.axis_index(("zl", "x", "y", "zh", "c")).astype(jnp.int32).reshape(1)
    (copies,) = call(
        keys_kernel,
        [like((4, 8, 8, 256), BF16)],
        [HBM] * 2,
        scratch=[pltpu.VMEM((8, 512), BF16), pltpu.VMEM((8, 512), BF16), pltpu.SemaphoreType.DMA((2,))],
    )(in_hbm(keys), in_hbm(values))
    own = lax.all_to_all(copies.reshape(32, 8, 256), YZ_AXES, 0, 0, tiled=True).reshape(4, 2, 32, 256)
    *packs, w, seg = call(
        queries_kernel,
        [like((BLOCK + 16, WIDE), BF16)] * 4 + [like((2, 4 * WIDE), F32), like((1, TOKENS), jnp.int32)],
        [SMEM] + [HBM] * 5,
        scratch=[
            pltpu.VMEM((1, BLOCK), jnp.int32),
            pltpu.VMEM((1, BLOCK), jnp.int32),
            pltpu.SemaphoreType.DMA((8,)),
        ],
    )(
        did,
        in_hbm(labels.reshape(1, BLOCK)),
        in_hbm(label_mask.reshape(1, BLOCK)),
        in_hbm(queries[0]),
        in_hbm(head[0].T),
        in_hbm(segments.reshape(1, TOKENS)),
    )
    over_x = [own]
    for k in range(1, 4):
        over_x.append(shift(own, "x", 4, k))
    half_kv = like((4 * HALF, 256), BF16)
    (kv0,) = call(place_kernel, [half_kv], [VMEM] * 4)(*over_x)
    kv1 = shift(kv0, "c", 2, 1)
    for k in range(1, 4):
        packs[k] = shift(packs[k], "y", 4, k)
    half_p = like((7 * HALF, WIDE), BF16)
    row_set = like((4, 8, WIDE), F32)
    wide_set = like((4, HEAD_WIDTH, WIDE), BF16)
    half_scratch = [pltpu.VMEM((3 * HALF, WIDE), F32), pltpu.VMEM((16, 4 * HALF), BF16)]
    q, qt, kt0, u0, p0, top0, sums0 = call(
        near_kernel,
        [
            like((4, WIDE, HEAD_WIDTH), BF16),
            wide_set,
            like((HEAD_WIDTH, 4 * HALF), BF16),
            like((4 * HALF, BLOCK), F32),
            half_p,
            row_set,
            like((4, 16, WIDE), F32),
        ],
        [SMEM] + [VMEM] * 7,
        scratch=half_scratch,
    )(did, seg, w, *packs, kv0)
    plog, inv, delta, alpha, p1 = call(
        rest_kernel,
        [like((8, BLOCK), F32), row_set, row_set, row_set, half_p],
        [SMEM] + [VMEM] * 6,
        scratch=[pltpu.VMEM((4, 8, WIDE), F32), pltpu.VMEM((4, 16, WIDE), F32)] + half_scratch,
    )(did, seg, w, q, top0, sums0, kv1)
    logs = [plog]
    for k in range(1, 4):
        logs.append(shift(plog, "y", 4, k))
    g0, g1, dqt = call(
        middle_kernel,
        [half_p, half_p, like((4, HEAD_WIDTH, WIDE), F32)],
        [SMEM] + [VMEM] * 8,
        scratch=[pltpu.VMEM((HEAD_WIDTH, 4 * HALF), BF16), pltpu.VMEM((4 * HALF, BLOCK), F32)],
    )(did, w, p0, p1, delta, alpha, kv1, kt0, u0)
    factor_scratch = [pltpu.VMEM((4, HEAD_WIDTH, WIDE), BF16), pltpu.VMEM((4, HEAD_WIDTH, WIDE), BF16)]
    far_d, f, wt, loss_rows = call(
        far_kernel,
        [like((4, 4, 2, 32, 256), BF16), row_set, like((HEAD_WIDTH, WIDE), F32), like((8, BLOCK), F32)],
        [SMEM] + [VMEM] * 14,
        scratch=[pltpu.VMEM((4, 4, 8, BLOCK), F32), pltpu.VMEM((4, 8, 256), F32)] + factor_scratch,
    )(did, w, *logs, *packs, p1, g1, inv, alpha, qt)
    far = shift(far_d, "c", 2, 1)
    own_d, hg, *dq = call(
        own_kernel,
        [like((4, 4, 2, 32, 256), BF16), like((8, BLOCK), F32)] + [like((BLOCK, WIDE), BF16)] * 4,
        [SMEM] + [VMEM] * 11,
        scratch=[pltpu.VMEM((4, BLOCK, WIDE), BF16), pltpu.VMEM((8, 4 * HALF), F32)] + factor_scratch,
    )(did, p0, p1, g0, qt, wt, f, alpha, loss_rows, kv0, kv1, dqt)
    by_x = call(core_kernel, [like((4, 2, 32, 256), BF16)] * 4, [VMEM] * 2)(own_d, far)
    got = [by_x[0]]
    for k in range(1, 4):
        got.append(shift(by_x[k], "x", 4, -k))
    hg_far = shift(hg, "c", 2, 1)
    (by_z,) = call(x_kernel, [like((4, 2, 4, 8, WIDE), BF16)], [VMEM] * 6)(*got, hg, hg_far)
    pieces = lax.all_to_all(by_z.reshape(32, 8, WIDE), YZ_AXES, 0, 0, tiled=True).reshape(4, 2, 4, 8, WIDE)
    back = [dq[0]]
    for k in range(1, 4):
        back.append(shift(dq[k], "y", 4, -k))
    (query_gradient,) = call(rows_kernel, [like((BLOCK, 4 * WIDE), F32)], [SMEM] + [VMEM] * 4)(did, *back)
    grad_keys, grad_values, head_t, loss = call(
        finish_kernel,
        [like((8, 512), F32), like((8, 512), F32), like((2, 4 * WIDE), F32), like((1,), F32)],
        [SMEM, VMEM],
        [VMEM] * 3 + [SMEM],
    )(did, pieces)
    return loss, query_gradient[None], grad_keys, grad_values, head_t.T[None]


def solution(mesh):
    fine = Mesh(mesh.devices.reshape(4, 4, 4, 2, 2), ("zl", "x", "y", "zh", "c"))
    layer, ctx = ("zl", "x"), ("y", "zh", "c")
    return jax.shard_map(
        per_device,
        mesh=fine,
        in_specs=(
            P(layer, ctx, None),
            P(ctx + layer, None),
            P(ctx + layer, None),
            P(layer, None, None),
            P(),
            P(ctx),
            P(ctx),
        ),
        out_specs=(
            P(layer),
            P(layer, ctx, None),
            P(ctx + layer, None),
            P(ctx + layer, None),
            P(layer, None, None),
        ),
        check_vma=False,
    )
```

```python
import jax
import jax.numpy as jnp
from jax import lax
from jax.experimental import pallas as pl
from jax.experimental.pallas import tpu as pltpu
from jax.sharding import Mesh, PartitionSpec as P

HEAD_WIDTH = 128
GROUP = 3
WIDE = GROUP * HEAD_WIDTH
BLOCK = 128
CHUNK = 512
HALF = 256
TOKENS = 2048
SCALE = HEAD_WIDTH ** -0.5
LOG2E = 1.4426950408889634
NEG = -1.0e30
F32 = jnp.float32
BF16 = jnp.bfloat16
CHUNKS = ((0,), (0, 1), (0, 1, 2), (3,))
P_AT = (0, 1, 3, 6)
YZ_AXES = ("y", "zh", "zl")


VMEM = pl.BlockSpec(memory_space=pltpu.VMEM)
HBM = pl.BlockSpec(memory_space=pltpu.HBM)
SMEM = pl.BlockSpec(memory_space=pltpu.SMEM)


def coords(did_ref):
    d = did_ref[0]
    return d // 64, (d // 16) % 4, (d // 4) % 4, (d // 2) % 2, d % 2


def keys_kernel(keys, values, kv_out, kb, vb, sems):
    copies = [pltpu.make_async_copy(keys, kb, sems.at[0]), pltpu.make_async_copy(values, vb, sems.at[1])]
    for copy in copies:
        copy.start()
    for copy in copies:
        copy.wait()
    for g in range(4):
        cols = slice(g * HEAD_WIDTH, (g + 1) * HEAD_WIDTH)
        both = jnp.concatenate([kb[:, cols], vb[:, cols]], axis=1)
        for z in range(8):
            kv_out[g, z] = both


def queries_kernel(did, labels, mask, queries, w, seg, q0, q1, q2, q3, w_out, seg_out, lb, mb, sems):
    _, _, y, _, _ = coords(did)
    outs = (q0, q1, q2, q3)
    early = [pltpu.make_async_copy(labels, lb, sems.at[0]), pltpu.make_async_copy(mask, mb, sems.at[1])]
    late = [pltpu.make_async_copy(w, w_out, sems.at[2]), pltpu.make_async_copy(seg, seg_out, sems.at[3])]
    for k in range(4):
        g = pl.multiple_of(((y + k) % 4) * WIDE, HEAD_WIDTH)
        late.append(pltpu.make_async_copy(queries.at[:, pl.ds(g, WIDE)], outs[k].at[pl.ds(0, BLOCK)], sems.at[4 + k]))
    for copy in early + late:
        copy.start()
    for copy in early:
        copy.wait()
    lab = jnp.broadcast_to(lb[...].astype(F32), (16, BLOCK))
    msk = jnp.broadcast_to(mb[...].astype(F32), (16, BLOCK))
    tail = jnp.concatenate([lab, msk, lab], axis=1).astype(BF16)
    for k in range(4):
        outs[k][BLOCK:, :] = tail
    for copy in late:
        copy.wait()


def head_diff(w, y, h):
    at = pl.multiple_of(y * WIDE + h * HEAD_WIDTH, HEAD_WIDTH)
    return w[0:1, pl.ds(at, HEAD_WIDTH)] - w[1:2, pl.ds(at, HEAD_WIDTH)]


def halves(v):
    high = v.astype(BF16).astype(F32)
    return high, v - high


def stack8(rows):
    at = lax.broadcasted_iota(jnp.int32, (8, rows[0].shape[1]), 0)
    out = jnp.zeros((8, rows[0].shape[1]), F32)
    for r, row in enumerate(rows):
        out = jnp.where(at == r, row, out)
    return out


def on_both(v):
    high, low = halves(v)
    return jnp.concatenate([high, low], axis=0).astype(BF16)


NT = (((1,), (1,)), ((), ()))


def times_t(a, b):
    return lax.dot_general(a, b, NT, preferred_element_type=F32)


def place_kernel(k0, k1, k2, k3, kv_out):
    for kx, ref in enumerate((k0, k1, k2, k3)):
        for ys in range(4):
            for z in range(2):
                row = ys * HALF + z * BLOCK + kx * 32
                kv_out[row : row + 32, :] = ref[ys, z]


def eye_of():
    return jnp.where(
        lax.broadcasted_iota(jnp.int32, (BLOCK, BLOCK), 0) == lax.broadcasted_iota(jnp.int32, (BLOCK, BLOCK), 1), 1.0, 0.0
    ).astype(BF16)


def columns_half(w, y, kv, kt, u):
    eye = eye_of()
    pad = jnp.zeros((BLOCK - 8, HEAD_WIDTH), F32)
    high, low = halves(jnp.concatenate([stack8([head_diff(w, y, h) for h in range(GROUP)]), pad], axis=0))
    high, low = high.astype(BF16), low.astype(BF16)
    for n in range(2):
        rows = slice(n * 2 * HALF, (n + 1) * 2 * HALF)
        kt[:, rows] = times_t(eye, kv[rows, :HEAD_WIDTH]).astype(BF16)
        u[rows, :] = times_t(kv[rows, HEAD_WIDTH:], high) + times_t(kv[rows, HEAD_WIDTH:], low)


def scores_half(cc, place, q, seg, w, kv_out, p_out, top_out, sums_out, s_buf, u_rows):
    _, x, y, zh, c = place
    diffs16 = on_both(stack8([head_diff(w, y, h) for h in range(GROUP)]))
    ones = stack8([jnp.zeros((1, 2 * HALF), F32)] * GROUP + [jnp.ones((1, 2 * HALF), F32)])
    for n in range(2):
        rows = slice(n * 2 * HALF, (n + 1) * 2 * HALF)
        part = times_t(diffs16, kv_out[rows, HEAD_WIDTH:])
        high, low = halves(part[:8] + part[8:])
        u_rows[:, rows] = jnp.concatenate([high + ones, low], axis=0).astype(BF16)
    j = zh * 2 + c
    r = lax.broadcasted_iota(jnp.int32, (BLOCK, BLOCK), 0)
    from_x = jnp.bitwise_and(x + 4 - jnp.right_shift(r, 5), 3)
    inner = jnp.bitwise_and(jnp.right_shift(r, 3), 3) * 32 + from_x * 8 + jnp.bitwise_and(r, 7)
    inner = inner + ((c + cc) % 2) * BLOCK
    query_at = lax.broadcasted_iota(jnp.int32, (BLOCK, BLOCK), 1) + j * BLOCK
    last = seg[:, pl.ds(pl.multiple_of(3 * CHUNK + j * BLOCK, BLOCK), BLOCK)]
    start = jnp.zeros((1, BLOCK), F32)
    for b in range(4):
        row = 3 * CHUNK + b * BLOCK
        ids = jnp.broadcast_to(seg[:, row : row + BLOCK], (BLOCK, BLOCK)).T
        start = start + jnp.sum(jnp.where(ids < last, 1.0, 0.0), axis=0, keepdims=True)
    start = start.astype(jnp.int32)
    for ys in range(4):
        top = jnp.full((1, WIDE), NEG, F32)
        for i, ch in enumerate(CHUNKS[ys]):
            whole = times_t(kv_out[ch * HALF : (ch + 1) * HALF, :HEAD_WIDTH], q[ys])
            for z in range(2):
                s = whole[z * BLOCK : (z + 1) * BLOCK]
                if ch == ys:
                    key_at = inner + z * 256
                    ok = key_at <= query_at
                    if ys == 3:
                        ok = ok & (key_at >= start)
                    s = jnp.where(jnp.concatenate([ok] * GROUP, axis=1), s, NEG)
                top = jnp.maximum(top, jnp.max(s, axis=0, keepdims=True))
                at = i * HALF + z * BLOCK
                s_buf[at : at + BLOCK, :] = s
        sums = jnp.zeros((16, WIDE), F32)
        for i, ch in enumerate(CHUNKS[ys]):
            at_p = (P_AT[ys] + i) * HALF
            for z in range(2):
                at = i * HALF + z * BLOCK
                p = jnp.exp2((s_buf[at : at + BLOCK, :] - top) * (SCALE * LOG2E))
                p_out[at_p + z * BLOCK : at_p + (z + 1) * BLOCK, :] = p.astype(BF16)
            sums = sums + jnp.dot(
                u_rows[:, ch * HALF : (ch + 1) * HALF], p_out[at_p : at_p + HALF, :], preferred_element_type=F32
            )
        top_out[ys] = jnp.broadcast_to(top, (8, WIDE))
        sums_out[ys] = sums


def near_kernel(did, seg, w, q0, q1, q2, q3, kv, q_out, qt_out, kt, u, p_out, top_out, sums_out, s_buf, u_rows):
    place = coords(did)
    y = place[2]
    for k, ref in enumerate((q0, q1, q2, q3)):
        slot = (y - k + 4) % 4
        for h in range(GROUP):
            q_out[slot, h * BLOCK : (h + 1) * BLOCK, :] = ref[:BLOCK, h * HEAD_WIDTH : (h + 1) * HEAD_WIDTH]
    scores_half(0, place, q_out, seg, w, kv, p_out, top_out, sums_out, s_buf, u_rows)
    for ys in range(4):
        qt_out[ys] = times_t(eye_of(), q_out[ys]).astype(BF16)
    columns_half(w, y, kv, kt, u)


def rest_kernel(
    did, seg, w, q, top0, sums0, kv, plog, inv_out, delta_out, alpha_out, p_out, top, sums, s_buf, u_rows
):
    place = coords(did)
    y = place[2]
    scores_half(1, place, q, seg, w, kv, p_out, top, sums, s_buf, u_rows)
    plog[...] = jnp.zeros_like(plog)
    row8 = lax.broadcasted_iota(jnp.int32, (8, WIDE), 0)
    for ys in range(4):
        a, b = top0[ys, 0:1, :], top[ys, 0:1, :]
        both = jnp.maximum(a, b)
        a = jnp.exp2((a - both) * (SCALE * LOG2E))
        b = jnp.exp2((b - both) * (SCALE * LOG2E))
        total = sums0[ys] * a + sums[ys] * b
        inv = 1.0 / total[GROUP : GROUP + 1, :]
        e = (total[:8] + total[8:]) * inv
        delta = jnp.concatenate([e[h : h + 1, h * BLOCK : (h + 1) * BLOCK] for h in range(GROUP)], axis=1)
        inv_out[ys] = jnp.broadcast_to(inv, (8, WIDE))
        delta_out[ys] = jnp.broadcast_to(delta, (8, WIDE))
        alpha_out[ys] = jnp.where(row8 == 0, a, b)
        lg = delta[:, :BLOCK] + delta[:, BLOCK : 2 * BLOCK] + delta[:, 2 * BLOCK :]
        plog[pl.ds((y - ys + 4) % 4, 1), :] = lg


def middle_kernel(did, w, p0, p1, delta, alpha, kv1, kt0, u0, g0, g1, dq_out, kt1, u1):
    _, _, y, _, _ = coords(did)
    columns_half(w, y, kv1, kt1, u1)
    sides = ((p0, g0, kt0, u0), (p1, g1, kt1, u1))
    for p, g, kt, u in sides:
        for ch in range(4):
            for z in range(2):
                row = ch * HALF + z * BLOCK
                ub = jnp.concatenate(
                    [jnp.broadcast_to(u[row : row + BLOCK, h : h + 1], (BLOCK, BLOCK)) for h in range(GROUP)], axis=1
                )
                for ys in range(4):
                    if ch in CHUNKS[ys]:
                        at = (P_AT[ys] + CHUNKS[ys].index(ch)) * HALF + z * BLOCK
                        rows = slice(at, at + BLOCK)
                        g[rows, :] = (p[rows, :].astype(F32) * (ub - delta[ys, 0:1, :])).astype(BF16)
    for ys in range(4):
        keys = slice(CHUNKS[ys][0] * HALF, (CHUNKS[ys][-1] + 1) * HALF)
        rows = slice(P_AT[ys] * HALF, (P_AT[ys] + len(CHUNKS[ys])) * HALF)
        total = jnp.zeros((HEAD_WIDTH, WIDE), F32)
        for half, (p, g, kt, u) in enumerate(sides):
            dqt = jnp.dot(kt[:, keys], g[rows, :], preferred_element_type=F32)
            total = total + dqt * alpha[ys, half : half + 1, :]
        dq_out[ys] = total


def key_terms(out, half, p, g, qt, wt, f, alpha, qf, at16):
    for ys in range(4):
        fa = f[ys, 0:1, :] * alpha[ys, half : half + 1, :]
        at16[ys] = (wt[...] * fa).astype(BF16)
        qf[ys] = (qt[ys].astype(F32) * (fa * SCALE)).astype(BF16)
    dks, dvs = [None] * 4, [None] * 4
    for ys in range(4):
        at = slice(P_AT[ys] * HALF, (P_AT[ys] + len(CHUNKS[ys])) * HALF)
        dk = times_t(g[at, :], qf[ys])
        dv = times_t(p[at, :], at16[ys])
        for i, ch in enumerate(CHUNKS[ys]):
            rows = slice(i * HALF, (i + 1) * HALF)
            dks[ch] = dk[rows] if dks[ch] is None else dks[ch] + dk[rows]
            dvs[ch] = dv[rows] if dvs[ch] is None else dvs[ch] + dv[rows]
    for ch in range(4):
        dk, dv = dks[ch], dvs[ch]
        both = jnp.concatenate([dk, dv], axis=1).astype(BF16)
        for z in range(2):
            for kx in range(4):
                row = z * BLOCK + kx * 32
                out[kx, ch, z] = both[row : row + 32]


def far_kernel(did, w, l0, l1, l2, l3, g0, g1, g2, g3, p, g, inv, alpha, qt, out, f_out, wt, loss_out, lgs, labs, qf, at16):
    _, _, y, _, _ = coords(did)
    for k, ref in enumerate((l0, l1, l2, l3)):
        src = (y - k + 4) % 4
        for m in range(4):
            ys = (y - m + 4) % 4
            lgs[src, ys] = jnp.broadcast_to(ref[(m - k) % 4 : (m - k) % 4 + 1, :], (8, BLOCK))
    for k, ref in enumerate((g0, g1, g2, g3)):
        labs[(y - k + 4) % 4] = ref[BLOCK:, :256].astype(F32)[8:16, :]
    wt[...] = jnp.concatenate([jnp.broadcast_to(head_diff(w, y, h), (BLOCK, HEAD_WIDTH)).T for h in range(GROUP)], axis=1)
    loss = jnp.zeros((1, BLOCK), F32)
    for ys in range(4):
        z = (lgs[0, ys] + lgs[1, ys] + lgs[2, ys] + lgs[3, ys])[0:1, :]
        one = labs[ys, 0:1, :BLOCK] > 0.5
        mask = labs[ys, 0:1, BLOCK:]
        a = jnp.where(one, z, -z)
        e = jnp.exp(-jnp.abs(a))
        loss = loss + mask * (jnp.maximum(a, 0.0) + jnp.log(1.0 + e))
        sig = jnp.where(a >= 0.0, 1.0, e) / (1.0 + e)
        d0 = mask * jnp.where(one, sig, -sig)
        f_out[ys] = jnp.broadcast_to(jnp.concatenate([d0] * GROUP, axis=1) * inv[ys, 0:1, :], (8, WIDE))
    loss_out[...] = jnp.broadcast_to(loss, (8, BLOCK))
    key_terms(out, 1, p, g, qt, wt, f_out, alpha, qf, at16)


def own_kernel(
    did, p0, p1, g, qt, wt, f, alpha, loss, kv0, kv1, dqt, out, hg_out, d0, d1, d2, d3, dqb, ct, qf, at16
):
    _, _, y, _, _ = coords(did)
    key_terms(out, 0, p0, g, qt, wt, f, alpha, qf, at16)
    head_of = lax.broadcasted_iota(jnp.int32, (8, WIDE), 1) // BLOCK
    head_at = lax.broadcasted_iota(jnp.int32, (8, WIDE), 0)
    hg = jnp.zeros((16, HEAD_WIDTH), F32)
    for half, (p, kv) in enumerate(((p0, kv0), (p1, kv1))):
        seen = set()
        for ys in range(4):
            fa = f[ys, 0:1, :] * alpha[ys, half : half + 1, :]
            fm = on_both(jnp.where(head_of == head_at, fa, 0.0))
            for i, ch in enumerate(CHUNKS[ys]):
                at = (P_AT[ys] + i) * HALF
                rows = slice(ch * HALF, (ch + 1) * HALF)
                cs = times_t(fm, p[at : at + HALF, :])
                cs = cs[:8] + cs[8:]
                ct[:, rows] = ct[:, rows] + cs if ch in seen else cs
                seen.add(ch)
        hg = hg + jnp.dot(on_both(ct[...]), kv[:, HEAD_WIDTH:], preferred_element_type=F32)
    for ys in range(4):
        dqs = dqt[ys] * (f[ys, 0:1, :] * SCALE)
        slot = (y - ys + 4) % 4
        for h in range(GROUP):
            cols = slice(h * BLOCK, (h + 1) * BLOCK)
            dqb[slot, :, cols] = dqs[:, cols].T.astype(BF16)
    for k, ref in enumerate((d0, d1, d2, d3)):
        ref[...] = dqb[k]
    row8 = lax.broadcasted_iota(jnp.int32, (8, BLOCK), 0)
    hg_out[...] = jnp.where(row8 == GROUP, loss[...], hg[:8] + hg[8:])


def core_kernel(own, far, b0, b1, b2, b3):
    for kx, out in enumerate((b0, b1, b2, b3)):

        def add(ys, carry, kx=kx, out=out):
            out[ys] = (own[kx, ys].astype(F32) + far[kx, ys].astype(F32)).astype(BF16)
            return carry

        lax.fori_loop(0, 4, add, 0)


def x_kernel(b0, b1, b2, b3, hg, hg_far, out):
    high, low = halves(hg[...] + hg_far[...])
    tail = jnp.concatenate([high[:4], low[:4]], axis=0).astype(BF16)
    tail = jnp.broadcast_to(tail[None, None], (2, 4, 8, BLOCK))

    def add(ys, carry):
        v = b0[ys].astype(F32) + b1[ys].astype(F32) + b2[ys].astype(F32) + b3[ys].astype(F32)
        out[ys, :, :, :, :256] = v.reshape(2, 4, 8, 256).astype(BF16)
        out[ys, :, :, :, 256:] = tail
        return carry

    lax.fori_loop(0, 4, add, 0)


def rows_kernel(did, d0, d1, d2, d3, qg):
    _, _, y, _, _ = coords(did)
    for k, d in enumerate((d0, d1, d2, d3)):
        wide = pl.ds(pl.multiple_of(((y + k) % 4) * WIDE, HEAD_WIDTH), WIDE)
        qg[:, wide] = d[...].astype(F32)


def finish_kernel(did, pieces, gk, gv, hg, loss):
    zl, _, _, _, _ = coords(did)
    for g in range(4):
        v = jnp.zeros((8, 256), F32)
        for k in range(2):
            for z in range(4):
                v = v + pieces[g, k, z, :, :256].astype(F32)
        gk[:, g * HEAD_WIDTH : (g + 1) * HEAD_WIDTH] = v[:, :HEAD_WIDTH]
        gv[:, g * HEAD_WIDTH : (g + 1) * HEAD_WIDTH] = v[:, HEAD_WIDTH:]
        v = pieces[g, 0, zl, :, 256:].astype(F32)
        t = pieces[g, 1, zl, :, 256:].astype(F32)
        v = (v[:4] + v[4:]) + (t[:4] + t[4:])
        for h in range(GROUP):
            cols = slice(g * WIDE + h * HEAD_WIDTH, g * WIDE + (h + 1) * HEAD_WIDTH)
            hg[0:1, cols] = v[h : h + 1]
            hg[1:2, cols] = -v[h : h + 1]
        if g == 0:
            loss[0] = jnp.sum(v[GROUP : GROUP + 1]) * (1.0 / TOKENS)


def shift(v, axis, size, k):
    return lax.ppermute(v, axis, [(i, (i + k) % size) for i in range(size)])


def like(shape, dtype):
    return jax.ShapeDtypeStruct(shape, dtype)


def in_hbm(v):
    return pltpu.with_memory_space_constraint(v, pltpu.HBM)


def call(kernel, out_shape, specs, out_specs=None, scratch=()):
    return pl.pallas_call(
        kernel,
        out_shape=out_shape,
        in_specs=specs,
        out_specs=out_specs or [VMEM] * len(out_shape),
        scratch_shapes=list(scratch),
        compiler_params=pltpu.CompilerParams(vmem_limit_bytes=20 << 20),
    )


def per_device(queries, keys, values, head, segments, label_mask, labels):
    did = lax.axis_index(("zl", "x", "y", "zh", "c")).astype(jnp.int32).reshape(1)
    (copies,) = call(
        keys_kernel,
        [like((4, 8, 8, 256), BF16)],
        [HBM] * 2,
        scratch=[pltpu.VMEM((8, 512), BF16), pltpu.VMEM((8, 512), BF16), pltpu.SemaphoreType.DMA((2,))],
    )(in_hbm(keys), in_hbm(values))
    own = lax.all_to_all(copies.reshape(32, 8, 256), YZ_AXES, 0, 0, tiled=True).reshape(4, 2, 32, 256)
    *packs, w, seg = call(
        queries_kernel,
        [like((BLOCK + 16, WIDE), BF16)] * 4 + [like((2, 4 * WIDE), F32), like((1, TOKENS), jnp.int32)],
        [SMEM] + [HBM] * 5,
        scratch=[
            pltpu.VMEM((1, BLOCK), jnp.int32),
            pltpu.VMEM((1, BLOCK), jnp.int32),
            pltpu.SemaphoreType.DMA((8,)),
        ],
    )(
        did,
        in_hbm(labels.reshape(1, BLOCK)),
        in_hbm(label_mask.reshape(1, BLOCK)),
        in_hbm(queries[0]),
        in_hbm(head[0].T),
        in_hbm(segments.reshape(1, TOKENS)),
    )
    over_x = [own]
    for k in range(1, 4):
        over_x.append(shift(own, "x", 4, k))
    half_kv = like((4 * HALF, 256), BF16)
    (kv0,) = call(place_kernel, [half_kv], [VMEM] * 4)(*over_x)
    kv1 = shift(kv0, "c", 2, 1)
    for k in range(1, 4):
        packs[k] = shift(packs[k], "y", 4, k)
    half_p = like((7 * HALF, WIDE), BF16)
    row_set = like((4, 8, WIDE), F32)
    wide_set = like((4, HEAD_WIDTH, WIDE), BF16)
    half_scratch = [pltpu.VMEM((3 * HALF, WIDE), F32), pltpu.VMEM((16, 4 * HALF), BF16)]
    q, qt, kt0, u0, p0, top0, sums0 = call(
        near_kernel,
        [
            like((4, WIDE, HEAD_WIDTH), BF16),
            wide_set,
            like((HEAD_WIDTH, 4 * HALF), BF16),
            like((4 * HALF, BLOCK), F32),
            half_p,
            row_set,
            like((4, 16, WIDE), F32),
        ],
        [SMEM] + [VMEM] * 7,
        scratch=half_scratch,
    )(did, seg, w, *packs, kv0)
    plog, inv, delta, alpha, p1 = call(
        rest_kernel,
        [like((8, BLOCK), F32), row_set, row_set, row_set, half_p],
        [SMEM] + [VMEM] * 6,
        scratch=[pltpu.VMEM((4, 8, WIDE), F32), pltpu.VMEM((4, 16, WIDE), F32)] + half_scratch,
    )(did, seg, w, q, top0, sums0, kv1)
    logs = [plog]
    for k in range(1, 4):
        logs.append(shift(plog, "y", 4, k))
    g0, g1, dqt = call(
        middle_kernel,
        [half_p, half_p, like((4, HEAD_WIDTH, WIDE), F32)],
        [SMEM] + [VMEM] * 8,
        scratch=[pltpu.VMEM((HEAD_WIDTH, 4 * HALF), BF16), pltpu.VMEM((4 * HALF, BLOCK), F32)],
    )(did, w, p0, p1, delta, alpha, kv1, kt0, u0)
    factor_scratch = [pltpu.VMEM((4, HEAD_WIDTH, WIDE), BF16), pltpu.VMEM((4, HEAD_WIDTH, WIDE), BF16)]
    far_d, f, wt, loss_rows = call(
        far_kernel,
        [like((4, 4, 2, 32, 256), BF16), row_set, like((HEAD_WIDTH, WIDE), F32), like((8, BLOCK), F32)],
        [SMEM] + [VMEM] * 14,
        scratch=[pltpu.VMEM((4, 4, 8, BLOCK), F32), pltpu.VMEM((4, 8, 256), F32)] + factor_scratch,
    )(did, w, *logs, *packs, p1, g1, inv, alpha, qt)
    far = shift(far_d, "c", 2, 1)
    own_d, hg, *dq = call(
        own_kernel,
        [like((4, 4, 2, 32, 256), BF16), like((8, BLOCK), F32)] + [like((BLOCK, WIDE), BF16)] * 4,
        [SMEM] + [VMEM] * 11,
        scratch=[pltpu.VMEM((4, BLOCK, WIDE), BF16), pltpu.VMEM((8, 4 * HALF), F32)] + factor_scratch,
    )(did, p0, p1, g0, qt, wt, f, alpha, loss_rows, kv0, kv1, dqt)
    by_x = call(core_kernel, [like((4, 2, 32, 256), BF16)] * 4, [VMEM] * 2)(own_d, far)
    got = [by_x[0]]
    for k in range(1, 4):
        got.append(shift(by_x[k], "x", 4, -k))
    hg_far = shift(hg, "c", 2, 1)
    (by_z,) = call(x_kernel, [like((4, 2, 4, 8, WIDE), BF16)], [VMEM] * 6)(*got, hg, hg_far)
    pieces = lax.all_to_all(by_z.reshape(32, 8, WIDE), YZ_AXES, 0, 0, tiled=True).reshape(4, 2, 4, 8, WIDE)
    back = [dq[0]]
    for k in range(1, 4):
        back.append(shift(dq[k], "y", 4, -k))
    (query_gradient,) = call(rows_kernel, [like((BLOCK, 4 * WIDE), F32)], [SMEM] + [VMEM] * 4)(did, *back)
    grad_keys, grad_values, head_t, loss = call(
        finish_kernel,
        [like((8, 512), F32), like((8, 512), F32), like((2, 4 * WIDE), F32), like((1,), F32)],
        [SMEM, VMEM],
        [VMEM] * 3 + [SMEM],
    )(did, pieces)
    return loss, query_gradient[None], grad_keys, grad_values, head_t.T[None]


def solution(mesh):
    fine = Mesh(mesh.devices.reshape(4, 4, 4, 2, 2), ("zl", "x", "y", "zh", "c"))
    layer, ctx = ("zl", "x"), ("y", "zh", "c")
    return jax.shard_map(
        per_device,
        mesh=fine,
        in_specs=(
            P(layer, ctx, None),
            P(ctx + layer, None),
            P(ctx + layer, None),
            P(layer, None, None),
            P(),
            P(ctx),
            P(ctx),
        ),
        out_specs=(
            P(layer),
            P(layer, ctx, None),
            P(ctx + layer, None),
            P(ctx + layer, None),
            P(layer, None, None),
        ),
        check_vma=False,
    )
```
